32 devices in a mesh: dp: 8 (over z, y), fsdp: 4 (over x, core).
Axes of the slice: x: 2, y: 2, z: 4, core: 2. Of those that a mesh axis runs over, the one named last changes fastest.
Arguments:
- tokens: bfloat16 [1024, 40, 768], P(('dp', 'fsdp')), may hold values from -6 to 6
- patches: bfloat16 [128, 145, 1024], P(('dp', 'fsdp')), may hold values from -6 to 6
- segments: int32 [1024, 40], P(('dp', 'fsdp')), may hold values from 0 to 3, never falling along the last dimension, each value on 1 to 20 neighbouring positions
- owner: int32 [1024], P(('dp', 'fsdp')), may hold values from 0 to 7, as said below
- image_slot: int32 [1024], P(('dp', 'fsdp')), may hold values from 0 to 3
- out_grad: bfloat16 [1024, 40, 768], P(('dp', 'fsdp')), may hold values from -6 to 6
- self_query: bfloat16 [768, 768], P(('dp', 'fsdp')), may hold values from -0.21875 to 0.21875
- query_bias: bfloat16 [768], P(('dp', 'fsdp')), may hold values from -3 to 3
- self_key: bfloat16 [768, 768], P(('dp', 'fsdp')), may hold values from -0.21875 to 0.21875
- self_value: bfloat16 [768, 768], P(('dp', 'fsdp')), may hold values from -0.21875 to 0.21875
- value_bias: bfloat16 [768], P(('dp', 'fsdp')), may hold values from -3 to 3
- self_output: bfloat16 [768, 768], P(('dp', 'fsdp')), may hold values from -0.625 to 0.625
- output_bias: bfloat16 [768], P(('dp', 'fsdp')), may hold values from -3 to 3
- first_gain: bfloat16 [768], P(('dp', 'fsdp')), may hold values from 0.25 to 1.75
- first_norm_bias: bfloat16 [768], P(('dp', 'fsdp')), may hold values from -3 to 3
- patch_proj: bfloat16 [1024, 768], P(('dp', 'fsdp')), may hold values from -0.1875 to 0.1875
- patch_bias: bfloat16 [768], P(('dp', 'fsdp')), may hold values from -3 to 3
- cross_query: bfloat16 [768, 768], P(('dp', 'fsdp')), may hold values from -0.21875 to 0.21875
- probe_bias: bfloat16 [768], P(('dp', 'fsdp')), may hold values from -3 to 3
- cross_key: bfloat16 [768, 768], P(('dp', 'fsdp')), may hold values from -0.21875 to 0.21875
- cross_value: bfloat16 [768, 768], P(('dp', 'fsdp')), may hold values from -0.21875 to 0.21875
- content_bias: bfloat16 [768], P(('dp', 'fsdp')), may hold values from -3 to 3
- cross_output: bfloat16 [768, 768], P(('dp', 'fsdp')), may hold values from -1.25 to 1.25
- cross_bias: bfloat16 [768], P(('dp', 'fsdp')), may hold values from -3 to 3
- second_gain: bfloat16 [768], P(('dp', 'fsdp')), may hold values from 0.25 to 1.75
- second_shift: bfloat16 [768], P(('dp', 'fsdp')), may hold values from -3 to 3
- widen_weight: bfloat16 [768, 3072], P(('dp', 'fsdp')), may hold values from -0.21875 to 0.21875
- widen_bias: bfloat16 [3072], P(('dp', 'fsdp')), may hold values from -3 to 3
- narrow_weight: bfloat16 [3072, 768], P(('dp', 'fsdp')), may hold values from -0.15625 to 0.15625
- narrow_bias: bfloat16 [768], P(('dp', 'fsdp')), may hold values from -3 to 3
- third_gain: bfloat16 [768], P(('dp', 'fsdp')), may hold values from 0.25 to 1.75
- third_shift: bfloat16 [768], P(('dp', 'fsdp')), may hold values from -3 to 3
Outputs:
- output: bfloat16 [1024, 40, 768], P(('dp', 'fsdp'))
- tokens_grad: bfloat16 [1024, 40, 768], P(('dp', 'fsdp'))
- patches_grad: bfloat16 [128, 145, 1024], P(('dp', 'fsdp'))
- self_query_grad: float32 [768, 768], P(('dp', 'fsdp'))
- query_bias_grad: float32 [768], P(('dp', 'fsdp'))
- self_key_grad: float32 [768, 768], P(('dp', 'fsdp'))
- self_value_grad: float32 [768, 768], P(('dp', 'fsdp'))
- value_bias_grad: float32 [768], P(('dp', 'fsdp'))
- self_output_grad: float32 [768, 768], P(('dp', 'fsdp'))
- output_bias_grad: float32 [768], P(('dp', 'fsdp'))
- first_norm_gain_gradient: float32 [768], P(('dp', 'fsdp'))
- first_shift_grad: float32 [768], P(('dp', 'fsdp'))
- patch_proj_grad: float32 [1024, 768], P(('dp', 'fsdp'))
- patch_bias_grad: float32 [768], P(('dp', 'fsdp'))
- cross_query_grad: float32 [768, 768], P(('dp', 'fsdp'))
- probe_bias_grad: float32 [768], P(('dp', 'fsdp'))
- cross_key_grad: float32 [768, 768], P(('dp', 'fsdp'))
- cross_value_grad: float32 [768, 768], P(('dp', 'fsdp'))
- content_bias_grad: float32 [768], P(('dp', 'fsdp'))
- cross_output_grad: float32 [768, 768], P(('dp', 'fsdp'))
- cross_attention_bias_gradient: float32 [768], P(('dp', 'fsdp'))
- second_gain_grad: float32 [768], P(('dp', 'fsdp'))
- second_shift_grad: float32 [768], P(('dp', 'fsdp'))
- widen_weight_grad: float32 [768, 3072], P(('dp', 'fsdp'))
- widen_bias_grad: float32 [3072], P(('dp', 'fsdp'))
- narrow_weight_grad: float32 [3072, 768], P(('dp', 'fsdp'))
- narrow_bias_grad: float32 [768], P(('dp', 'fsdp'))
- third_gain_grad: float32 [768], P(('dp', 'fsdp'))
- third_shift_grad: float32 [768], P(('dp', 'fsdp'))
The draws below stay inside these ranges and needn't reach their ends.
Inputs may be any that keep to these rules, and one draw needn't show every extreme that they name: Among the 32 rows of one device at most 8 name the same owner, and among the devices with one fsdp index one owner is named by exactly 8 rows of each of them.
All inputs are finite; a program needn't handle non-finite values.
Results may differ from the reference program's by a relative error of at most 0.024.
Values may be sent and summed in bfloat16 or wider, within the bound.
A program may use at most 384 MiB of HBM per device.

```python
import math
import jax
import jax.numpy as jnp
import numpy as np
from jax import lax

D = 768
HEADS = 12
FF = 3072
PW = 1024
P_SIZE = 145
ROW = 40
R_DEV = 32
IMG_DEV = 4
CAP = 8
ROWS = 1024
IMAGE_TOTAL = 128
N_DP = 8
N_FSDP = 4


def draw_owner(key, part):
    devices = ROWS // R_DEV
    hot_key, pick_key = jax.random.split(jax.random.fold_in(key, 7))
    hot_group = jax.random.randint(hot_key, (N_FSDP,), 0, N_DP)
    hot = hot_group[jnp.arange(devices) % N_FSDP]
    others = jnp.repeat(jnp.arange(N_DP - 1, dtype=jnp.int32), CAP)

    def one_device(dev_key, hot_owner):
        first_key, second_key = jax.random.split(dev_key)
        chosen = jax.random.permutation(first_key, others)[:R_DEV - CAP]
        chosen = chosen + (chosen >= hot_owner).astype(jnp.int32)
        listed = jnp.concatenate([jnp.full((CAP,), hot_owner, jnp.int32), chosen])
        return jax.random.permutation(second_key, listed)
    keys = jax.random.split(pick_key, devices)
    return jax.vmap(one_device)(keys, hot).reshape(ROWS).astype(jnp.int32)


def plant(entries, own_key, least, largest):
    extent = entries.shape
    index_at = [jax.random.randint(jax.random.fold_in(own_key, axis), (), 0, extent[axis]) for axis in range(len(extent))]
    entries = entries.at[tuple(index_at)].set(least)
    longest = extent.index(max(extent))
    index_at[longest] = (index_at[longest] + 1) % extent[longest]
    return entries.at[tuple(index_at)].set(largest)


def level_of(rng, shape, shards, smallest, high):
    level = 1.0
    for dim, parts in shards:
        draws = jax.random.uniform(jax.random.fold_in(jax.random.fold_in(rng, 6), dim), (parts,), jnp.float32, smallest / len(shards), high / len(shards))
        level = level * jnp.repeat(jnp.exp(draws), shape[dim] // parts).reshape((-1,) + (1,) * (len(shape) - 1 - dim))
    return level


def profile(amount, total, most, skew):
    portions = [(1 << 20) // math.isqrt(rank ** skew) + 1 for rank in range(2, amount + 1)]
    rest, holding = total - most - (amount - 1), [1] * (amount - 1)
    while rest > 0:
        free = [i for i in range(amount - 1) if holding[i] < most]
        pool, left = sum([portions[i] for i in free]), rest
        for i in free:
            extra = min(most - holding[i], max(1, left * portions[i] // pool), rest)
            holding[i] = holding[i] + extra
            rest = rest - extra
    return np.array([most] + holding)


def uneven(rng, count, total, most, slope):
    if count == 2:
        one = jax.random.randint(rng, (), max(1, total - most), min(most, total - 1) + 1)
        return jnp.stack([one, total - one])
    sizes = jnp.asarray(profile(count, total, most, slope), jnp.int32)
    couples = (count - 1) // 2
    giver, receiver = sizes[1:1 + 2 * couples:2], sizes[2:2 + 2 * couples:2]
    slack = jnp.minimum(giver - 1, most - receiver)
    shifted = jax.random.randint(jax.random.fold_in(rng, 1), (couples,), 0, 1 << 20) % (slack + 1)
    sizes = sizes.at[1:1 + 2 * couples:2].set(giver - shifted).at[2:2 + 2 * couples:2].set(receiver + shifted)
    return sizes[jax.random.permutation(jax.random.fold_in(rng, 2), count)]


def bell_draw(rng, shape, deviation, most, shards=(), kind=jnp.bfloat16):
    values = jax.random.normal(rng, shape, jnp.float32) * deviation
    if len(shards) > 0:
        values = level_of(rng, shape, shards, -0.22, 0.18) * values
    return jnp.clip(values, min=-most, max=most).astype(kind)


def setup_inputs(seed: int = 0) -> dict:
    key_of = jax.random.split(jax.random.key(seed), 33)
    return {
        "tokens": bell_draw(key_of[0], (ROWS, ROW, D), 1.0, 6.0, ((0, 32),)),
        "patches": bell_draw(key_of[1], (IMAGE_TOTAL, P_SIZE, PW), 1.0, 6.0, ((0, 32),)),
        "segments": jax.vmap(lambda own: jnp.searchsorted(jnp.cumsum(uneven(own, 4, ROW, ROW // 2, 0)), jnp.arange(ROW), side="right"))(jax.random.split(key_of[2], ROWS)).reshape((ROWS, ROW)).astype(jnp.int32),
        "owner": draw_owner(jax.random.fold_in(key_of[32], 71), 0),
        "image_slot": plant(jax.random.randint(key_of[4], (ROWS,), 0, IMG_DEV), jax.random.fold_in(key_of[4], 1), 0, IMG_DEV - 1).astype(jnp.int32),
        "out_grad": bell_draw(key_of[5], (ROWS, ROW, D), 1.0, 6.0, ((0, 32),)),
        "self_query": bell_draw(key_of[6], (D, D), D ** -0.5, 0.21875, ((0, 32),)),
        "query_bias": bell_draw(key_of[7], (D,), 0.5, 3.0, ((0, 32),)),
        "self_key": bell_draw(key_of[8], (D, D), D ** -0.5, 0.21875, ((0, 32),)),
        "self_value": bell_draw(key_of[9], (D, D), D ** -0.5, 0.21875, ((0, 32),)),
        "value_bias": bell_draw(key_of[10], (D,), 0.5, 3.0, ((0, 32),)),
        "self_output": bell_draw(key_of[11], (D, D), (D // 9) ** -0.5, 0.625, ((0, 32),)),
        "output_bias": bell_draw(key_of[12], (D,), 0.5, 3.0, ((0, 32),)),
        "first_gain": jnp.clip(1.0 + 0.15 * jax.random.normal(key_of[13], (D,), jnp.float32), 0.25, 1.75).astype(jnp.bfloat16),
        "first_norm_bias": bell_draw(key_of[14], (D,), 0.4, 3.0, ((0, 32),)),
        "patch_proj": bell_draw(key_of[15], (PW, D), PW ** -0.5, 0.1875, ((0, 32),)),
        "patch_bias": bell_draw(key_of[16], (D,), 0.5, 3.0, ((0, 32),)),
        "cross_query": bell_draw(key_of[17], (D, D), D ** -0.5, 0.21875, ((0, 32),)),
        "probe_bias": bell_draw(key_of[18], (D,), 0.5, 3.0, ((0, 32),)),
        "cross_key": bell_draw(key_of[19], (D, D), D ** -0.5, 0.21875, ((0, 32),)),
        "cross_value": bell_draw(key_of[20], (D, D), D ** -0.5, 0.21875, ((0, 32),)),
        "content_bias": bell_draw(key_of[21], (D,), 0.5, 3.0, ((0, 32),)),
        "cross_output": bell_draw(key_of[22], (D, D), (D // 36) ** -0.5, 1.25, ((0, 32),)),
        "cross_bias": bell_draw(key_of[23], (D,), 0.5, 3.0, ((0, 32),)),
        "second_gain": jnp.clip(1.0 + 0.15 * jax.random.normal(key_of[24], (D,), jnp.float32), 0.25, 1.75).astype(jnp.bfloat16),
        "second_shift": bell_draw(key_of[25], (D,), 0.4, 3.0, ((0, 32),)),
        "widen_weight": bell_draw(key_of[26], (D, FF), D ** -0.5, 0.21875, ((0, 32),)),
        "widen_bias": bell_draw(key_of[27], (FF,), 0.5, 3.0, ((0, 32),)),
        "narrow_weight": bell_draw(key_of[28], (FF, D), (FF // 2) ** -0.5, 0.15625, ((0, 32),)),
        "narrow_bias": bell_draw(key_of[29], (D,), 0.5, 3.0, ((0, 32),)),
        "third_gain": jnp.clip(1.0 + 0.15 * jax.random.normal(key_of[30], (D,), jnp.float32), 0.25, 1.75).astype(jnp.bfloat16),
        "third_shift": bell_draw(key_of[31], (D,), 0.4, 3.0, ((0, 32),)),
    }


@jax.custom_vjp
def low(v):
    return lax.optimization_barrier(v.astype(jnp.bfloat16)).astype(jnp.float32)

@jax.custom_vjp
def low_back(v):
    return v

def retained_lower_part(v):
    return (low(v), None)

def low_pass(kept, grad):
    return (grad,)

def back_keep(v):
    return (v, None)

def back_low(kept, grad):
    return (low(grad),)
low.defvjp(retained_lower_part, low_pass)
low_back.defvjp(back_keep, back_low)
norm_eps = 1e-06
neg_fill = -1000000000.0

def both(value):
    return low_back(low(value))

def matmul(left, right):
    return jnp.dot(left, right, precision=lax.Precision.HIGHEST)

def layer_norm(value, gain, shift):
    mean = lax.optimization_barrier(jnp.mean(value, -1, keepdims=True))
    centred = value - mean
    spread = lax.optimization_barrier(jnp.mean(centred * centred, -1, keepdims=True))
    return centred * lax.rsqrt(spread + norm_eps) * gain + shift

def attention(query, keys, values, mask):
    count, length, width = query.shape
    points = keys.shape[1]
    size = width // HEADS
    heads_q = query.reshape(count, length, HEADS, size)
    heads_k = keys.reshape(count, points, HEADS, size)
    heads_v = values.reshape(count, points, HEADS, size)
    scores = jnp.einsum('blhe,bmhe->bhlm', heads_q, heads_k, precision=lax.Precision.HIGHEST) * size ** (-0.5)
    scores = low_back(scores)
    if mask is not None:
        scores = jnp.where(mask[:, None], scores, neg_fill)
    top = lax.optimization_barrier(jnp.max(scores, -1, keepdims=True))
    expd = jnp.exp(scores - top)
    probs = low(expd / lax.optimization_barrier(jnp.sum(expd, -1, keepdims=True)))
    mixed = jnp.einsum('bhlm,bmhe->blhe', probs, heads_v, precision=lax.Precision.HIGHEST)
    return mixed.reshape(count, length, width)

def forward(tokens, patches, weights, segments, images):
    self_query, query_bias, self_key, self_value, value_bias, self_output, output_bias, first_gain, first_norm_bias, patch_proj, patch_bias, cross_query, probe_bias, cross_key, cross_value, content_bias, cross_output, cross_bias, second_gain, second_shift, widen_weight, widen_bias, narrow_weight, narrow_bias, third_gain, third_shift = weights
    points = patches.shape[1]
    projected = both(matmul(patches.reshape(-1, PW), patch_proj) + patch_bias)
    image_keys = both(matmul(projected, cross_key)).reshape(-1, points, D)
    image_values = both(matmul(projected, cross_value) + content_bias).reshape(-1, points, D)

    def one_block(pieces):
        block_rows, block_segments, block_images = pieces
        count = block_rows.shape[0]
        flat = block_rows.reshape(-1, D)
        query = both(matmul(flat, self_query) + query_bias).reshape(count, ROW, D)
        key = both(matmul(flat, self_key)).reshape(count, ROW, D)
        value = both(matmul(flat, self_value) + value_bias).reshape(count, ROW, D)
        mask = block_segments[:, :, None] == block_segments[:, None, :]
        attended = both(attention(query, key, value, mask)).reshape(-1, D)
        branch = low_back(matmul(attended, self_output) + output_bias)
        first = layer_norm(flat + branch, first_gain, first_norm_bias)
        probe = both(matmul(low(first), cross_query) + probe_bias).reshape(count, ROW, D)
        crossed = both(attention(probe, image_keys[block_images], image_values[block_images], None)).reshape(-1, D)
        branch_two = low_back(matmul(crossed, cross_output) + cross_bias)
        second = both(layer_norm(first + branch_two, second_gain, second_shift))
        inner = low_back(matmul(second, widen_weight) + widen_bias)
        active = low(jax.nn.gelu(inner, approximate=False))
        branch_three = low_back(matmul(active, narrow_weight) + narrow_bias)
        third = layer_norm(second + branch_three, third_gain, third_shift)
        return third.reshape(count, ROW, D)
    blocks = tokens.shape[0] // R_DEV
    layer_result = lax.map(jax.checkpoint(one_block), (tokens.reshape(blocks, R_DEV, ROW, D), segments.reshape(blocks, R_DEV, ROW), images.reshape(blocks, R_DEV)))
    return layer_result.reshape(-1, ROW, D)

def reference(tokens, patches, segments, owner, image_slot, out_grad, self_query, query_bias, self_key, self_value, value_bias, self_output, output_bias, first_gain, first_norm_bias, patch_proj, patch_bias, cross_query, probe_bias, cross_key, cross_value, content_bias, cross_output, cross_bias, second_gain, second_shift, widen_weight, widen_bias, narrow_weight, narrow_bias, third_gain, third_shift):
    weights = tuple((item.astype(jnp.float32) for item in (self_query, query_bias, self_key, self_value, value_bias, self_output, output_bias, first_gain, first_norm_bias, patch_proj, patch_bias, cross_query, probe_bias, cross_key, cross_value, content_bias, cross_output, cross_bias, second_gain, second_shift, widen_weight, widen_bias, narrow_weight, narrow_bias, third_gain, third_shift)))
    device = jnp.arange(ROWS, dtype=jnp.int32) // R_DEV
    images = ((owner * N_FSDP + device % N_FSDP) * IMG_DEV + image_slot).astype(jnp.int32)

    def apply_layer(tok_values, patch_values, weight_values):
        return forward(tok_values, patch_values, weight_values, segments, images)
    layer_result, pullback = jax.vjp(apply_layer, tokens.astype(jnp.float32), patches.astype(jnp.float32), weights)
    grad_tokens, grad_patches, grad_weights = pullback(out_grad.astype(jnp.float32))
    return (layer_result.astype(jnp.bfloat16), grad_tokens.astype(jnp.bfloat16), grad_patches.astype(jnp.bfloat16), *grad_weights)
```

```python
import functools

import jax
import jax.numpy as jnp
from jax import lax
from jax.experimental import pallas as pl
from jax.experimental.pallas import tpu as pltpu
from jax.sharding import PartitionSpec as P

HEADS = 12
AXES = ("dp", "fsdp")
BF = jnp.bfloat16
F32 = jnp.float32
norm_eps = 1e-06
mask_fill = -1000000000.0

WINDOWS = ((0, 0), (128, 64), (384, 0), (512, 64))

ERFC_POLE = 0.3
ERFC_POLY = (
    0.16918935391840687,
    0.17069093065701252,
    0.14852123834149009,
    0.214181489197379,
    -0.09282620690981414,
    0.5449671942862269,
    -0.5097726086693966,
    0.4843018450108595,
    -0.12925324449453648,
)
INV_SQRT2 = 0.7071067811865476
INV_SQRT2PI = 0.3989422804014327


def nn(left, right):
    return lax.dot_general(left, right, (((1,), (0,)), ((), ())), preferred_element_type=F32)


def nt(left, right):
    return lax.dot_general(left, right, (((1,), (1,)), ((), ())), preferred_element_type=F32)


def tn(left, right):
    return lax.dot_general(left, right, (((0,), (0,)), ((), ())), preferred_element_type=F32)


def norm_parts(value):
    mean = jnp.mean(value, -1, keepdims=True)
    centred = value - mean
    spread = jnp.mean(centred * centred, -1, keepdims=True)
    inv = lax.rsqrt(spread + norm_eps)
    return centred * inv, inv


def norm_back(grad, gain, xhat, inv):
    scaled = grad * gain
    first = jnp.mean(scaled, -1, keepdims=True)
    second = jnp.mean(scaled * xhat, -1, keepdims=True)
    return inv * (scaled - first - xhat * second)


def gelu_parts(v):
    z = jnp.abs(v) * INV_SQRT2
    t = 1.0 / (1.0 + ERFC_POLE * z)
    poly = jnp.full_like(t, ERFC_POLY[-1])
    for c in ERFC_POLY[-2::-1]:
        poly = poly * t + c
    bell = jnp.exp(-0.5 * (v * v))
    half = (0.5 * bell) * (t * poly)
    cdf = jnp.where(v >= 0, 1.0 - half, half)
    return v * cdf, cdf + (v * INV_SQRT2PI) * bell


def stack_heads(full, index):
    base, off = WINDOWS[index]
    win = full[:, base : base + 256]
    lane = lax.broadcasted_iota(jnp.int32, win.shape, 1)
    blocks = []
    for h in range(3):
        lo = off + 64 * h
        blocks.append(jnp.where((lane >= lo) & (lane < lo + 64), win, 0.0))
    return jnp.concatenate(blocks, 0).astype(BF)


def unstack_heads(stacked, index, rows):
    _, off = WINDOWS[index]
    lane = lax.broadcasted_iota(jnp.int32, (rows, 256), 1)
    out = None
    for h in range(3):
        lo = off + 64 * h
        part = jnp.where((lane >= lo) & (lane < lo + 64), stacked[rows * h : rows * (h + 1)], 0.0)
        out = part if out is None else out + part
    return out


def join_windows(parts):
    a, b, c, d = parts
    return jnp.concatenate(
        [
            a[:, :128],
            a[:, 128:] + b[:, :128],
            b[:, 128:],
            c[:, :128],
            c[:, 128:] + d[:, :128],
            d[:, 128:],
        ],
        1,
    )


def self_forward(
    tok, bias, wq, wk, wv, wo, wc, qb, vb, ob, g1, b1, pb, q_o, k_o, v_o, p_o, att_o, u1_o, f_o, pr_o, att_s
):
    rb, length, width = tok.shape
    n = rb * length
    x32 = tok[...].astype(F32).reshape(n, width)
    x = x32.astype(BF)
    q = (nn(x, wq[...]) + qb[...]).astype(BF)
    k = nn(x, wk[...]).astype(BF)
    v = (nn(x, wv[...]) + vb[...]).astype(BF)
    q_o[...] = q.astype(F32).reshape(rb, length, width).astype(BF)
    k_o[...] = k.astype(F32).reshape(rb, length, width).astype(BF)
    v_o[...] = v.astype(F32).reshape(rb, length, width).astype(BF)

    def row(r, carry):
        qr = q_o[r].astype(F32) * 0.125
        kr = k_o[r].astype(F32)
        vr = v_o[r].astype(F32)
        outs = []
        for i in range(4):
            base = WINDOWS[i][0]
            qs = stack_heads(qr, i)
            kw = kr[:, base : base + 256].astype(BF)
            vw = vr[:, base : base + 256].astype(BF)
            st = nt(kw, qs) + bias[r]
            top = jnp.max(st, 0, keepdims=True)
            e = jnp.exp(st - top)
            p = (e * (1.0 / jnp.sum(e, 0, keepdims=True))).astype(BF)
            p_o[r, i] = p
            outs.append(unstack_heads(tn(p, vw), i, length))
        att_s[r] = join_windows(outs)
        return carry

    lax.fori_loop(0, rb, row, 0)
    att32 = att_s[...]
    att_o[...] = att32.astype(BF)
    att = att32.reshape(n, width).astype(BF)
    u1 = x32 + nn(att, wo[...]) + ob[...]
    u1_o[...] = u1.reshape(rb, length, width)
    xhat, _ = norm_parts(u1)
    first = (xhat * g1[...] + b1[...]).astype(BF)
    f_o[...] = first.astype(F32).reshape(rb, length, width).astype(BF)
    pr_o[...] = (nn(first, wc[...]) + pb[...]).reshape(rb, length, width).astype(BF)


def cross_forward(starts, order, proj, wk, wv, cb, probe, k_o, v_o, p_o, mix_o, pr_s):
    i = pl.program_id(0)
    points = proj.shape[1]
    padded = k_o.shape[1]
    length = probe.shape[1]

    @pl.when(i == 0)
    def _():
        pr_s[...] = jnp.zeros_like(pr_s)

    lo, hi = starts[i], starts[i + 1]

    @pl.when(hi > lo)
    def _():
        pr_s[0:points, :] = proj[0]
        pr = pr_s[...]
        k_o[0] = nn(pr, wk[...]).astype(BF)
        v_o[0] = (nn(pr, wv[...]) + cb[...]).astype(BF)

        def row(j, carry):
            r = order[j]
            qr = probe[r].astype(F32) * 0.125
            outs = []
            for g in range(4):
                base = WINDOWS[g][0]
                qs = stack_heads(qr, g)
                st = nt(k_o[0, :, base : base + 256], qs)
                point = lax.broadcasted_iota(jnp.int32, st.shape, 0)
                st = jnp.where(point < points, st, -1e30)
                top = jnp.max(st, 0, keepdims=True)
                e = jnp.exp(st - top)
                p = (e * (1.0 / jnp.sum(e, 0, keepdims=True))).astype(BF)
                p_o[r, g] = p
                outs.append(unstack_heads(tn(p, v_o[0, :, base : base + 256]), g, length))
            mix_o[r] = join_windows(outs).astype(BF)
            return carry

        lax.fori_loop(lo, hi, row, 0)


def tail_kernel(
    u1, mix, og, wco, w1, w2, g1, b1, cb, g2, s2, wb, nb, g3, s3,
    out_o, act_o, gi_o, sec_o, gb3_o, gm_o, gb2_o, gc_o, vec_o, wbg_o,
    act_s, gp_s, acc_s,
):
    step = pl.program_id(0)
    rb, length, width = u1.shape
    n = rb * length
    chunks = w1.shape[0]

    @pl.when(step == 0)
    def _():
        vec_o[...] = jnp.zeros_like(vec_o)
        wbg_o[...] = jnp.zeros_like(wbg_o)

    def flat(ref):
        return ref[...].astype(F32).reshape(n, width)

    def fold(value):
        return value.reshape(rb, length, width)

    xhat1, _ = norm_parts(flat(u1))
    first = xhat1 * g1[...] + b1[...]
    u2 = first + nn(flat(mix).astype(BF), wco[...]) + cb[...]
    xhat2, inv2 = norm_parts(u2)
    second = (xhat2 * g2[...] + s2[...]).astype(BF)
    sec32 = second.astype(F32)
    sec_o[...] = fold(sec32).astype(BF)
    acc_s[...] = sec32 + nb[...]

    def up(c, carry):
        inner = nn(second, w1[c]) + wb[c]
        act, slope = gelu_parts(inner)
        act = act.astype(BF)
        gp_s[c] = slope
        act_o[c] = act
        acc_s[...] += nn(act, w2[c])
        return carry

    lax.fori_loop(0, chunks, up, 0)
    xhat3, inv3 = norm_parts(acc_s[...])
    out_o[...] = fold(xhat3 * g3[...] + s3[...]).astype(BF)
    y = flat(og)
    grad_summed = norm_back(y, g3[...], xhat3, inv3)
    gb3 = grad_summed.astype(BF)
    gb3f = gb3.astype(F32)
    gb3_o[...] = fold(gb3f).astype(BF)
    vec_o[0:1] += jnp.sum(y * xhat3, 0, keepdims=True)
    vec_o[1:2] += jnp.sum(y, 0, keepdims=True)
    vec_o[2:3] += jnp.sum(gb3f, 0, keepdims=True)
    acc_s[...] = grad_summed

    def down(c, carry):
        gi = (nt(gb3, w2[c]) * gp_s[c]).astype(BF)
        gi_o[c] = gi
        wbg_o[c] += jnp.sum(gi.astype(F32), 0, keepdims=True)
        acc_s[...] += nt(gi, w1[c])
        return carry

    lax.fori_loop(0, chunks, down, 0)
    y2 = acc_s[...].astype(BF).astype(F32)
    gm = norm_back(y2, g2[...], xhat2, inv2)
    gm_o[...] = fold(gm)
    gb2 = gm.astype(BF)
    gb2f = gb2.astype(F32)
    gb2_o[...] = fold(gb2f).astype(BF)
    vec_o[3:4] += jnp.sum(y2 * xhat2, 0, keepdims=True)
    vec_o[4:5] += jnp.sum(y2, 0, keepdims=True)
    vec_o[5:6] += jnp.sum(gb2f, 0, keepdims=True)
    gc_o[...] = fold(nt(gb2, wco[...])).astype(BF)


def cross_backward(
    starts, order, proj, keys, values, wk, wv, probe, grad, probs,
    dpr_o, dproj_o, dwk_o, dwv_o, dcb_o,
    pr_s, dk_s, dv_s, dwk_s, dwv_s,
):
    i = pl.program_id(0)
    points = proj.shape[1]
    length = probe.shape[1]

    @pl.when(i == 0)
    def _():
        pr_s[...] = jnp.zeros_like(pr_s)
        dwk_s[...] = jnp.zeros_like(dwk_s)
        dwv_s[...] = jnp.zeros_like(dwv_s)
        dcb_o[...] = jnp.zeros_like(dcb_o)

    lo, hi = starts[i], starts[i + 1]

    @pl.when(hi == lo)
    def _():
        dproj_o[...] = jnp.zeros_like(dproj_o)

    @pl.when(hi > lo)
    def _():
        dk_s[...] = jnp.zeros_like(dk_s)
        dv_s[...] = jnp.zeros_like(dv_s)

        def row(j, carry):
            r = order[j]
            qr = probe[r].astype(F32) * 0.125
            gr = grad[r].astype(F32)
            outs = []
            for g in range(4):
                base = WINDOWS[g][0]
                qs = stack_heads(qr, g)
                gs = stack_heads(gr, g)
                pb = probs[r, g]
                p = pb.astype(F32)
                dp = nt(values[0, :, base : base + 256], gs)
                w = jnp.sum(dp * p, 0, keepdims=True)
                ds = (p * (dp - w)).astype(BF)
                dk_s[:, base : base + 256] += nn(ds, qs)
                dv_s[:, base : base + 256] += nn(pb, gs)
                outs.append(unstack_heads(tn(ds, keys[0, :, base : base + 256]), g, length))
            dpr_o[r] = (join_windows(outs) * 0.125).astype(BF)
            return carry

        lax.fori_loop(lo, hi, row, 0)
        pr_s[0:points, :] = proj[0]
        pr = pr_s[...]
        dk = dk_s[...].astype(BF)
        dv = dv_s[...].astype(BF)
        dcb_o[0:1] += jnp.sum(dv.astype(F32), 0, keepdims=True)
        dproj = (nt(dk, wk[...]) + nt(dv, wv[...])).astype(BF)
        dproj_o[0] = dproj[0:points]
        dwk_s[...] += tn(pr, dk)
        dwv_s[...] += tn(pr, dv)

    @pl.when(i == pl.num_programs(0) - 1)
    def _():
        dwk_o[...] = dwk_s[...].astype(BF)
        dwv_o[...] = dwv_s[...].astype(BF)


def self_backward(
    gm, dpr, u1, q, k, v, probs, wq, wk, wv, wo, wc, g1,
    gb1_o, dq_o, dk_o, dv_o, tg_o, vec_o,
    ga_s, dq_s, dk_s, dv_s,
):
    step = pl.program_id(0)
    rb, length, width = u1.shape
    n = rb * length

    @pl.when(step == 0)
    def _():
        vec_o[...] = jnp.zeros_like(vec_o)

    def flat(ref):
        return ref[...].astype(F32).reshape(n, width)

    def fold(value):
        return value.reshape(rb, length, width)

    dpr32 = flat(dpr)
    grad_first = flat(gm) + nt(dpr32.astype(BF), wc[...])
    xhat, inv = norm_parts(flat(u1))
    low = norm_back(grad_first, g1[...], xhat, inv)
    gb1 = low.astype(BF)
    gb1f = gb1.astype(F32)
    gb1_o[...] = fold(gb1f).astype(BF)
    vec_o[0:1] += jnp.sum(grad_first * xhat, 0, keepdims=True)
    vec_o[1:2] += jnp.sum(grad_first, 0, keepdims=True)
    vec_o[2:3] += jnp.sum(gb1f, 0, keepdims=True)
    vec_o[3:4] += jnp.sum(dpr32, 0, keepdims=True)
    ga_s[...] = fold(nt(gb1, wo[...]).astype(BF).astype(F32))

    def row(r, carry):
        qr = q[r].astype(F32) * 0.125
        kr = k[r].astype(F32)
        vr = v[r].astype(F32)
        gr = ga_s[r]
        dqs, dks, dvs = [], [], []
        for i in range(4):
            base = WINDOWS[i][0]
            qs = stack_heads(qr, i)
            gs = stack_heads(gr, i)
            kw = kr[:, base : base + 256].astype(BF)
            vw = vr[:, base : base + 256].astype(BF)
            pb = probs[r, i]
            p = pb.astype(F32)
            dp = nt(vw, gs)
            w = jnp.sum(dp * p, 0, keepdims=True)
            ds = (p * (dp - w)).astype(BF)
            dks.append(nn(ds, qs))
            dvs.append(nn(pb, gs))
            dqs.append(unstack_heads(tn(ds, kw), i, length))
        dq_s[r] = join_windows(dqs) * 0.125
        dk_s[r] = join_windows(dks)
        dv_s[r] = join_windows(dvs)
        return carry

    lax.fori_loop(0, rb, row, 0)
    dq = dq_s[...].reshape(n, width).astype(BF)
    dk = dk_s[...].reshape(n, width).astype(BF)
    dv = dv_s[...].reshape(n, width).astype(BF)
    dq_o[...] = dq_s[...].astype(BF)
    dk_o[...] = dk_s[...].astype(BF)
    dv_o[...] = dv_s[...].astype(BF)
    vec_o[4:5] += jnp.sum(dq.astype(F32), 0, keepdims=True)
    vec_o[5:6] += jnp.sum(dv.astype(F32), 0, keepdims=True)
    total = low + nt(dq, wq[...]) + nt(dk, wk[...]) + nt(dv, wv[...])
    tg_o[...] = fold(total).astype(BF)


def sds(shape, dtype):
    return jax.ShapeDtypeStruct(shape, dtype)


def whole(shape, *, single=True):
    zeros = (0,) * len(shape)
    mode = pl.Buffered(1) if single else None
    return pl.BlockSpec(shape, lambda i, *_: zeros, pipeline_mode=mode)


def rows_block(shape, rb):
    rest = tuple(shape[1:])
    return pl.BlockSpec((rb,) + rest, lambda i, *_: (i,) + (0,) * len(rest))


def params(mib):
    return pltpu.CompilerParams(
        dimension_semantics=("arbitrary",), vmem_limit_bytes=mib * 1024 * 1024
    )


def cost(flops, bytes_accessed):
    return pl.CostEstimate(flops=int(flops), bytes_accessed=int(bytes_accessed), transcendentals=0)


def gather(value, axis):
    return lax.all_gather(value, AXES, axis=axis, tiled=True)


def on_device(
    tokens, patches, segments, owner, image_slot, out_grad,
    self_query, query_bias, self_key, self_value, value_bias, self_output, output_bias,
    first_gain, first_norm_bias, patch_proj, patch_bias, cross_query, probe_bias, cross_key,
    cross_value, content_bias, cross_output, cross_bias, second_gain, second_shift,
    widen_weight, widen_bias, narrow_weight, narrow_bias, third_gain, third_shift,
):
    rows, length, width = tokens.shape
    images, points, pwidth = patches.shape
    groups = lax.axis_size("dp")
    shards = groups * lax.axis_size("fsdp")
    total_images = groups * images
    hidden = widen_weight.shape[1]
    chunks = hidden // width
    sr = self_query.shape[0]
    wr = widen_bias.shape[0]

    vec_list = (
        query_bias, value_bias, output_bias, first_gain, first_norm_bias, patch_bias, probe_bias,
        content_bias, cross_bias, second_gain, second_shift, narrow_bias, third_gain, third_shift,
    )
    packed = jnp.concatenate(vec_list + (widen_bias,))
    packed = jnp.pad(packed, (0, width - packed.shape[0]))[None]
    packed_all = gather(jnp.pad(packed, ((0, 7), (0, 0))), 0).reshape(shards, 8, width)[:, 0].astype(F32)
    vecs = [packed_all[:, sr * j : sr * (j + 1)].reshape(1, width) for j in range(len(vec_list))]
    (qb, vb, ob, g1, b1, pab, prb, cob, crb, g2, s2, nab, g3, s3) = vecs
    wb = packed_all[:, sr * len(vec_list) : sr * len(vec_list) + wr]
    wb = wb.reshape(shards, chunks, sr).transpose(1, 0, 2).reshape(chunks, 1, width)

    patch_full = gather(patch_proj, 0)
    w_a = gather(
        jnp.stack([self_query, self_key, self_value, self_output, cross_query, cross_key, cross_value, cross_output]), 1
    )
    widen_slabs = widen_weight.reshape(sr, shards, chunks, sr).transpose(2, 0, 1, 3).reshape(chunks, sr, width)
    narrow_slabs = narrow_weight.reshape(chunks, sr, width)
    w_b = gather(jnp.concatenate([widen_slabs, narrow_slabs], 0), 1)

    projected = (
        lax.dot_general(patches, patch_full, (((2,), (0,)), ((), ())), preferred_element_type=F32) + pab
    ).astype(BF)
    proj_all = lax.all_gather(projected, "dp", axis=0, tiled=True)

    image = owner * images + image_slot
    idx = jnp.arange(rows, dtype=jnp.int32)
    before = (image[None, :] < image[:, None]) | ((image[None, :] == image[:, None]) & (idx[None, :] < idx[:, None]))
    rank = jnp.sum(before.astype(jnp.int32), 1)
    order = jnp.sum(jnp.where(rank[:, None] == idx[None, :], idx[:, None], 0), 0).astype(jnp.int32)
    starts = jnp.sum((image[None, :] < jnp.arange(total_images + 1, dtype=jnp.int32)[:, None]).astype(jnp.int32), 1)

    same = segments[:, :, None] == segments[:, None, :]
    bias = jnp.where(same, 0.0, mask_fill).astype(F32)
    bias = jnp.concatenate([bias, bias, bias], 2)

    rb = 8 if rows % 8 == 0 else 1
    grid = (rows // rb,)
    tok_sh = (rows, length, width)
    slab = (width, width)

    def wspec(j):
        return pl.BlockSpec((None, width, width), lambda i, *_: (j, 0, 0), pipeline_mode=pl.Buffered(1))

    vspec = whole((1, width))
    tb = rows_block(tok_sh, rb)
    self_p = (rows, 4, length, 3 * length)
    q, k, v, probs, attended, u1, first_low, probe = pl.pallas_call(
        self_forward,
        grid=grid,
        in_specs=[tb, rows_block((rows, length, 3 * length), rb)]
        + [wspec(0), wspec(1), wspec(2), wspec(3), wspec(4)]
        + [vspec] * 6,
        out_specs=[tb, tb, tb, rows_block(self_p, rb), tb, tb, tb, tb],
        out_shape=[
            sds(tok_sh, BF), sds(tok_sh, BF), sds(tok_sh, BF), sds(self_p, BF),
            sds(tok_sh, BF), sds(tok_sh, F32), sds(tok_sh, BF), sds(tok_sh, BF),
        ],
        scratch_shapes=[pltpu.VMEM((rb, length, width), F32)],
        compiler_params=params(48),
        cost_estimate=cost(11 * rows * length * width * width, 30e6),
        name="self_forward",
    )(tokens, bias, w_a, w_a, w_a, w_a, w_a, qb, vb, ob, g1, b1, prb)

    padded = -(-points // 16) * 16
    kv_sh = (total_images, padded, width)
    cross_p = (rows, 4, padded, 3 * length)
    img_spec = pl.BlockSpec((1, points, width), lambda i, *_: (i, 0, 0))
    kv_spec = pl.BlockSpec((1, padded, width), lambda i, *_: (i, 0, 0))
    image_keys, image_values, cprobs, mixed = pl.pallas_call(
        cross_forward,
        grid_spec=pltpu.PrefetchScalarGridSpec(
            num_scalar_prefetch=2,
            grid=(total_images,),
            in_specs=[img_spec, wspec(5), wspec(6), vspec, whole(tok_sh)],
            out_specs=[kv_spec, kv_spec, whole(cross_p), whole(tok_sh)],
            scratch_shapes=[pltpu.VMEM((padded, width), BF)],
        ),
        out_shape=[sds(kv_sh, BF), sds(kv_sh, BF), sds(cross_p, BF), sds(tok_sh, BF)],
        compiler_params=params(48),
        cost_estimate=cost(4 * total_images * points * width * width, 40e6),
        name="cross_forward",
    )(starts, order, proj_all, w_a, w_a, cob, probe)

    def chunk_w(j):
        return pl.BlockSpec((chunks, width, width), lambda i, *_: (j, 0, 0), pipeline_mode=pl.Buffered(1))

    n_tok = rows * length
    hid_sh = (chunks, n_tok, width)
    hid_spec = pl.BlockSpec((chunks, rb * length, width), lambda i, *_: (0, i, 0))
    (output, active, grad_inner, second, gb3, grad_mid, gb2, grad_crossed, vec_t, wb_grad) = pl.pallas_call(
        tail_kernel,
        grid=grid,
        in_specs=[tb, tb, tb, wspec(7), chunk_w(0), chunk_w(1)]
        + [vspec] * 5
        + [whole((chunks, 1, width))]
        + [vspec] * 3,
        out_specs=[tb, hid_spec, hid_spec, tb, tb, tb, tb, tb, whole((8, width)), whole((chunks, 1, width))],
        out_shape=[
            sds(tok_sh, BF), sds(hid_sh, BF), sds(hid_sh, BF), sds(tok_sh, BF), sds(tok_sh, BF),
            sds(tok_sh, F32), sds(tok_sh, BF), sds(tok_sh, BF), sds((8, width), F32), sds((chunks, 1, width), F32),
        ],
        scratch_shapes=[
            pltpu.VMEM((8, 128), BF),
            pltpu.VMEM((chunks, rb * length, width), F32),
            pltpu.VMEM((rb * length, width), F32),
        ],
        compiler_params=params(56),
        cost_estimate=cost(18 * n_tok * width * width + 8 * n_tok * width * hidden, 50e6),
        name="tail",
    )(u1, mixed, out_grad, w_a, w_b, w_b, g1, b1, crb, g2, s2, wb, nab, g3, s3)

    dprobe, dproj, dwk, dwv, dcb = pl.pallas_call(
        cross_backward,
        grid_spec=pltpu.PrefetchScalarGridSpec(
            num_scalar_prefetch=2,
            grid=(total_images,),
            in_specs=[img_spec, kv_spec, kv_spec, wspec(5), wspec(6), whole(tok_sh), whole(tok_sh), whole(cross_p)],
            out_specs=[whole(tok_sh), img_spec, whole(slab), whole(slab), whole((8, width))],
            scratch_shapes=[
                pltpu.VMEM((padded, width), BF),
                pltpu.VMEM((padded, width), F32),
                pltpu.VMEM((padded, width), F32),
                pltpu.VMEM((width, width), F32),
                pltpu.VMEM((width, width), F32),
            ],
        ),
        out_shape=[sds(tok_sh, BF), sds((total_images, points, width), BF), sds(slab, BF), sds(slab, BF), sds((8, width), F32)],
        compiler_params=params(52),
        cost_estimate=cost(8 * total_images * points * width * width, 50e6),
        name="cross_backward",
    )(starts, order, proj_all, image_keys, image_values, w_a, w_a, probe, grad_crossed, cprobs)
    grad_projected = lax.psum_scatter(dproj, "dp", scatter_dimension=0, tiled=True)

    gb1, dq, dk, dv, tokens_grad, vec_s = pl.pallas_call(
        self_backward,
        grid=grid,
        in_specs=[tb, tb, tb, tb, tb, tb, rows_block(self_p, rb)]
        + [wspec(0), wspec(1), wspec(2), wspec(3), wspec(4)]
        + [vspec],
        out_specs=[tb, tb, tb, tb, tb, whole((8, width))],
        out_shape=[sds(tok_sh, BF)] * 5 + [sds((8, width), F32)],
        scratch_shapes=[pltpu.VMEM((rb, length, width), F32)] * 4,
        compiler_params=params(52),
        cost_estimate=cost(14 * n_tok * width * width, 40e6),
        name="self_backward",
    )(grad_mid, dprobe, u1, q, k, v, probs, w_a, w_a, w_a, w_a, w_a, g1)

    def wgrad(left, right):
        return tn(left.reshape(n_tok, width), right.reshape(n_tok, width)).astype(BF)

    grad_narrow = lax.dot_general(
        active, gb3.reshape(n_tok, width), (((1,), (0,)), ((), ())), preferred_element_type=F32
    ).astype(BF)
    grad_widen = jnp.stack([wgrad(second, grad_inner[c]) for c in range(chunks)])
    ffn_shard = lax.psum_scatter(
        jnp.concatenate([grad_widen, grad_narrow], 0), AXES, scatter_dimension=1, tiled=True
    ).astype(F32)

    patch_low = grad_projected
    grad_patch_proj = lax.dot_general(
        patches, patch_low, (((0, 1), (0, 1)), ((), ())), preferred_element_type=F32
    ).astype(BF)
    grad_patch_bias = jnp.sum(patch_low.astype(F32), (0, 1))[None]
    patches_grad = lax.dot_general(
        patch_low, patch_full, (((2,), (1,)), ((), ())), preferred_element_type=F32
    ).astype(BF)

    vec_grads = [
        vec_s[4:5], vec_s[5:6], vec_s[2:3], vec_s[0:1], vec_s[1:2], grad_patch_bias, vec_s[3:4], dcb[0:1],
        vec_t[5:6], vec_t[3:4], vec_t[4:5], vec_t[2:3], vec_t[0:1], vec_t[1:2],
    ]
    wb_flat = wb_grad.reshape(chunks, shards, sr).transpose(1, 0, 2).reshape(shards, wr)
    vec_rows = jnp.concatenate([item.reshape(shards, sr) for item in vec_grads] + [wb_flat], 1)
    vec_rows = jnp.pad(vec_rows, ((0, 0), (0, width - vec_rows.shape[1])))
    vec_shard = lax.psum_scatter(vec_rows, AXES, scatter_dimension=0, tiled=True)[0]

    slabs = jnp.stack(
        [
            wgrad(tokens, dq), wgrad(tokens, dk), wgrad(tokens, dv), wgrad(attended, gb1),
            wgrad(first_low, dprobe), dwk, dwv, wgrad(mixed, gb2),
        ]
    )
    slab_shard = lax.psum_scatter(slabs, AXES, scatter_dimension=1, tiled=True).astype(F32)
    patch_shard = lax.psum_scatter(grad_patch_proj, AXES, scatter_dimension=0, tiled=True).astype(F32)

    vg = [vec_shard[sr * j : sr * (j + 1)] for j in range(len(vec_list))]
    wbg = vec_shard[sr * len(vec_list) : sr * len(vec_list) + wr]
    widen_shard = ffn_shard[:chunks].reshape(chunks, sr, shards, sr).transpose(1, 2, 0, 3).reshape(sr, hidden)
    narrow_shard = ffn_shard[chunks:].reshape(chunks * sr, width)
    return (
        output, tokens_grad, patches_grad,
        slab_shard[0], vg[0], slab_shard[1], slab_shard[2], vg[1], slab_shard[3], vg[2], vg[3], vg[4],
        patch_shard, vg[5], slab_shard[4], vg[6], slab_shard[5], slab_shard[6], vg[7], slab_shard[7],
        vg[8], vg[9], vg[10], widen_shard, wbg, narrow_shard, vg[11], vg[12], vg[13],
    )


def solution(mesh):
    three, two, one = P(AXES, None, None), P(AXES, None), P(AXES)
    in_specs = (
        three, three, two, one, one, three,
        two, one, two, two, one, two, one, one, one, two, one, two, one, two,
        two, one, two, one, one, one, two, one, two, one, one, one,
    )
    out_specs = (
        three, three, three,
        two, one, two, two, one, two, one, one, one, two, one, two, one, two, two, one, two,
        one, one, one, two, one, two, one, one, one,
    )
    return jax.shard_map(on_device, mesh=mesh, in_specs=in_specs, out_specs=out_specs, check_vma=False)
```

```python
import functools

import jax
import jax.numpy as jnp
from jax import lax
from jax.experimental import pallas as pl
from jax.experimental.pallas import tpu as pltpu
from jax.sharding import PartitionSpec as P

HEADS = 12
AXES = ("dp", "fsdp")
BF = jnp.bfloat16
F32 = jnp.float32
norm_eps = 1e-06
mask_fill = -1000000000.0

WINDOWS = ((0, 0), (128, 64), (384, 0), (512, 64))

ERFC_POLE = 0.3
ERFC_POLY = (
    0.16918935391840687,
    0.17069093065701252,
    0.14852123834149009,
    0.214181489197379,
    -0.09282620690981414,
    0.5449671942862269,
    -0.5097726086693966,
    0.4843018450108595,
    -0.12925324449453648,
)
INV_SQRT2 = 0.7071067811865476
INV_SQRT2PI = 0.3989422804014327


def nn(left, right):
    return lax.dot_general(left, right, (((1,), (0,)), ((), ())), preferred_element_type=F32)


def nt(left, right):
    return lax.dot_general(left, right, (((1,), (1,)), ((), ())), preferred_element_type=F32)


def tn(left, right):
    return lax.dot_general(left, right, (((0,), (0,)), ((), ())), preferred_element_type=F32)


def norm_parts(value):
    mean = jnp.mean(value, -1, keepdims=True)
    centred = value - mean
    spread = jnp.mean(centred * centred, -1, keepdims=True)
    inv = lax.rsqrt(spread + norm_eps)
    return centred * inv, inv


def norm_back(grad, gain, xhat, inv):
    scaled = grad * gain
    first = jnp.mean(scaled, -1, keepdims=True)
    second = jnp.mean(scaled * xhat, -1, keepdims=True)
    return inv * (scaled - first - xhat * second)


def gelu_parts(v):
    z = jnp.abs(v) * INV_SQRT2
    t = 1.0 / (1.0 + ERFC_POLE * z)
    poly = jnp.full_like(t, ERFC_POLY[-1])
    for c in ERFC_POLY[-2::-1]:
        poly = poly * t + c
    bell = jnp.exp(-0.5 * (v * v))
    half = (0.5 * bell) * (t * poly)
    cdf = jnp.where(v >= 0, 1.0 - half, half)
    return v * cdf, cdf + (v * INV_SQRT2PI) * bell


def stack_heads(full, index):
    base, off = WINDOWS[index]
    win = full[:, base : base + 256]
    lane = lax.broadcasted_iota(jnp.int32, win.shape, 1)
    blocks = []
    for h in range(3):
        lo = off + 64 * h
        blocks.append(jnp.where((lane >= lo) & (lane < lo + 64), win, 0.0))
    return jnp.concatenate(blocks, 0).astype(BF)


def unstack_heads(stacked, index, rows):
    _, off = WINDOWS[index]
    lane = lax.broadcasted_iota(jnp.int32, (rows, 256), 1)
    out = None
    for h in range(3):
        lo = off + 64 * h
        part = jnp.where((lane >= lo) & (lane < lo + 64), stacked[rows * h : rows * (h + 1)], 0.0)
        out = part if out is None else out + part
    return out


def join_windows(parts):
    a, b, c, d = parts
    return jnp.concatenate(
        [
            a[:, :128],
            a[:, 128:] + b[:, :128],
            b[:, 128:],
            c[:, :128],
            c[:, 128:] + d[:, :128],
            d[:, 128:],
        ],
        1,
    )


def self_forward(
    tok, bias, wq, wk, wv, wo, wc, qb, vb, ob, g1, b1, pb, q_o, k_o, v_o, p_o, att_o, u1_o, f_o, pr_o, att_s
):
    rb, length, width = tok.shape
    n = rb * length
    x32 = tok[...].astype(F32).reshape(n, width)
    x = x32.astype(BF)
    q = (nn(x, wq[...]) + qb[...]).astype(BF)
    k = nn(x, wk[...]).astype(BF)
    v = (nn(x, wv[...]) + vb[...]).astype(BF)
    q_o[...] = q.astype(F32).reshape(rb, length, width).astype(BF)
    k_o[...] = k.astype(F32).reshape(rb, length, width).astype(BF)
    v_o[...] = v.astype(F32).reshape(rb, length, width).astype(BF)

    def row(r, carry):
        qr = q_o[r].astype(F32) * 0.125
        kr = k_o[r].astype(F32)
        vr = v_o[r].astype(F32)
        outs = []
        for i in range(4):
            base = WINDOWS[i][0]
            qs = stack_heads(qr, i)
            kw = kr[:, base : base + 256].astype(BF)
            vw = vr[:, base : base + 256].astype(BF)
            st = nt(kw, qs) + bias[r]
            top = jnp.max(st, 0, keepdims=True)
            e = jnp.exp(st - top)
            p = (e * (1.0 / jnp.sum(e, 0, keepdims=True))).astype(BF)
            p_o[r, i] = p
            outs.append(unstack_heads(tn(p, vw), i, length))
        att_s[r] = join_windows(outs)
        return carry

    lax.fori_loop(0, rb, row, 0)
    att32 = att_s[...]
    att_o[...] = att32.astype(BF)
    att = att32.reshape(n, width).astype(BF)
    u1 = x32 + nn(att, wo[...]) + ob[...]
    u1_o[...] = u1.reshape(rb, length, width)
    xhat, _ = norm_parts(u1)
    first = (xhat * g1[...] + b1[...]).astype(BF)
    f_o[...] = first.astype(F32).reshape(rb, length, width).astype(BF)
    pr_o[...] = (nn(first, wc[...]) + pb[...]).reshape(rb, length, width).astype(BF)


def cross_forward(starts, order, pat, wp, wk, wv, pab, cb, probe, pr_o, k_o, v_o, p_o, mix_o, pat_s):
    i = pl.program_id(0)
    points = pat.shape[1]
    length = probe.shape[1]

    @pl.when(i == 0)
    def _():
        pat_s[...] = jnp.zeros_like(pat_s)

    lo, hi = starts[i], starts[i + 1]

    @pl.when(hi > lo)
    def _():
        pat_s[0:points, :] = pat[0]
        pr = (nn(pat_s[...], wp[...]) + pab[...]).astype(BF)
        pr_o[0] = pr
        k_o[0] = nn(pr, wk[...]).astype(BF)
        v_o[0] = (nn(pr, wv[...]) + cb[...]).astype(BF)

        def row(j, carry):
            r = order[j]
            qr = probe[r].astype(F32) * 0.125
            outs = []
            for g in range(4):
                base = WINDOWS[g][0]
                qs = stack_heads(qr, g)
                st = nt(k_o[0, :, base : base + 256], qs)
                point = lax.broadcasted_iota(jnp.int32, st.shape, 0)
                st = jnp.where(point < points, st, -1e30)
                top = jnp.max(st, 0, keepdims=True)
                e = jnp.exp(st - top)
                p = (e * (1.0 / jnp.sum(e, 0, keepdims=True))).astype(BF)
                p_o[r, g] = p
                outs.append(unstack_heads(tn(p, v_o[0, :, base : base + 256]), g, length))
            mix_o[r] = join_windows(outs).astype(BF)
            return carry

        lax.fori_loop(lo, hi, row, 0)


def tail_kernel(
    u1, mix, og, wco, w1, w2, g1, b1, cb, g2, s2, wb, nb, g3, s3,
    out_o, act_o, gi_o, sec_o, gb3_o, gm_o, gb2_o, gc_o, vec_o, wbg_o,
    act_s, gp_s, acc_s,
):
    step = pl.program_id(0)
    rb, length, width = u1.shape
    n = rb * length
    chunks = w1.shape[0]

    @pl.when(step == 0)
    def _():
        vec_o[...] = jnp.zeros_like(vec_o)
        wbg_o[...] = jnp.zeros_like(wbg_o)

    def flat(ref):
        return ref[...].astype(F32).reshape(n, width)

    def fold(value):
        return value.reshape(rb, length, width)

    xhat1, _ = norm_parts(flat(u1))
    first = xhat1 * g1[...] + b1[...]
    u2 = first + nn(flat(mix).astype(BF), wco[...]) + cb[...]
    xhat2, inv2 = norm_parts(u2)
    second = (xhat2 * g2[...] + s2[...]).astype(BF)
    sec32 = second.astype(F32)
    sec_o[...] = fold(sec32).astype(BF)
    acc_s[...] = sec32 + nb[...]

    def up(c, carry):
        inner = nn(second, w1[c]) + wb[c]
        act, slope = gelu_parts(inner)
        act = act.astype(BF)
        gp_s[c] = slope
        act_o[c] = act
        acc_s[...] += nn(act, w2[c])
        return carry

    lax.fori_loop(0, chunks, up, 0)
    xhat3, inv3 = norm_parts(acc_s[...])
    out_o[...] = fold(xhat3 * g3[...] + s3[...]).astype(BF)
    y = flat(og)
    grad_summed = norm_back(y, g3[...], xhat3, inv3)
    gb3 = grad_summed.astype(BF)
    gb3f = gb3.astype(F32)
    gb3_o[...] = fold(gb3f).astype(BF)
    vec_o[0:1] += jnp.sum(y * xhat3, 0, keepdims=True)
    vec_o[1:2] += jnp.sum(y, 0, keepdims=True)
    vec_o[2:3] += jnp.sum(gb3f, 0, keepdims=True)
    acc_s[...] = grad_summed

    def down(c, carry):
        gi = (nt(gb3, w2[c]) * gp_s[c]).astype(BF)
        gi_o[c] = gi
        wbg_o[c] += jnp.sum(gi.astype(F32), 0, keepdims=True)
        acc_s[...] += nt(gi, w1[c])
        return carry

    lax.fori_loop(0, chunks, down, 0)
    y2 = acc_s[...].astype(BF).astype(F32)
    gm = norm_back(y2, g2[...], xhat2, inv2)
    gm_o[...] = fold(gm)
    gb2 = gm.astype(BF)
    gb2f = gb2.astype(F32)
    gb2_o[...] = fold(gb2f).astype(BF)
    vec_o[3:4] += jnp.sum(y2 * xhat2, 0, keepdims=True)
    vec_o[4:5] += jnp.sum(y2, 0, keepdims=True)
    vec_o[5:6] += jnp.sum(gb2f, 0, keepdims=True)
    gc_o[...] = fold(nt(gb2, wco[...])).astype(BF)


def cross_backward(
    starts, order, pat, proj, keys, values, wk, wv, probe, grad, probs,
    dpr_o, dproj_o, dwk_o, dwv_o, dwp_o, dcb_o,
    pat_s, dk_s, dv_s, dwk_s, dwv_s, dwp_s,
):
    i = pl.program_id(0)
    points = pat.shape[1]
    length = probe.shape[1]

    @pl.when(i == 0)
    def _():
        pat_s[...] = jnp.zeros_like(pat_s)
        dwk_s[...] = jnp.zeros_like(dwk_s)
        dwv_s[...] = jnp.zeros_like(dwv_s)
        dwp_s[...] = jnp.zeros_like(dwp_s)
        dcb_o[...] = jnp.zeros_like(dcb_o)

    lo, hi = starts[i], starts[i + 1]

    @pl.when(hi == lo)
    def _():
        dproj_o[...] = jnp.zeros_like(dproj_o)

    @pl.when(hi > lo)
    def _():
        dk_s[...] = jnp.zeros_like(dk_s)
        dv_s[...] = jnp.zeros_like(dv_s)

        def row(j, carry):
            r = order[j]
            qr = probe[r].astype(F32) * 0.125
            gr = grad[r].astype(F32)
            outs = []
            for g in range(4):
                base = WINDOWS[g][0]
                qs = stack_heads(qr, g)
                gs = stack_heads(gr, g)
                pb = probs[r, g]
                p = pb.astype(F32)
                dp = nt(values[0, :, base : base + 256], gs)
                w = jnp.sum(dp * p, 0, keepdims=True)
                ds = (p * (dp - w)).astype(BF)
                dk_s[:, base : base + 256] += nn(ds, qs)
                dv_s[:, base : base + 256] += nn(pb, gs)
                outs.append(unstack_heads(tn(ds, keys[0, :, base : base + 256]), g, length))
            dpr_o[r] = (join_windows(outs) * 0.125).astype(BF)
            return carry

        lax.fori_loop(lo, hi, row, 0)
        pat_s[0:points, :] = pat[0]
        pr = proj[0]
        dk = dk_s[...].astype(BF)
        dv = dv_s[...].astype(BF)
        dcb_o[0:1] += jnp.sum(dv.astype(F32), 0, keepdims=True)
        dproj = (nt(dk, wk[...]) + nt(dv, wv[...])).astype(BF)
        dproj_o[0] = dproj[0:points]
        dwk_s[...] += tn(pr, dk)
        dwv_s[...] += tn(pr, dv)
        dwp_s[...] += tn(pat_s[...], dproj)
        dcb_o[1:2] += jnp.sum(dproj.astype(F32), 0, keepdims=True)

    @pl.when(i == pl.num_programs(0) - 1)
    def _():
        dwk_o[...] = dwk_s[...].astype(BF)
        dwv_o[...] = dwv_s[...].astype(BF)
        dwp_o[...] = dwp_s[...].astype(BF)


def self_backward(
    gm, dpr, u1, q, k, v, probs, wq, wk, wv, wo, wc, g1,
    gb1_o, dq_o, dk_o, dv_o, tg_o, vec_o,
    ga_s, dq_s, dk_s, dv_s,
):
    step = pl.program_id(0)
    rb, length, width = u1.shape
    n = rb * length

    @pl.when(step == 0)
    def _():
        vec_o[...] = jnp.zeros_like(vec_o)

    def flat(ref):
        return ref[...].astype(F32).reshape(n, width)

    def fold(value):
        return value.reshape(rb, length, width)

    dpr32 = flat(dpr)
    grad_first = flat(gm) + nt(dpr32.astype(BF), wc[...])
    xhat, inv = norm_parts(flat(u1))
    low = norm_back(grad_first, g1[...], xhat, inv)
    gb1 = low.astype(BF)
    gb1f = gb1.astype(F32)
    gb1_o[...] = fold(gb1f).astype(BF)
    vec_o[0:1] += jnp.sum(grad_first * xhat, 0, keepdims=True)
    vec_o[1:2] += jnp.sum(grad_first, 0, keepdims=True)
    vec_o[2:3] += jnp.sum(gb1f, 0, keepdims=True)
    vec_o[3:4] += jnp.sum(dpr32, 0, keepdims=True)
    ga_s[...] = fold(nt(gb1, wo[...]).astype(BF).astype(F32))

    def row(r, carry):
        qr = q[r].astype(F32) * 0.125
        kr = k[r].astype(F32)
        vr = v[r].astype(F32)
        gr = ga_s[r]
        dqs, dks, dvs = [], [], []
        for i in range(4):
            base = WINDOWS[i][0]
            qs = stack_heads(qr, i)
            gs = stack_heads(gr, i)
            kw = kr[:, base : base + 256].astype(BF)
            vw = vr[:, base : base + 256].astype(BF)
            pb = probs[r, i]
            p = pb.astype(F32)
            dp = nt(vw, gs)
            w = jnp.sum(dp * p, 0, keepdims=True)
            ds = (p * (dp - w)).astype(BF)
            dks.append(nn(ds, qs))
            dvs.append(nn(pb, gs))
            dqs.append(unstack_heads(tn(ds, kw), i, length))
        dq_s[r] = join_windows(dqs) * 0.125
        dk_s[r] = join_windows(dks)
        dv_s[r] = join_windows(dvs)
        return carry

    lax.fori_loop(0, rb, row, 0)
    dq = dq_s[...].reshape(n, width).astype(BF)
    dk = dk_s[...].reshape(n, width).astype(BF)
    dv = dv_s[...].reshape(n, width).astype(BF)
    dq_o[...] = dq_s[...].astype(BF)
    dk_o[...] = dk_s[...].astype(BF)
    dv_o[...] = dv_s[...].astype(BF)
    vec_o[4:5] += jnp.sum(dq.astype(F32), 0, keepdims=True)
    vec_o[5:6] += jnp.sum(dv.astype(F32), 0, keepdims=True)
    total = low + nt(dq, wq[...]) + nt(dk, wk[...]) + nt(dv, wv[...])
    tg_o[...] = fold(total).astype(BF)


def sds(shape, dtype):
    return jax.ShapeDtypeStruct(shape, dtype)


def whole(shape, *, single=True):
    zeros = (0,) * len(shape)
    mode = pl.Buffered(1) if single else None
    return pl.BlockSpec(shape, lambda i, *_: zeros, pipeline_mode=mode)


def rows_block(shape, rb):
    rest = tuple(shape[1:])
    return pl.BlockSpec((rb,) + rest, lambda i, *_: (i,) + (0,) * len(rest))


def params(mib):
    return pltpu.CompilerParams(
        dimension_semantics=("arbitrary",), vmem_limit_bytes=mib * 1024 * 1024
    )


def cost(flops, bytes_accessed):
    return pl.CostEstimate(flops=int(flops), bytes_accessed=int(bytes_accessed), transcendentals=0)


def my_place():
    dp, fs = lax.axis_index("dp"), lax.axis_index("fsdp")
    return dp // 2, dp % 2, fs // 2, fs % 2


def device_at(z, y, x, c):
    return (z * 2 + y, x * 2 + c)


def meet(z, y, x, c):
    sem = pltpu.get_barrier_semaphore()
    others = [device_at((z + k) % 4, y, x, c) for k in (1, 2, 3)]
    others += [device_at(z, 1 - y, x, c), device_at(z, y, 1 - x, c), device_at(z, y, x, 1 - c)]
    for other in others:
        pl.semaphore_signal(sem, inc=1, device_id=other, device_id_type=pl.DeviceIdType.MESH)
    pl.semaphore_wait(sem, len(others))


class Copies:
    def __init__(self, send, recv, local):
        self.send, self.recv, self.local = send, recv, local
        self.far = self.near = 0

    def remote(self, src, dst, device):
        i = self.far
        self.far += 1
        copy = pltpu.make_async_remote_copy(
            src_ref=src, dst_ref=dst, send_sem=self.send.at[i], recv_sem=self.recv.at[i],
            device_id=device, device_id_type=pl.DeviceIdType.MESH,
        )
        copy.start()
        return copy

    def here(self, src, dst):
        i = self.near
        self.near += 1
        copy = pltpu.make_async_copy(src, dst, self.local.at[i])
        copy.start()
        return copy


def arrived(copies):
    for copy in copies:
        copy.wait()


def drive(jobs, order):
    for name in order:
        next(jobs[name], None)
    for job in jobs.values():
        for _ in job:
            pass


def gather_kernel(parts, w_in, p_in, w_out, p_out, send, recv, local):
    z, y, x, c = my_place()
    meet(z, y, x, c)
    copies = Copies(send, recv, local)

    def slabs(lo, n):
        pick = pl.ds(lo, n)
        mine = w_out.at[pick, z, y, x, c]
        pending = [copies.here(w_in.at[pick], mine)]
        pending += [
            copies.remote(w_in.at[pick], mine, device_at((z + k) % 4, y, x, c)) for k in (1, 3, 2)
        ]
        yield
        arrived(pending)
        line = w_out.at[pick, :, y, x, c]
        step = copies.remote(line, line, device_at(z, 1 - y, x, c))
        yield
        step.wait()
        plane = w_out.at[pick, :, :, x, c]
        step = copies.remote(plane, plane, device_at(z, y, 1 - x, c))
        yield
        step.wait()
        half = w_out.at[pick, :, :, :, c]
        step = copies.remote(half, half, device_at(z, y, x, 1 - c))
        yield
        step.wait()

    def image(i):
        mine = p_out.at[z, y, i]
        pending = [copies.here(p_in.at[i], mine)]
        pending += [
            copies.remote(p_in.at[i], mine, device_at((z + k) % 4, y, x, c)) for k in (1, 3, 2)
        ]
        yield
        arrived(pending)
        line = p_out.at[:, y, i]
        step = copies.remote(line, line, device_at(z, 1 - y, x, c))
        yield
        step.wait()

    jobs = {}
    for j, (lo, n) in enumerate(parts):
        jobs["w%d" % j] = slabs(lo, n)
    for i in range(p_in.shape[0]):
        jobs["p%d" % i] = image(i)
    drive(jobs, ["w0", "p0", "w1", "p1", "p2", "p3", "w0", "p0", "w0", "w1", "w0", "p1", "w1", "p2", "w1", "p3"])


def reduce_kernel(
    parts, w_in, p_in, w_out, p_out, acc, rc, rx, ry, rz, pacc, pry, prz, send, recv, local
):
    z, y, x, c = my_place()
    meet(z, y, x, c)
    copies = Copies(send, recv, local)

    def up(ref, *at):
        return ref[at].astype(F32)

    def slabs(lo, n):
        pick = pl.ds(lo, n)
        own = copies.here(w_in.at[pick, :, :, :, c], acc.at[pick])
        step = copies.remote(w_in.at[pick, :, :, :, 1 - c], rc.at[pick], device_at(z, y, x, 1 - c))
        yield
        own.wait()
        step.wait()

        def add_x(i, carry):
            s, zz = lo + i // 4, i % 4
            for yy in range(2):
                acc[s, zz, yy, 1 - x] = (up(acc, s, zz, yy, 1 - x) + up(rc, s, zz, yy, 1 - x)).astype(BF)
            return carry

        lax.fori_loop(0, 4 * n, add_x, 0)
        step = copies.remote(acc.at[pick, :, :, 1 - x], rx.at[pick], device_at(z, y, 1 - x, c))
        yield
        step.wait()

        def add_y(i, carry):
            s, zz = lo + i // 4, i % 4
            acc[s, zz, 1 - y, x] = (
                up(acc, s, zz, 1 - y, x) + up(rc, s, zz, 1 - y, x) + up(rx, s, zz, 1 - y)
            ).astype(BF)
            return carry

        lax.fori_loop(0, 4 * n, add_y, 0)
        step = copies.remote(acc.at[pick, :, 1 - y, x], ry.at[pick], device_at(z, 1 - y, x, c))
        yield
        step.wait()
        steps = []
        for k in (1, 3, 2):
            zz = (z + k) % 4

            def add_z(i, carry):
                s = lo + i
                acc[s, zz, y, x] = (
                    up(acc, s, zz, y, x) + up(rc, s, zz, y, x) + up(rx, s, zz, y) + up(ry, s, zz)
                ).astype(BF)
                return carry

            lax.fori_loop(0, n, add_z, 0)
            steps.append(
                copies.remote(acc.at[pick, zz, y, x], rz.at[k - 1, pick], device_at(zz, y, x, c))
            )
        yield
        arrived(steps)

        def add_last(i, carry):
            s = lo + i
            w_out[s] = (
                up(acc, s, z, y, x) + up(rc, s, z, y, x) + up(rx, s, z, y) + up(ry, s, z)
                + up(rz, 0, s) + up(rz, 1, s) + up(rz, 2, s)
            )
            return carry

        lax.fori_loop(0, n, add_last, 0)

    def image(i):
        own = copies.here(p_in.at[:, y, i], pacc.at[i])
        step = copies.remote(p_in.at[:, 1 - y, i], pry.at[i], device_at(z, 1 - y, x, c))
        yield
        own.wait()
        step.wait()
        steps = []
        for k in (1, 3, 2):
            zz = (z + k) % 4
            pacc[i, zz] = (up(pacc, i, zz) + up(pry, i, zz)).astype(BF)
            steps.append(copies.remote(pacc.at[i, zz], prz.at[k - 1, i], device_at(zz, y, x, c)))
        yield
        arrived(steps)
        p_out[i] = (
            up(pacc, i, z) + up(pry, i, z) + up(prz, 0, i) + up(prz, 1, i) + up(prz, 2, i)
        ).astype(BF)

    jobs = {}
    for i in range(p_in.shape[2]):
        jobs["p%d" % i] = image(i)
    for j, (lo, n) in enumerate(parts):
        jobs["w%d" % j] = slabs(lo, n)
    drive(
        jobs,
        ["w0", "p0", "p1", "w1", "p2", "p3", "w0", "w1", "p0", "w0", "p1", "w1", "p2", "w0", "p3", "w1"],
    )


def split_slabs(count):
    first = (count + 1) // 2
    return ((0, first), (first, count - first))


def gather_all(slabs, patches):
    n, sr, width = slabs.shape
    images, points, pwidth = patches.shape
    parts = split_slabs(n)
    copies = 6 * len(parts) + 4 * images
    w_all, p_all = pl.pallas_call(
        functools.partial(gather_kernel, parts),
        in_specs=[pl.BlockSpec(memory_space=pl.ANY)] * 2,
        out_specs=[pl.BlockSpec(memory_space=pl.ANY)] * 2,
        out_shape=[sds((n, 4, 2, 2, 2, sr, width), BF), sds((4, 2, images, points, pwidth), BF)],
        scratch_shapes=[
            pltpu.SemaphoreType.DMA((copies,)),
            pltpu.SemaphoreType.DMA((copies,)),
            pltpu.SemaphoreType.DMA((len(parts) + images,)),
        ],
        compiler_params=pltpu.CompilerParams(
            collective_id=0, has_side_effects=True, vmem_limit_bytes=8 * 1024 * 1024
        ),
        name="gather_all",
    )(slabs, patches)
    return w_all.reshape(n, 32 * sr, width), p_all.reshape(8 * images, points, pwidth)


def reduce_all(slabs, grads):
    n, full, width = slabs.shape
    sr = full // 32
    total, points, _ = grads.shape
    images = total // 8
    parts = split_slabs(n)
    copies = 6 * len(parts) + 4 * images
    w_shard, p_shard = pl.pallas_call(
        functools.partial(reduce_kernel, parts),
        in_specs=[pl.BlockSpec(memory_space=pl.ANY)] * 2,
        out_specs=[pl.BlockSpec(memory_space=pltpu.VMEM)] * 2,
        out_shape=[sds((n, sr, width), F32), sds((images, points, width), BF)],
        scratch_shapes=[
            pltpu.VMEM((n, 4, 2, 2, sr, width), BF),
            pltpu.VMEM((n, 4, 2, 2, sr, width), BF),
            pltpu.VMEM((n, 4, 2, sr, width), BF),
            pltpu.VMEM((n, 4, sr, width), BF),
            pltpu.VMEM((3, n, sr, width), BF),
            pltpu.VMEM((images, 4, points, width), BF),
            pltpu.VMEM((images, 4, points, width), BF),
            pltpu.VMEM((3, images, points, width), BF),
            pltpu.SemaphoreType.DMA((copies,)),
            pltpu.SemaphoreType.DMA((copies,)),
            pltpu.SemaphoreType.DMA((len(parts) + images,)),
        ],
        compiler_params=pltpu.CompilerParams(
            collective_id=1, has_side_effects=True, vmem_limit_bytes=56 * 1024 * 1024
        ),
        name="reduce_all",
    )(slabs.reshape(n, 4, 2, 2, 2, sr, width), grads.reshape(4, 2, images, points, width))
    return w_shard, p_shard


def gather(value, axis):
    return lax.all_gather(value, AXES, axis=axis, tiled=True)


def on_device(
    tokens, patches, segments, owner, image_slot, out_grad,
    self_query, query_bias, self_key, self_value, value_bias, self_output, output_bias,
    first_gain, first_norm_bias, patch_proj, patch_bias, cross_query, probe_bias, cross_key,
    cross_value, content_bias, cross_output, cross_bias, second_gain, second_shift,
    widen_weight, widen_bias, narrow_weight, narrow_bias, third_gain, third_shift,
):
    rows, length, width = tokens.shape
    images, points, pwidth = patches.shape
    groups = lax.axis_size("dp")
    shards = groups * lax.axis_size("fsdp")
    total_images = groups * images
    hidden = widen_weight.shape[1]
    chunks = hidden // width
    sr = self_query.shape[0]
    wr = widen_bias.shape[0]

    place = lax.axis_index("dp") * lax.axis_size("fsdp") + lax.axis_index("fsdp")
    vec_list = (
        query_bias, value_bias, output_bias, first_gain, first_norm_bias, patch_bias, probe_bias,
        content_bias, cross_bias, second_gain, second_shift, narrow_bias, third_gain, third_shift,
    )
    nv = len(vec_list)
    pr = patch_proj.shape[0]
    tails = pr - sr
    lane_block = jnp.arange(width, dtype=jnp.int32)[None, :] // sr
    vec_rows = jnp.where(lane_block == place, jnp.tile(jnp.stack(vec_list), (1, shards)), jnp.zeros((), BF))
    wb_row = jnp.pad(widen_bias, (0, width - wr))[None]
    extra = jnp.concatenate([patch_proj[sr:], vec_rows, wb_row], 0)
    er = max(sr, extra.shape[0])
    own_rows = er == sr and groups == 8 and shards == 32
    extra = jnp.pad(extra, ((0, er - extra.shape[0]), (0, 0)))
    mats = [self_query, self_key, self_value, self_output, cross_query, cross_key, cross_value, cross_output, patch_proj[:sr]]
    if own_rows:
        w_a, patches_all = gather_all(jnp.stack(mats + [extra]), patches)
        extra_all = w_a[len(mats)].reshape(shards, er, width)
    else:
        w_a = gather(jnp.stack(mats), 1)
        extra_all = gather(extra, 0).reshape(shards, er, width)
        patches_all = lax.all_gather(patches, "dp", axis=0, tiled=True)
    vec_all = jnp.sum(extra_all[:, tails : tails + nv].astype(F32), 0)
    (qb, vb, ob, g1, b1, pab, prb, cob, crb, g2, s2, nab, g3, s3) = [vec_all[j : j + 1] for j in range(nv)]
    wb = extra_all[:, tails + nv, :wr].astype(F32)
    wb = wb.reshape(shards, chunks, sr).transpose(1, 0, 2).reshape(chunks, 1, width)
    patch_full = jnp.concatenate(
        [w_a[len(mats) - 1].reshape(shards, sr, width), extra_all[:, :tails]], 1
    ).reshape(shards * pr, width)

    widen_slabs = widen_weight.reshape(sr, shards, chunks, sr).transpose(2, 0, 1, 3).reshape(chunks, sr, width)
    narrow_slabs = narrow_weight.reshape(chunks, sr, width)
    w_b_in = jnp.concatenate([widen_slabs, narrow_slabs], 0)
    if own_rows:
        w_b_in, w_a = lax.optimization_barrier((w_b_in, w_a))
    w_b = gather(w_b_in, 1)

    image = owner * images + image_slot
    idx = jnp.arange(rows, dtype=jnp.int32)
    before = (image[None, :] < image[:, None]) | ((image[None, :] == image[:, None]) & (idx[None, :] < idx[:, None]))
    rank = jnp.sum(before.astype(jnp.int32), 1)
    order = jnp.sum(jnp.where(rank[:, None] == idx[None, :], idx[:, None], 0), 0).astype(jnp.int32)
    starts = jnp.sum((image[None, :] < jnp.arange(total_images + 1, dtype=jnp.int32)[:, None]).astype(jnp.int32), 1)

    same = segments[:, :, None] == segments[:, None, :]
    bias = jnp.where(same, 0.0, mask_fill).astype(F32)
    bias = jnp.concatenate([bias, bias, bias], 2)

    rb = 8 if rows % 8 == 0 else 1
    grid = (rows // rb,)
    tok_sh = (rows, length, width)
    slab = (width, width)

    def wspec(j):
        return pl.BlockSpec((None, width, width), lambda i, *_: (j, 0, 0), pipeline_mode=pl.Buffered(1))

    vspec = whole((1, width))
    tb = rows_block(tok_sh, rb)
    self_p = (rows, 4, length, 3 * length)
    q, k, v, probs, attended, u1, first_low, probe = pl.pallas_call(
        self_forward,
        grid=grid,
        in_specs=[tb, rows_block((rows, length, 3 * length), rb)]
        + [wspec(0), wspec(1), wspec(2), wspec(3), wspec(4)]
        + [vspec] * 6,
        out_specs=[tb, tb, tb, rows_block(self_p, rb), tb, tb, tb, tb],
        out_shape=[
            sds(tok_sh, BF), sds(tok_sh, BF), sds(tok_sh, BF), sds(self_p, BF),
            sds(tok_sh, BF), sds(tok_sh, F32), sds(tok_sh, BF), sds(tok_sh, BF),
        ],
        scratch_shapes=[pltpu.VMEM((rb, length, width), F32)],
        compiler_params=params(48),
        cost_estimate=cost(11 * rows * length * width * width, 30e6),
        name="self_forward",
    )(tokens, bias, w_a, w_a, w_a, w_a, w_a, qb, vb, ob, g1, b1, prb)

    padded = -(-points // 16) * 16
    kv_sh = (total_images, padded, width)
    cross_p = (rows, 4, padded, 3 * length)
    img_spec = pl.BlockSpec((1, points, pwidth), lambda i, *_: (i, 0, 0))
    grad_spec = pl.BlockSpec((1, points, width), lambda i, *_: (i, 0, 0))
    kv_spec = pl.BlockSpec((1, padded, width), lambda i, *_: (i, 0, 0))
    projected, image_keys, image_values, cprobs, mixed = pl.pallas_call(
        cross_forward,
        grid_spec=pltpu.PrefetchScalarGridSpec(
            num_scalar_prefetch=2,
            grid=(total_images,),
            in_specs=[img_spec, whole(patch_full.shape), wspec(5), wspec(6), vspec, vspec, whole(tok_sh)],
            out_specs=[kv_spec, kv_spec, kv_spec, whole(cross_p), whole(tok_sh)],
            scratch_shapes=[pltpu.VMEM((padded, pwidth), BF)],
        ),
        out_shape=[sds(kv_sh, BF), sds(kv_sh, BF), sds(kv_sh, BF), sds(cross_p, BF), sds(tok_sh, BF)],
        compiler_params=params(48),
        cost_estimate=cost(4 * total_images * points * width * width, 40e6),
        name="cross_forward",
    )(starts, order, patches_all, patch_full, w_a, w_a, pab, cob, probe)

    def chunk_w(j):
        return pl.BlockSpec((chunks, width, width), lambda i, *_: (j, 0, 0), pipeline_mode=pl.Buffered(1))

    n_tok = rows * length
    hid_sh = (chunks, n_tok, width)
    hid_spec = pl.BlockSpec((chunks, rb * length, width), lambda i, *_: (0, i, 0))
    (output, active, grad_inner, second, gb3, grad_mid, gb2, grad_crossed, vec_t, wb_grad) = pl.pallas_call(
        tail_kernel,
        grid=grid,
        in_specs=[tb, tb, tb, wspec(7), chunk_w(0), chunk_w(1)]
        + [vspec] * 5
        + [whole((chunks, 1, width))]
        + [vspec] * 3,
        out_specs=[tb, hid_spec, hid_spec, tb, tb, tb, tb, tb, whole((8, width)), whole((chunks, 1, width))],
        out_shape=[
            sds(tok_sh, BF), sds(hid_sh, BF), sds(hid_sh, BF), sds(tok_sh, BF), sds(tok_sh, BF),
            sds(tok_sh, F32), sds(tok_sh, BF), sds(tok_sh, BF), sds((8, width), F32), sds((chunks, 1, width), F32),
        ],
        scratch_shapes=[
            pltpu.VMEM((8, 128), BF),
            pltpu.VMEM((chunks, rb * length, width), F32),
            pltpu.VMEM((rb * length, width), F32),
        ],
        compiler_params=params(56),
        cost_estimate=cost(18 * n_tok * width * width + 8 * n_tok * width * hidden, 50e6),
        name="tail",
    )(u1, mixed, out_grad, w_a, w_b, w_b, g1, b1, crb, g2, s2, wb, nab, g3, s3)

    dprobe, dproj, dwk, dwv, dwp, dcb = pl.pallas_call(
        cross_backward,
        grid_spec=pltpu.PrefetchScalarGridSpec(
            num_scalar_prefetch=2,
            grid=(total_images,),
            in_specs=[img_spec, kv_spec, kv_spec, kv_spec, wspec(5), wspec(6), whole(tok_sh), whole(tok_sh), whole(cross_p)],
            out_specs=[whole(tok_sh), grad_spec, whole(slab), whole(slab), whole((pwidth, width)), whole((8, width))],
            scratch_shapes=[
                pltpu.VMEM((padded, pwidth), BF),
                pltpu.VMEM((padded, width), F32),
                pltpu.VMEM((padded, width), F32),
                pltpu.VMEM((width, width), F32),
                pltpu.VMEM((width, width), F32),
                pltpu.VMEM((pwidth, width), F32),
            ],
        ),
        out_shape=[sds(tok_sh, BF), sds((total_images, points, width), BF), sds(slab, BF), sds(slab, BF), sds((pwidth, width), BF), sds((8, width), F32)],
        compiler_params=params(56),
        cost_estimate=cost(8 * total_images * points * width * width, 50e6),
        name="cross_backward",
    )(starts, order, patches_all, projected, image_keys, image_values, w_a, w_a, probe, grad_crossed, cprobs)

    gb1, dq, dk, dv, tokens_grad, vec_s = pl.pallas_call(
        self_backward,
        grid=grid,
        in_specs=[tb, tb, tb, tb, tb, tb, rows_block(self_p, rb)]
        + [wspec(0), wspec(1), wspec(2), wspec(3), wspec(4)]
        + [vspec],
        out_specs=[tb, tb, tb, tb, tb, whole((8, width))],
        out_shape=[sds(tok_sh, BF)] * 5 + [sds((8, width), F32)],
        scratch_shapes=[pltpu.VMEM((rb, length, width), F32)] * 4,
        compiler_params=params(52),
        cost_estimate=cost(14 * n_tok * width * width, 40e6),
        name="self_backward",
    )(grad_mid, dprobe, u1, q, k, v, probs, w_a, w_a, w_a, w_a, w_a, g1)

    def wgrad(left, right):
        return tn(left.reshape(n_tok, width), right.reshape(n_tok, width)).astype(BF)

    grad_narrow = lax.dot_general(
        active, gb3.reshape(n_tok, width), (((1,), (0,)), ((), ())), preferred_element_type=F32
    ).astype(BF)
    grad_widen = jnp.stack([wgrad(second, grad_inner[c]) for c in range(chunks)])
    ffn_shard = lax.psum_scatter(
        jnp.concatenate([grad_widen, grad_narrow], 0), AXES, scatter_dimension=1, tiled=True
    ).astype(F32)

    vec_grads = jnp.concatenate(
        [
            vec_s[4:5], vec_s[5:6], vec_s[2:3], vec_s[0:1], vec_s[1:2], dcb[1:2], vec_s[3:4], dcb[0:1],
            vec_t[5:6], vec_t[3:4], vec_t[4:5], vec_t[2:3], vec_t[0:1], vec_t[1:2],
        ]
    ).astype(BF)
    wb_flat = wb_grad.reshape(chunks, shards, sr).transpose(1, 0, 2).reshape(shards, 1, wr).astype(BF)
    dwp = dwp.reshape(shards, pr, width)
    extra_grad = jnp.concatenate(
        [
            dwp[:, sr:],
            jnp.broadcast_to(vec_grads[None], (shards, nv, width)),
            jnp.pad(wb_flat, ((0, 0), (0, 0), (0, width - wr))),
            jnp.zeros((shards, er - tails - nv - 1, width), BF),
        ],
        1,
    )
    slabs = [
        wgrad(tokens, dq), wgrad(tokens, dk), wgrad(tokens, dv), wgrad(attended, gb1),
        wgrad(first_low, dprobe), dwk, dwv, wgrad(mixed, gb2), dwp[:, :sr].reshape(slab),
    ]
    if own_rows:
        slab_shard, grad_projected = reduce_all(jnp.stack(slabs + [extra_grad.reshape(slab)]), dproj)
        extra_shard = slab_shard[len(slabs)]
    else:
        grad_projected = lax.psum_scatter(dproj, "dp", scatter_dimension=0, tiled=True)
        slab_shard = lax.psum_scatter(jnp.stack(slabs), AXES, scatter_dimension=1, tiled=True).astype(F32)
        extra_shard = lax.psum_scatter(extra_grad, AXES, scatter_dimension=0, tiled=True)[0].astype(F32)
    patch_shard = jnp.concatenate([slab_shard[len(slabs) - 1], extra_shard[:tails]], 0)
    patches_grad = lax.dot_general(
        grad_projected, patch_full, (((2,), (1,)), ((), ())), preferred_element_type=F32
    ).astype(BF)
    vg = lax.dynamic_slice(extra_shard, (tails, place * sr), (nv, sr))
    vg = [vg[j] for j in range(nv)]
    wbg = extra_shard[tails + nv, :wr]
    widen_shard = ffn_shard[:chunks].reshape(chunks, sr, shards, sr).transpose(1, 2, 0, 3).reshape(sr, hidden)
    narrow_shard = ffn_shard[chunks:].reshape(chunks * sr, width)
    return (
        output, tokens_grad, patches_grad,
        slab_shard[0], vg[0], slab_shard[1], slab_shard[2], vg[1], slab_shard[3], vg[2], vg[3], vg[4],
        patch_shard, vg[5], slab_shard[4], vg[6], slab_shard[5], slab_shard[6], vg[7], slab_shard[7],
        vg[8], vg[9], vg[10], widen_shard, wbg, narrow_shard, vg[11], vg[12], vg[13],
    )


def solution(mesh):
    three, two, one = P(AXES, None, None), P(AXES, None), P(AXES)
    in_specs = (
        three, three, two, one, one, three,
        two, one, two, two, one, two, one, one, one, two, one, two, one, two,
        two, one, two, one, one, one, two, one, two, one, one, one,
    )
    out_specs = (
        three, three, three,
        two, one, two, two, one, two, one, one, one, two, one, two, one, two, two, one, two,
        one, one, one, two, one, two, one, one, one,
    )
    return jax.shard_map(on_device, mesh=mesh, in_specs=in_specs, out_specs=out_specs, check_vma=False)
```

```python
import functools

import jax
import jax.numpy as jnp
from jax import lax
from jax.experimental import pallas as pl
from jax.experimental.pallas import tpu as pltpu
from jax.sharding import PartitionSpec as P

HEADS = 12
AXES = ("dp", "fsdp")
BF = jnp.bfloat16
F32 = jnp.float32
norm_eps = 1e-06
mask_fill = -1000000000.0

WINDOWS = ((0, 0), (128, 64), (384, 0), (512, 64))

ERFC_POLE = 0.3
ERFC_POLY = (
    0.16918935391840687,
    0.17069093065701252,
    0.14852123834149009,
    0.214181489197379,
    -0.09282620690981414,
    0.5449671942862269,
    -0.5097726086693966,
    0.4843018450108595,
    -0.12925324449453648,
)
INV_SQRT2 = 0.7071067811865476
INV_SQRT2PI = 0.3989422804014327


def nn(left, right):
    return lax.dot_general(left, right, (((1,), (0,)), ((), ())), preferred_element_type=F32)


def nt(left, right):
    return lax.dot_general(left, right, (((1,), (1,)), ((), ())), preferred_element_type=F32)


def tn(left, right):
    return lax.dot_general(left, right, (((0,), (0,)), ((), ())), preferred_element_type=F32)


def norm_parts(value):
    mean = jnp.mean(value, -1, keepdims=True)
    centred = value - mean
    spread = jnp.mean(centred * centred, -1, keepdims=True)
    inv = lax.rsqrt(spread + norm_eps)
    return centred * inv, inv


def norm_back(grad, gain, xhat, inv):
    scaled = grad * gain
    first = jnp.mean(scaled, -1, keepdims=True)
    second = jnp.mean(scaled * xhat, -1, keepdims=True)
    return inv * (scaled - first - xhat * second)


def gelu_parts(v):
    z = jnp.abs(v) * INV_SQRT2
    t = 1.0 / (1.0 + ERFC_POLE * z)
    poly = jnp.full_like(t, ERFC_POLY[-1])
    for c in ERFC_POLY[-2::-1]:
        poly = poly * t + c
    bell = jnp.exp(-0.5 * (v * v))
    half = (0.5 * bell) * (t * poly)
    cdf = jnp.where(v >= 0, 1.0 - half, half)
    return v * cdf, cdf + (v * INV_SQRT2PI) * bell


def window(full, index):
    base = WINDOWS[index][0]
    return full[:, base : base + 256]


def column_softmax(scores):
    e = jnp.exp(scores - jnp.max(scores, 0, keepdims=True))
    return (e * (1.0 / jnp.sum(e, 0, keepdims=True))).astype(BF)


def score_grads(probs, grads):
    p = probs.astype(F32)
    return (p * (grads - jnp.sum(grads * p, 0, keepdims=True))).astype(BF)


def stack_heads(full, index):
    base, off = WINDOWS[index]
    win = full[:, base : base + 256]
    lane = lax.broadcasted_iota(jnp.int32, win.shape, 1)
    blocks = []
    for h in range(3):
        lo = off + 64 * h
        blocks.append(jnp.where((lane >= lo) & (lane < lo + 64), win, 0.0))
    return jnp.concatenate(blocks, 0).astype(BF)


def unstack_heads(stacked, index, rows):
    _, off = WINDOWS[index]
    lane = lax.broadcasted_iota(jnp.int32, (rows, 256), 1)
    out = None
    for h in range(3):
        lo = off + 64 * h
        part = jnp.where((lane >= lo) & (lane < lo + 64), stacked[rows * h : rows * (h + 1)], 0.0)
        out = part if out is None else out + part
    return out


def join_windows(parts):
    a, b, c, d = parts
    return jnp.concatenate(
        [
            a[:, :128],
            a[:, 128:] + b[:, :128],
            b[:, 128:],
            c[:, :128],
            c[:, 128:] + d[:, :128],
            d[:, 128:],
        ],
        1,
    )


def self_block(x32, bias, mats, vecs, put, att_s):
    rb, length, width = x32.shape
    n = rb * length
    wq, wk, wv, wo, wc = mats
    qb, vb, ob, g1, b1, pb = vecs
    x32 = x32.reshape(n, width)
    x = x32.astype(BF)
    q_o, k_o, v_o, p_o = put("q"), put("k"), put("v"), put("p")
    q_o[...] = (nn(x, wq()) + qb).reshape(rb, length, width).astype(BF)
    k_o[...] = nn(x, wk()).reshape(rb, length, width).astype(BF)
    v_o[...] = (nn(x, wv()) + vb).reshape(rb, length, width).astype(BF)

    def row(r, carry):
        qr = q_o[r].astype(F32) * 0.125
        kr = k_o[r].astype(F32)
        vr = v_o[r].astype(F32)
        kws = [window(kr, i).astype(BF) for i in range(4)]
        vws = [window(vr, i).astype(BF) for i in range(4)]
        qss = [stack_heads(qr, i) for i in range(4)]
        mask = bias[r]
        scores = [nt(kws[i], qss[i]) + mask for i in range(4)]
        ps = [column_softmax(st) for st in scores]
        outs = [tn(ps[i], vws[i]) for i in range(4)]
        for i in range(4):
            p_o[r, i] = ps[i]
        att_s[r] = join_windows([unstack_heads(outs[i], i, length) for i in range(4)])
        return carry

    lax.fori_loop(0, rb, row, 0)
    att32 = att_s[...]
    put("att")[...] = att32.astype(BF)
    att = att32.reshape(n, width).astype(BF)
    u1 = x32 + nn(att, wo()) + ob
    put("u1")[...] = u1.reshape(rb, length, width)
    xhat, _ = norm_parts(u1)
    first32 = xhat * g1 + b1
    put("first")[...] = first32.reshape(rb, length, width).astype(BF)
    put("probe")[...] = (nn(first32.astype(BF), wc()) + pb).reshape(rb, length, width).astype(BF)


SELF_OUTS = ("q", "k", "v", "p", "att", "u1", "first", "probe")


def self_forward(
    tok, bias, wq, wk, wv, wo, wc, qb, vb, ob, g1, b1, pb, q_o, k_o, v_o, p_o, att_o, u1_o, f_o, pr_o, att_s
):
    outs = dict(zip(SELF_OUTS, (q_o, k_o, v_o, p_o, att_o, u1_o, f_o, pr_o)))
    mats = [lambda ref=ref: ref[...] for ref in (wq, wk, wv, wo, wc)]
    vecs = [ref[...] for ref in (qb, vb, ob, g1, b1, pb)]
    self_block(tok[...].astype(F32), bias, mats, vecs, lambda name: outs[name], att_s)


def cross_forward(starts, order, proj, wk, wv, cb, probe, k_o, v_o, p_o, mix_o, pr_s):
    i = pl.program_id(0)
    points = proj.shape[1]
    length = probe.shape[1]

    @pl.when(i == 0)
    def _():
        pr_s[...] = jnp.zeros_like(pr_s)

    lo, hi = starts[i], starts[i + 1]

    @pl.when(hi > lo)
    def _():
        pr_s[0:points, :] = proj[0]
        pr = pr_s[...]
        k_o[0] = nn(pr, wk[...]).astype(BF)
        v_o[0] = (nn(pr, wv[...]) + cb[...]).astype(BF)

        def row(j, carry):
            r = order[j]
            qr = probe[r].astype(F32) * 0.125
            qss = [stack_heads(qr, g) for g in range(4)]
            scores = [nt(k_o[0, :, WINDOWS[g][0] : WINDOWS[g][0] + 256], qss[g]) for g in range(4)]
            point = lax.broadcasted_iota(jnp.int32, scores[0].shape, 0)
            ps = [column_softmax(jnp.where(point < points, st, -1e30)) for st in scores]
            outs = [tn(ps[g], v_o[0, :, WINDOWS[g][0] : WINDOWS[g][0] + 256]) for g in range(4)]
            for g in range(4):
                p_o[r, g] = ps[g]
            mix_o[r] = join_windows([unstack_heads(outs[g], g, length) for g in range(4)]).astype(BF)
            return carry

        lax.fori_loop(lo, hi, row, 0)


def tail_kernel(
    u1, mix, og, wco, w1, w2, g1, b1, cb, g2, s2, wb, nb, g3, s3,
    out_o, act_o, gi_o, sec_o, gb3_o, gm_o, gb2_o, gc_o, vec_o, wbg_o,
    act_s, gp_s, acc_s,
):
    step = pl.program_id(0)
    rb, length, width = u1.shape
    n = rb * length
    chunks = w1.shape[0]

    @pl.when(step == 0)
    def _():
        vec_o[...] = jnp.zeros_like(vec_o)
        wbg_o[...] = jnp.zeros_like(wbg_o)

    def flat(ref):
        return ref[...].astype(F32).reshape(n, width)

    def fold(value):
        return value.reshape(rb, length, width)

    xhat1, _ = norm_parts(flat(u1))
    first = xhat1 * g1[...] + b1[...]
    u2 = first + nn(flat(mix).astype(BF), wco[...]) + cb[...]
    xhat2, inv2 = norm_parts(u2)
    second = (xhat2 * g2[...] + s2[...]).astype(BF)
    sec32 = second.astype(F32)
    sec_o[...] = fold(sec32).astype(BF)
    acc_s[...] = sec32 + nb[...]

    def up(c, carry):
        inner = nn(second, w1[c]) + wb[c]
        act, slope = gelu_parts(inner)
        act = act.astype(BF)
        gp_s[c] = slope
        act_o[c] = act
        acc_s[...] += nn(act, w2[c])
        return carry

    lax.fori_loop(0, chunks, up, 0)
    xhat3, inv3 = norm_parts(acc_s[...])
    out_o[...] = fold(xhat3 * g3[...] + s3[...]).astype(BF)
    y = flat(og)
    grad_summed = norm_back(y, g3[...], xhat3, inv3)
    gb3 = grad_summed.astype(BF)
    gb3f = gb3.astype(F32)
    gb3_o[...] = fold(gb3f).astype(BF)
    vec_o[0:1] += jnp.sum(y * xhat3, 0, keepdims=True)
    vec_o[1:2] += jnp.sum(y, 0, keepdims=True)
    vec_o[2:3] += jnp.sum(gb3f, 0, keepdims=True)
    acc_s[...] = grad_summed

    def down(c, carry):
        gi = (nt(gb3, w2[c]) * gp_s[c]).astype(BF)
        gi_o[c] = gi
        wbg_o[c] += jnp.sum(gi.astype(F32), 0, keepdims=True)
        acc_s[...] += nt(gi, w1[c])
        return carry

    lax.fori_loop(0, chunks, down, 0)
    y2 = acc_s[...].astype(BF).astype(F32)
    gm = norm_back(y2, g2[...], xhat2, inv2)
    gm_o[...] = fold(gm)
    gb2 = gm.astype(BF)
    gb2f = gb2.astype(F32)
    gb2_o[...] = fold(gb2f).astype(BF)
    vec_o[3:4] += jnp.sum(y2 * xhat2, 0, keepdims=True)
    vec_o[4:5] += jnp.sum(y2, 0, keepdims=True)
    vec_o[5:6] += jnp.sum(gb2f, 0, keepdims=True)
    gc_o[...] = fold(nt(gb2, wco[...])).astype(BF)


def cross_backward(
    starts, order, proj, keys, values, wk, wv, probe, grad, probs,
    dpr_o, dproj_o, dwk_o, dwv_o, dcb_o,
    pr_s, dk_s, dv_s, dwk_s, dwv_s,
):
    i = pl.program_id(0)
    points = proj.shape[1]
    length = probe.shape[1]

    @pl.when(i == 0)
    def _():
        pr_s[...] = jnp.zeros_like(pr_s)
        dwk_s[...] = jnp.zeros_like(dwk_s)
        dwv_s[...] = jnp.zeros_like(dwv_s)
        dcb_o[...] = jnp.zeros_like(dcb_o)

    lo, hi = starts[i], starts[i + 1]

    @pl.when(hi == lo)
    def _():
        dproj_o[...] = jnp.zeros_like(dproj_o)

    @pl.when(hi > lo)
    def _():
        dk_s[...] = jnp.zeros_like(dk_s)
        dv_s[...] = jnp.zeros_like(dv_s)

        def row(j, carry):
            r = order[j]
            qr = probe[r].astype(F32) * 0.125
            gr = grad[r].astype(F32)
            gss = [stack_heads(gr, g) for g in range(4)]
            dps = [nt(values[0, :, WINDOWS[g][0] : WINDOWS[g][0] + 256], gss[g]) for g in range(4)]
            qss = [stack_heads(qr, g) for g in range(4)]
            pbs = [probs[r, g] for g in range(4)]
            dvs = [nn(pbs[g], gss[g]) for g in range(4)]
            dss = [score_grads(pbs[g], dps[g]) for g in range(4)]
            dks = [nn(dss[g], qss[g]) for g in range(4)]
            outs = [tn(dss[g], keys[0, :, WINDOWS[g][0] : WINDOWS[g][0] + 256]) for g in range(4)]
            dv_s[...] += join_windows(dvs)
            dk_s[...] += join_windows(dks)
            dpr_o[r] = (join_windows([unstack_heads(outs[g], g, length) for g in range(4)]) * 0.125).astype(BF)
            return carry

        lax.fori_loop(lo, hi, row, 0)
        pr_s[0:points, :] = proj[0]
        pr = pr_s[...]
        dk = dk_s[...].astype(BF)
        dv = dv_s[...].astype(BF)
        dcb_o[0:1] += jnp.sum(dv.astype(F32), 0, keepdims=True)
        dproj = (nt(dk, wk[...]) + nt(dv, wv[...])).astype(BF)
        dproj_o[0] = dproj[0:points]
        dwk_s[...] += tn(pr, dk)
        dwv_s[...] += tn(pr, dv)

    @pl.when(i == pl.num_programs(0) - 1)
    def _():
        dwk_o[...] = dwk_s[...].astype(BF)
        dwv_o[...] = dwv_s[...].astype(BF)


def self_backward(
    gm, dpr, u1, q, k, v, probs, wq, wk, wv, wo, wc, g1,
    gb1_o, dq_o, dk_o, dv_o, tg_o, vec_o,
    ga_s, dq_s, dk_s, dv_s,
):
    step = pl.program_id(0)
    rb, length, width = u1.shape
    n = rb * length

    @pl.when(step == 0)
    def _():
        vec_o[...] = jnp.zeros_like(vec_o)

    def flat(ref):
        return ref[...].astype(F32).reshape(n, width)

    def fold(value):
        return value.reshape(rb, length, width)

    dpr32 = flat(dpr)
    grad_first = flat(gm) + nt(dpr32.astype(BF), wc[...])
    xhat, inv = norm_parts(flat(u1))
    low = norm_back(grad_first, g1[...], xhat, inv)
    gb1 = low.astype(BF)
    gb1f = gb1.astype(F32)
    gb1_o[...] = fold(gb1f).astype(BF)
    vec_o[0:1] += jnp.sum(grad_first * xhat, 0, keepdims=True)
    vec_o[1:2] += jnp.sum(grad_first, 0, keepdims=True)
    vec_o[2:3] += jnp.sum(gb1f, 0, keepdims=True)
    vec_o[3:4] += jnp.sum(dpr32, 0, keepdims=True)
    ga_s[...] = fold(nt(gb1, wo[...]).astype(BF).astype(F32))

    def row(r, carry):
        qr = q[r].astype(F32) * 0.125
        kr = k[r].astype(F32)
        vr = v[r].astype(F32)
        gr = ga_s[r]
        gss = [stack_heads(gr, i) for i in range(4)]
        vws = [window(vr, i).astype(BF) for i in range(4)]
        dps = [nt(vws[i], gss[i]) for i in range(4)]
        qss = [stack_heads(qr, i) for i in range(4)]
        kws = [window(kr, i).astype(BF) for i in range(4)]
        pbs = [probs[r, i] for i in range(4)]
        dvs = [nn(pbs[i], gss[i]) for i in range(4)]
        dss = [score_grads(pbs[i], dps[i]) for i in range(4)]
        dks = [nn(dss[i], qss[i]) for i in range(4)]
        outs = [tn(dss[i], kws[i]) for i in range(4)]
        dq_s[r] = join_windows([unstack_heads(outs[i], i, length) for i in range(4)]) * 0.125
        dk_s[r] = join_windows(dks)
        dv_s[r] = join_windows(dvs)
        return carry

    lax.fori_loop(0, rb, row, 0)
    dq = dq_s[...].reshape(n, width).astype(BF)
    dk = dk_s[...].reshape(n, width).astype(BF)
    dv = dv_s[...].reshape(n, width).astype(BF)
    dq_o[...] = dq_s[...].astype(BF)
    dk_o[...] = dk_s[...].astype(BF)
    dv_o[...] = dv_s[...].astype(BF)
    vec_o[4:5] += jnp.sum(dq.astype(F32), 0, keepdims=True)
    vec_o[5:6] += jnp.sum(dv.astype(F32), 0, keepdims=True)
    total = low + nt(dq, wq[...]) + nt(dk, wk[...]) + nt(dv, wv[...])
    tg_o[...] = fold(total).astype(BF)


def sds(shape, dtype):
    return jax.ShapeDtypeStruct(shape, dtype)


def whole(shape, *, single=True):
    zeros = (0,) * len(shape)
    mode = pl.Buffered(1) if single else None
    return pl.BlockSpec(shape, lambda i, *_: zeros, pipeline_mode=mode)


def rows_block(shape, rb):
    rest = tuple(shape[1:])
    return pl.BlockSpec((rb,) + rest, lambda i, *_: (i,) + (0,) * len(rest))


def params(mib):
    return pltpu.CompilerParams(
        dimension_semantics=("arbitrary",), vmem_limit_bytes=mib * 1024 * 1024
    )


def cost(flops, bytes_accessed):
    return pl.CostEstimate(flops=int(flops), bytes_accessed=int(bytes_accessed), transcendentals=0)


def my_place():
    dp, fs = lax.axis_index("dp"), lax.axis_index("fsdp")
    return dp // 2, dp % 2, fs // 2, fs % 2


def device_at(z, y, x, c):
    return (z * 2 + y, x * 2 + c)


def meet(z, y, x, c):
    sem = pltpu.get_barrier_semaphore()
    others = [device_at((z + k) % 4, y, x, c) for k in (1, 2, 3)]
    others += [device_at(z, 1 - y, x, c), device_at(z, y, 1 - x, c), device_at(z, y, x, 1 - c)]
    for other in others:
        pl.semaphore_signal(sem, inc=1, device_id=other, device_id_type=pl.DeviceIdType.MESH)
    pl.semaphore_wait(sem, len(others))


class Copies:
    def __init__(self, send, recv, local):
        self.send, self.recv, self.local = send, recv, local
        self.far = self.near = 0
        self.sent = []

    def prepare(self, src, dst, device):
        i = self.far
        self.far += 1
        return pltpu.make_async_remote_copy(
            src_ref=src, dst_ref=dst, send_sem=self.send.at[i], recv_sem=self.recv.at[i],
            device_id=device, device_id_type=pl.DeviceIdType.MESH,
        )

    def remote(self, src, dst, device):
        copy = self.prepare(src, dst, device)
        copy.start()
        return copy

    def here(self, src, dst):
        i = self.near
        self.near += 1
        copy = pltpu.make_async_copy(src, dst, self.local.at[i])
        copy.start()
        return copy


def arrived(copies):
    for copy in copies:
        copy.wait()


def drive(jobs, order):
    for name in order:
        next(jobs[name], None)
    for job in jobs.values():
        for _ in job:
            pass


PATCH, EXTRA, QUERY, KEY, VALUE, OUT, CQ, CK, W1 = range(9)
W2, CV, CO = 12, 16, 17


FRONT_ORDER = (
    "P", "Q", "P", "P", "Q", "P", "Q", "R", "P", "P", "P", "F", "Q", "P", "Q", "Q", "F", "P",
    "weights", "F", "i0", "i1", "Q", "F", "i0", "i3", "G", "F", "R", "i1", "i3", "Q", "G", "G",
    "i0", "i0", "F", "Q", "self", "i2", "i3", "G", "self", "R", "i2", "F", "G", "self", "i3", "i1",
    "G", "self", "G", "R", "R", "i1", "F", "i2", "self", "R", "R", "G", "i2", "R",
)
REDUCE_ORDER = (
    "p0", "p1", "w0", "p2", "p3", "w1", "p0", "w0", "p1", "p2", "w0", "p3", "p0", "p1", "w1", "p2",
    "p3", "v", "w0", "w1", "v", "w0", "v", "w1", "v",
)


def front_kernel(
    parts, tails, nv, rb, w_in, pat, tok, bias, w_out, p_out, q_o, k_o, v_o, pr_o, att_o, u1_o, f_o, prb_o, vec_o,
    pw, ex, wm, proj_s, q_s, k_s, v_s, pr_s, att_b, u1_s, f_s, prb_s, att_s, send, recv, local,
):
    z, y, x, c = my_place()
    meet(z, y, x, c)
    copies = Copies(send, recv, local)
    rows, length, width = tok.shape
    images = pat.shape[0]

    inner = (z + 1) % 4 >= 2
    partner = z + 1 - 2 * (z % 2)
    across = 3 - z
    ours, theirs = 2 * (z // 2), 2 - 2 * (z // 2)

    def along_z(source, view, tell, local):
        step = copies.remote(source, view(z, 0), device_at(partner, y, x, c))
        tell("own")
        yield
        step.wait()
        if local is not None:
            local.wait()
        tell("partner")
        middle = copies.prepare(view(ours, 2), view(ours, 2), device_at(across, y, x, c))
        outward = copies.prepare(view(theirs, 2), view(theirs, 2), device_at(partner, y, x, c))

        @pl.when(inner)
        def _():
            middle.start()

        yield

        @pl.when(inner)
        def _():
            middle.wait()
            outward.start()
            tell("inner")

        yield

        @pl.when(jnp.logical_not(inner))
        def _():
            outward.wait_recv()
            tell("outer")

        copies.sent.append((inner, outward))
        yield

    def exchanged(source, view, local):
        own = copies.prepare(source, view(z, 0), device_at(z, 1 - y, x, c))
        second = copies.prepare(view(partner, 0), view(partner, 0), device_at(z, 1 - y, x, c))
        third = copies.prepare(view(theirs, 2), view(theirs, 2), device_at(z, 1 - y, x, c))
        start = {"own": own, "partner": second, "inner": third, "outer": third}
        return along_z(source, view, lambda which: start[which].start(), local), (own, second, third)

    def slabs(lo, n):
        pick = pl.ds(lo, n)

        def view(at, many):
            return w_out.at[pick, pl.ds(at, many) if many else at, y, x, c]

        def plane(at, many):
            return w_out.at[pick, pl.ds(at, many) if many else at, :, x, c]

        local = copies.here(w_in.at[pick], view(z, 0))
        moving, (own, second, third) = exchanged(w_in.at[pick], view, None)
        next(moving)
        yield
        own.wait()
        local.wait()
        steps = [copies.remote(plane(z, 0), plane(z, 0), device_at(z, y, 1 - x, c))]
        yield
        for _ in range(3):
            next(moving)
            yield
        second.wait()
        steps.append(copies.remote(plane(partner, 0), plane(partner, 0), device_at(z, y, 1 - x, c)))
        yield
        third.wait()
        steps.append(copies.remote(plane(theirs, 2), plane(theirs, 2), device_at(z, y, 1 - x, c)))
        yield
        arrived(steps)
        half = w_out.at[pick, :, :, :, c]
        step = copies.remote(half, half, device_at(z, y, x, 1 - c))
        yield
        step.wait()

    def patch_weights():
        rest = pw.shape[4] - tails
        arrived(
            [
                copies.here(w_out.at[PATCH], pw.at[:, :, :, :, 0:rest]),
                copies.here(w_out.at[EXTRA, :, :, :, :, 0:tails], pw.at[:, :, :, :, rest:]),
                copies.here(w_out.at[EXTRA], ex),
            ]
        )
        total = jnp.zeros(ex.shape[4:], F32)
        for zz in range(4):
            for yy in range(2):
                for xx in range(2):
                    for cc in range(2):
                        total = total + ex[zz, yy, xx, cc].astype(F32)
        vec_o[...] = total
        yield

    def vec(j):
        return vec_o[tails + j : tails + j + 1, :]

    def image(i):
        full = pw[...].reshape(pat.shape[2], width)
        proj_s[i] = (nn(pat[i], full) + vec(5)).astype(BF)

        def view(at, many):
            return p_out.at[pl.ds(at, many) if many else at, y, i]

        moving, steps = exchanged(proj_s.at[i], view, copies.here(proj_s.at[i], view(z, 0)))
        yield from moving
        arrived(steps)

    def attention():
        arrived([copies.here(w_out.at[QUERY + m], wm.at[m]) for m in range(5)])
        yield
        scratch = dict(zip(SELF_OUTS, (q_s, k_s, v_s, pr_s, att_b, u1_s, f_s, prb_s)))
        finals = dict(zip(SELF_OUTS, (q_o, k_o, v_o, pr_o, att_o, u1_o, f_o, prb_o)))
        mats = [lambda m=m: wm[m].reshape(width, width) for m in range(5)]
        outgoing = []
        for b in range(rows // rb):
            pick = pl.ds(b * rb, rb)
            self_block(
                tok[pick].astype(F32), bias.at[pick], mats, [vec(j) for j in (0, 1, 2, 3, 4, 6)],
                lambda name: scratch[name].at[pick], att_s,
            )
            outgoing += [copies.here(scratch[name].at[pick], finals[name].at[pick]) for name in SELF_OUTS]
            yield
        arrived(outgoing)

    jobs = {name: slabs(lo, n) for name, (lo, n) in parts.items()}
    jobs["weights"] = patch_weights()
    for i in range(images):
        jobs["i%d" % i] = image(i)
    jobs["self"] = attention()
    drive(jobs, FRONT_ORDER)
    for when, copy in copies.sent:

        @pl.when(when)
        def _(copy=copy):
            copy.wait_send()


def reduce_kernel(
    parts, w_in, p_in, pat, vb_in, w_out, p_out, acc, rc, rx, ry, rz, pacc, pry, prz, dwp, pv, send, recv, local
):
    z, y, x, c = my_place()
    meet(z, y, x, c)
    copies = Copies(send, recv, local)

    def up(ref, *at):
        return ref[at].astype(F32)

    def slabs(lo, n, src):
        pick = pl.ds(lo, n)
        own = copies.here(src.at[:, :, :, :, c], acc.at[pick])
        step = copies.remote(src.at[:, :, :, :, 1 - c], rc.at[pick], device_at(z, y, x, 1 - c))
        yield
        own.wait()
        step.wait()

        def add_x(i, carry):
            s, zz = lo + i // 4, i % 4
            for yy in range(2):
                acc[s, zz, yy, 1 - x] = (up(acc, s, zz, yy, 1 - x) + up(rc, s, zz, yy, 1 - x)).astype(BF)
            return carry

        lax.fori_loop(0, 4 * n, add_x, 0)
        step = copies.remote(acc.at[pick, :, :, 1 - x], rx.at[pick], device_at(z, y, 1 - x, c))
        yield
        step.wait()

        def add_y(i, carry):
            s, zz = lo + i // 4, i % 4
            acc[s, zz, 1 - y, x] = (
                up(acc, s, zz, 1 - y, x) + up(rc, s, zz, 1 - y, x) + up(rx, s, zz, 1 - y)
            ).astype(BF)
            return carry

        lax.fori_loop(0, 4 * n, add_y, 0)
        step = copies.remote(acc.at[pick, :, 1 - y, x], ry.at[pick], device_at(z, 1 - y, x, c))
        yield
        step.wait()
        steps = []
        for k in (1, 3, 2):
            zz = (z + k) % 4

            def add_z(i, carry):
                s = lo + i
                acc[s, zz, y, x] = (
                    up(acc, s, zz, y, x) + up(rc, s, zz, y, x) + up(rx, s, zz, y) + up(ry, s, zz)
                ).astype(BF)
                return carry

            lax.fori_loop(0, n, add_z, 0)
            steps.append(
                copies.remote(acc.at[pick, zz, y, x], rz.at[k - 1, pick], device_at(zz, y, x, c))
            )
        yield
        arrived(steps)

        def add_last(i, carry):
            s = lo + i
            w_out[s] = (
                up(acc, s, z, y, x) + up(rc, s, z, y, x) + up(rx, s, z, y) + up(ry, s, z)
                + up(rz, 0, s) + up(rz, 1, s) + up(rz, 2, s)
            )
            return carry

        lax.fori_loop(0, n, add_last, 0)

    def image(i):
        own = copies.here(p_in.at[:, y, i], pacc.at[i])
        step = copies.remote(p_in.at[:, 1 - y, i], pry.at[i], device_at(z, 1 - y, x, c))
        yield
        own.wait()
        step.wait()
        steps = []
        for k in (1, 3, 2):
            zz = (z + k) % 4
            pacc[i, zz] = (up(pacc, i, zz) + up(pry, i, zz)).astype(BF)
            steps.append(copies.remote(pacc.at[i, zz], prz.at[k - 1, i], device_at(zz, y, x, c)))
        yield
        arrived(steps)
        p_out[i] = (
            up(pacc, i, z) + up(pry, i, z) + up(prz, 0, i) + up(prz, 1, i) + up(prz, 2, i)
        ).astype(BF)
        yield

    def patch_grads(first):
        sr, width = w_out.shape[1:]
        images = p_in.shape[2]
        total = tn(pat[0], p_out[0])
        bias = jnp.sum(p_out[0].astype(F32), 0, keepdims=True)
        for i in range(1, images):
            total = total + tn(pat[i], p_out[i])
            bias = bias + jnp.sum(p_out[i].astype(F32), 0, keepdims=True)
        dwp[...] = total.reshape(dwp.shape)

        def fill(d, carry):
            zz, yy, xx, cc = d // 8, (d // 4) % 2, (d // 2) % 2, d % 2
            rows = dwp[d]
            pv[0, zz, yy, xx, cc] = rows[:sr].astype(BF)
            block = vb_in[d]
            row = lax.broadcasted_iota(jnp.int32, block.shape, 0)
            block = jnp.where(row == 5, bias, block)
            pv[1, zz, yy, xx, cc] = jnp.concatenate([rows[sr:], block], 0).astype(BF)
            return carry

        lax.fori_loop(0, 32, fill, 0)
        yield from slabs(first, 2, pv)

    jobs = {}
    for i in range(p_in.shape[2]):
        jobs["p%d" % i] = image(i)
    for j, (lo, n) in enumerate(parts):
        jobs["w%d" % j] = slabs(lo, n, w_in.at[pl.ds(lo, n)])
    jobs["v"] = patch_grads(w_in.shape[0])
    drive(jobs, REDUCE_ORDER)


def split_slabs(count):
    first = (count + 1) // 2
    return ((0, first), (first, count - first))


def front(slabs, patches, tokens, bias, tails, nv):
    n, sr, width = slabs.shape
    images, points, pwidth = patches.shape
    rows, length, _ = tokens.shape
    rb = 8 if rows % 8 == 0 else 1
    parts = {"P": (PATCH, 2), "Q": (QUERY, 6), "F": (W1, 4), "G": (W2, 4), "R": (CV, 2)}
    remote = 10 * len(parts) + 6 * images
    near = len(parts) + images + 3 + 5 + len(SELF_OUTS) * (rows // rb)
    tok_sh = (rows, length, width)
    probs = (rows, 4, length, 3 * length)
    kept = [sds(tok_sh, BF), sds(tok_sh, BF), sds(tok_sh, BF), sds(probs, BF), sds(tok_sh, BF), sds(tok_sh, F32), sds(tok_sh, BF), sds(tok_sh, BF)]
    hbm = pl.BlockSpec(memory_space=pl.ANY)
    vmem = pl.BlockSpec(memory_space=pltpu.VMEM)
    w_all, p_all, *rest = pl.pallas_call(
        functools.partial(front_kernel, parts, tails, nv, rb),
        in_specs=[hbm, vmem, vmem, vmem],
        out_specs=[hbm] * 10 + [vmem],
        out_shape=[
            sds((n, 4, 2, 2, 2, sr, width), BF), sds((4, 2, images, points, width), BF), *kept, sds((sr, width), F32),
        ],
        scratch_shapes=[
            pltpu.VMEM((4, 2, 2, 2, pwidth // 32, width), BF),
            pltpu.VMEM((4, 2, 2, 2, sr, width), BF),
            pltpu.VMEM((5, 4, 2, 2, 2, sr, width), BF),
            pltpu.VMEM((images, points, width), BF),
            *[pltpu.VMEM(item.shape, item.dtype) for item in kept],
            pltpu.VMEM((rb, length, width), F32),
            pltpu.SemaphoreType.DMA((remote,)),
            pltpu.SemaphoreType.DMA((remote,)),
            pltpu.SemaphoreType.DMA((near,)),
        ],
        compiler_params=pltpu.CompilerParams(
            collective_id=0, has_side_effects=True, vmem_limit_bytes=58 * 1024 * 1024
        ),
        name="front",
    )(slabs, patches, tokens, bias)
    return w_all.reshape(n, 32 * sr, width), p_all.reshape(8 * images, points, width), rest[:8], rest[8]


def reduce_all(slabs, grads, patches, vec_block):
    n, full, width = slabs.shape
    sr = full // 32
    total, points, _ = grads.shape
    images, _, pwidth = patches.shape
    parts = split_slabs(n)
    copies = 6 * (len(parts) + 1) + 4 * images
    hbm = pl.BlockSpec(memory_space=pl.ANY)
    vmem = pl.BlockSpec(memory_space=pltpu.VMEM)
    m = n + 2
    w_shard, p_shard = pl.pallas_call(
        functools.partial(reduce_kernel, parts),
        in_specs=[hbm, hbm, vmem, vmem],
        out_specs=[vmem] * 2,
        out_shape=[sds((m, sr, width), F32), sds((images, points, width), BF)],
        scratch_shapes=[
            pltpu.VMEM((m, 4, 2, 2, sr, width), BF),
            pltpu.VMEM((m, 4, 2, 2, sr, width), BF),
            pltpu.VMEM((m, 4, 2, sr, width), BF),
            pltpu.VMEM((m, 4, sr, width), BF),
            pltpu.VMEM((3, m, sr, width), BF),
            pltpu.VMEM((images, 4, points, width), BF),
            pltpu.VMEM((images, 4, points, width), BF),
            pltpu.VMEM((3, images, points, width), BF),
            pltpu.VMEM((32, pwidth // 32, width), F32),
            pltpu.VMEM((2, 4, 2, 2, 2, sr, width), BF),
            pltpu.SemaphoreType.DMA((copies,)),
            pltpu.SemaphoreType.DMA((copies,)),
            pltpu.SemaphoreType.DMA((len(parts) + 1 + images,)),
        ],
        compiler_params=pltpu.CompilerParams(
            collective_id=1, has_side_effects=True, vmem_limit_bytes=58 * 1024 * 1024
        ),
        name="reduce_all",
    )(slabs.reshape(n, 4, 2, 2, 2, sr, width), grads.reshape(4, 2, images, points, width), patches, vec_block)
    return w_shard, p_shard


def gather(value, axis):
    return lax.all_gather(value, AXES, axis=axis, tiled=True)


def on_device(
    tokens, patches, segments, owner, image_slot, out_grad,
    self_query, query_bias, self_key, self_value, value_bias, self_output, output_bias,
    first_gain, first_norm_bias, patch_proj, patch_bias, cross_query, probe_bias, cross_key,
    cross_value, content_bias, cross_output, cross_bias, second_gain, second_shift,
    widen_weight, widen_bias, narrow_weight, narrow_bias, third_gain, third_shift,
):
    rows, length, width = tokens.shape
    images, points, pwidth = patches.shape
    groups = lax.axis_size("dp")
    shards = groups * lax.axis_size("fsdp")
    total_images = groups * images
    hidden = widen_weight.shape[1]
    chunks = hidden // width
    sr = self_query.shape[0]
    wr = widen_bias.shape[0]

    place = lax.axis_index("dp") * lax.axis_size("fsdp") + lax.axis_index("fsdp")
    vec_list = (
        query_bias, value_bias, output_bias, first_gain, first_norm_bias, patch_bias, probe_bias,
        content_bias, cross_bias, second_gain, second_shift, narrow_bias, third_gain, third_shift,
    )
    nv = len(vec_list)
    pr = patch_proj.shape[0]
    tails = pr - sr
    lane_block = jnp.arange(width, dtype=jnp.int32)[None, :] // sr
    vec_rows = jnp.where(lane_block == place, jnp.tile(jnp.stack(vec_list), (1, shards)), jnp.zeros((), BF))
    wb_row = jnp.pad(widen_bias, (0, width - wr))[None]
    extra = jnp.concatenate([patch_proj[sr:], vec_rows, wb_row], 0)
    er = max(sr, extra.shape[0])
    own_rows = er == sr and groups == 8 and shards == 32
    extra = jnp.pad(extra, ((0, er - extra.shape[0]), (0, 0)))
    widen_slabs = widen_weight.reshape(sr, shards, chunks, sr).transpose(2, 0, 1, 3).reshape(chunks, sr, width)
    narrow_slabs = narrow_weight.reshape(chunks, sr, width)
    slabs_in = jnp.concatenate(
        [
            jnp.stack(
                [
                    patch_proj[:sr], extra[:sr], self_query, self_key, self_value, self_output,
                    cross_query, cross_key,
                ]
            ),
            widen_slabs, narrow_slabs, jnp.stack([cross_value, cross_output]),
        ]
    )

    image = owner * images + image_slot
    idx = jnp.arange(rows, dtype=jnp.int32)
    before = (image[None, :] < image[:, None]) | ((image[None, :] == image[:, None]) & (idx[None, :] < idx[:, None]))
    rank = jnp.sum(before.astype(jnp.int32), 1)
    order = jnp.sum(jnp.where(rank[:, None] == idx[None, :], idx[:, None], 0), 0).astype(jnp.int32)
    starts = jnp.sum((image[None, :] < jnp.arange(total_images + 1, dtype=jnp.int32)[:, None]).astype(jnp.int32), 1)

    same = segments[:, :, None] == segments[:, None, :]
    bias = jnp.where(same, 0.0, mask_fill).astype(F32)
    bias = jnp.concatenate([bias, bias, bias], 2)

    rb = 8 if rows % 8 == 0 else 1
    grid = (rows // rb,)
    tok_sh = (rows, length, width)
    slab = (width, width)

    def wspec(j):
        return pl.BlockSpec((None, width, width), lambda i, *_: (j, 0, 0), pipeline_mode=pl.Buffered(1))

    vspec = whole((1, width))
    tb = rows_block(tok_sh, rb)
    self_p = (rows, 4, length, 3 * length)
    if own_rows:
        w_a, proj_all, kept, vec_all = front(slabs_in, patches, tokens, bias, tails, nv)
        vec_all = vec_all[tails : tails + nv]
        extra_all = w_a[EXTRA].reshape(shards, er, width)
    else:
        w_a = gather(slabs_in, 1)
        extra_all = gather(extra, 0).reshape(shards, er, width)
        vec_all = jnp.sum(extra_all[:, tails : tails + nv].astype(F32), 0)
    (qb, vb, ob, g1, b1, pab, prb, cob, crb, g2, s2, nab, g3, s3) = [vec_all[j : j + 1] for j in range(nv)]
    wb = extra_all[:, tails + nv, :wr].astype(F32)
    wb = wb.reshape(shards, chunks, sr).transpose(1, 0, 2).reshape(chunks, 1, width)
    patch_full = jnp.concatenate([w_a[PATCH].reshape(shards, sr, width), extra_all[:, :tails]], 1)
    patch_full = patch_full.reshape(shards * pr, width)
    if not own_rows:
        projected = lax.dot_general(patches, patch_full, (((2,), (0,)), ((), ())), preferred_element_type=F32)
        proj_all = lax.all_gather((projected + pab).astype(BF), "dp", axis=0, tiled=True)
        kept = pl.pallas_call(
            self_forward,
            grid=grid,
            in_specs=[tb, rows_block((rows, length, 3 * length), rb)]
            + [wspec(j) for j in (QUERY, KEY, VALUE, OUT, CQ)]
            + [vspec] * 6,
            out_specs=[tb, tb, tb, rows_block(self_p, rb), tb, tb, tb, tb],
            out_shape=[
                sds(tok_sh, BF), sds(tok_sh, BF), sds(tok_sh, BF), sds(self_p, BF),
                sds(tok_sh, BF), sds(tok_sh, F32), sds(tok_sh, BF), sds(tok_sh, BF),
            ],
            scratch_shapes=[pltpu.VMEM((rb, length, width), F32)],
            compiler_params=params(48),
            cost_estimate=cost(11 * rows * length * width * width, 30e6),
            name="self_forward",
        )(tokens, bias, w_a, w_a, w_a, w_a, w_a, qb, vb, ob, g1, b1, prb)
    q, k, v, probs, attended, u1, first_low, probe = kept

    padded = -(-points // 16) * 16
    kv_sh = (total_images, padded, width)
    cross_p = (rows, 4, padded, 3 * length)
    img_spec = pl.BlockSpec((1, points, width), lambda i, *_: (i, 0, 0))
    kv_spec = pl.BlockSpec((1, padded, width), lambda i, *_: (i, 0, 0))
    image_keys, image_values, cprobs, mixed = pl.pallas_call(
        cross_forward,
        grid_spec=pltpu.PrefetchScalarGridSpec(
            num_scalar_prefetch=2,
            grid=(total_images,),
            in_specs=[img_spec, wspec(CK), wspec(CV), vspec, whole(tok_sh)],
            out_specs=[kv_spec, kv_spec, whole(cross_p), whole(tok_sh)],
            scratch_shapes=[pltpu.VMEM((padded, width), BF)],
        ),
        out_shape=[sds(kv_sh, BF), sds(kv_sh, BF), sds(cross_p, BF), sds(tok_sh, BF)],
        compiler_params=params(48),
        cost_estimate=cost(4 * total_images * points * width * width, 40e6),
        name="cross_forward",
    )(starts, order, proj_all, w_a, w_a, cob, probe)

    def chunk_w(j):
        return pl.BlockSpec(
            (chunks, width, width), lambda i, *_: (W1 // chunks + j, 0, 0), pipeline_mode=pl.Buffered(1)
        )

    n_tok = rows * length
    hid_sh = (chunks, n_tok, width)
    hid_spec = pl.BlockSpec((chunks, rb * length, width), lambda i, *_: (0, i, 0))
    (output, active, grad_inner, second, gb3, grad_mid, gb2, grad_crossed, vec_t, wb_grad) = pl.pallas_call(
        tail_kernel,
        grid=grid,
        in_specs=[tb, tb, tb, wspec(CO), chunk_w(0), chunk_w(1)]
        + [vspec] * 5
        + [whole((chunks, 1, width))]
        + [vspec] * 3,
        out_specs=[tb, hid_spec, hid_spec, tb, tb, tb, tb, tb, whole((8, width)), whole((chunks, 1, width))],
        out_shape=[
            sds(tok_sh, BF), sds(hid_sh, BF), sds(hid_sh, BF), sds(tok_sh, BF), sds(tok_sh, BF),
            sds(tok_sh, F32), sds(tok_sh, BF), sds(tok_sh, BF), sds((8, width), F32), sds((chunks, 1, width), F32),
        ],
        scratch_shapes=[
            pltpu.VMEM((8, 128), BF),
            pltpu.VMEM((chunks, rb * length, width), F32),
            pltpu.VMEM((rb * length, width), F32),
        ],
        compiler_params=params(56),
        cost_estimate=cost(18 * n_tok * width * width + 8 * n_tok * width * hidden, 50e6),
        name="tail",
    )(u1, mixed, out_grad, w_a, w_a, w_a, g1, b1, crb, g2, s2, wb, nab, g3, s3)

    dprobe, dproj, dwk, dwv, dcb = pl.pallas_call(
        cross_backward,
        grid_spec=pltpu.PrefetchScalarGridSpec(
            num_scalar_prefetch=2,
            grid=(total_images,),
            in_specs=[img_spec, kv_spec, kv_spec, wspec(CK), wspec(CV), whole(tok_sh), whole(tok_sh), whole(cross_p)],
            out_specs=[whole(tok_sh), img_spec, whole(slab), whole(slab), whole((8, width))],
            scratch_shapes=[
                pltpu.VMEM((padded, width), BF),
                pltpu.VMEM((padded, width), F32),
                pltpu.VMEM((padded, width), F32),
                pltpu.VMEM((width, width), F32),
                pltpu.VMEM((width, width), F32),
            ],
        ),
        out_shape=[sds(tok_sh, BF), sds((total_images, points, width), BF), sds(slab, BF), sds(slab, BF), sds((8, width), F32)],
        compiler_params=params(56),
        cost_estimate=cost(8 * total_images * points * width * width, 50e6),
        name="cross_backward",
    )(starts, order, proj_all, image_keys, image_values, w_a, w_a, probe, grad_crossed, cprobs)

    gb1, dq, dk, dv, tokens_grad, vec_s = pl.pallas_call(
        self_backward,
        grid=grid,
        in_specs=[tb, tb, tb, tb, tb, tb, rows_block(self_p, rb)]
        + [wspec(j) for j in (QUERY, KEY, VALUE, OUT, CQ)]
        + [vspec],
        out_specs=[tb, tb, tb, tb, tb, whole((8, width))],
        out_shape=[sds(tok_sh, BF)] * 5 + [sds((8, width), F32)],
        scratch_shapes=[pltpu.VMEM((rb, length, width), F32)] * 4,
        compiler_params=params(52),
        cost_estimate=cost(14 * n_tok * width * width, 40e6),
        name="self_backward",
    )(grad_mid, dprobe, u1, q, k, v, probs, w_a, w_a, w_a, w_a, w_a, g1)

    def wgrad(left, right):
        return tn(left.reshape(n_tok, width), right.reshape(n_tok, width)).astype(BF)

    grad_narrow = lax.dot_general(
        active, gb3.reshape(n_tok, width), (((1,), (0,)), ((), ())), preferred_element_type=F32
    ).astype(BF)
    grad_widen = jnp.stack([wgrad(second, grad_inner[c]) for c in range(chunks)])
    ffn_shard = lax.psum_scatter(
        jnp.concatenate([grad_widen, grad_narrow], 0), AXES, scatter_dimension=1, tiled=True
    ).astype(F32)

    zero_row = jnp.zeros((1, width), F32)
    vec_grads = jnp.concatenate(
        [
            vec_s[4:5], vec_s[5:6], vec_s[2:3], vec_s[0:1], vec_s[1:2], zero_row, vec_s[3:4], dcb[0:1],
            vec_t[5:6], vec_t[3:4], vec_t[4:5], vec_t[2:3], vec_t[0:1], vec_t[1:2],
        ]
    )
    wb_flat = wb_grad.reshape(chunks, shards, sr).transpose(1, 0, 2).reshape(shards, 1, wr)
    vec_block = jnp.concatenate(
        [
            jnp.broadcast_to(vec_grads[None], (shards, nv, width)),
            jnp.pad(wb_flat, ((0, 0), (0, 0), (0, width - wr))),
            jnp.zeros((shards, er - tails - nv - 1, width), F32),
        ],
        1,
    )
    slabs = [
        wgrad(tokens, dq), wgrad(tokens, dk), wgrad(tokens, dv), wgrad(attended, gb1),
        wgrad(first_low, dprobe), dwk, dwv, wgrad(mixed, gb2),
    ]
    ns = len(slabs)
    if own_rows:
        slab_shard, grad_projected = reduce_all(jnp.stack(slabs), dproj, patches, vec_block)
        extra_shard = slab_shard[ns + 1]
    else:
        grad_projected = lax.psum_scatter(dproj, "dp", scatter_dimension=0, tiled=True)
        dwp = lax.dot_general(patches, grad_projected, (((0, 1), (0, 1)), ((), ())), preferred_element_type=F32)
        dwp = dwp.reshape(shards, pr, width)
        pbg = jnp.sum(grad_projected.astype(F32), (0, 1))[None, None]
        vec_block = jnp.where(jnp.arange(vec_block.shape[1])[None, :, None] == 5, pbg, vec_block)
        slabs.append(dwp[:, :sr].reshape(slab).astype(BF))
        slab_shard = lax.psum_scatter(jnp.stack(slabs), AXES, scatter_dimension=1, tiled=True).astype(F32)
        extra_grad = jnp.concatenate([dwp[:, sr:], vec_block], 1).astype(BF)
        extra_shard = lax.psum_scatter(extra_grad, AXES, scatter_dimension=0, tiled=True)[0].astype(F32)
    patch_shard = jnp.concatenate([slab_shard[ns], extra_shard[:tails]], 0)
    patches_grad = lax.dot_general(
        grad_projected, patch_full, (((2,), (1,)), ((), ())), preferred_element_type=F32
    ).astype(BF)
    vg = lax.dynamic_slice(extra_shard, (tails, place * sr), (nv, sr))
    vg = [vg[j] for j in range(nv)]
    wbg = extra_shard[tails + nv, :wr]
    widen_shard = ffn_shard[:chunks].reshape(chunks, sr, shards, sr).transpose(1, 2, 0, 3).reshape(sr, hidden)
    narrow_shard = ffn_shard[chunks:].reshape(chunks * sr, width)
    return (
        output, tokens_grad, patches_grad,
        slab_shard[0], vg[0], slab_shard[1], slab_shard[2], vg[1], slab_shard[3], vg[2], vg[3], vg[4],
        patch_shard, vg[5], slab_shard[4], vg[6], slab_shard[5], slab_shard[6], vg[7], slab_shard[7],
        vg[8], vg[9], vg[10], widen_shard, wbg, narrow_shard, vg[11], vg[12], vg[13],
    )


def solution(mesh):
    three, two, one = P(AXES, None, None), P(AXES, None), P(AXES)
    in_specs = (
        three, three, two, one, one, three,
        two, one, two, two, one, two, one, one, one, two, one, two, one, two,
        two, one, two, one, one, one, two, one, two, one, one, one,
    )
    out_specs = (
        three, three, three,
        two, one, two, two, one, two, one, one, one, two, one, two, one, two, two, one, two,
        one, one, one, two, one, two, one, one, one,
    )
    return jax.shard_map(on_device, mesh=mesh, in_specs=in_specs, out_specs=out_specs, check_vma=False)
```

```python
import functools

import jax
import jax.numpy as jnp
from jax import lax
from jax.experimental import pallas as pl
from jax.experimental.pallas import tpu as pltpu
from jax.sharding import PartitionSpec as P

HEADS = 12
AXES = ("dp", "fsdp")
BF = jnp.bfloat16
F32 = jnp.float32
norm_eps = 1e-06
mask_fill = -1000000000.0

WINDOWS = ((0, 0), (128, 64), (384, 0), (512, 64))

ERFC_POLE = 0.3
ERFC_POLY = (
    0.16918935391840687,
    0.17069093065701252,
    0.14852123834149009,
    0.214181489197379,
    -0.09282620690981414,
    0.5449671942862269,
    -0.5097726086693966,
    0.4843018450108595,
    -0.12925324449453648,
)
INV_SQRT2 = 0.7071067811865476
INV_SQRT2PI = 0.3989422804014327


def nn(left, right):
    return lax.dot_general(left, right, (((1,), (0,)), ((), ())), preferred_element_type=F32)


def nt(left, right):
    return lax.dot_general(left, right, (((1,), (1,)), ((), ())), preferred_element_type=F32)


def tn(left, right):
    return lax.dot_general(left, right, (((0,), (0,)), ((), ())), preferred_element_type=F32)


def norm_parts(value):
    mean = jnp.mean(value, -1, keepdims=True)
    centred = value - mean
    spread = jnp.mean(centred * centred, -1, keepdims=True)
    inv = lax.rsqrt(spread + norm_eps)
    return centred * inv, inv


def norm_back(grad, gain, xhat, inv):
    scaled = grad * gain
    first = jnp.mean(scaled, -1, keepdims=True)
    second = jnp.mean(scaled * xhat, -1, keepdims=True)
    return inv * (scaled - first - xhat * second)


def gelu_parts(v):
    z = jnp.abs(v) * INV_SQRT2
    t = 1.0 / (1.0 + ERFC_POLE * z)
    poly = jnp.full_like(t, ERFC_POLY[-1])
    for c in ERFC_POLY[-2::-1]:
        poly = poly * t + c
    bell = jnp.exp(-0.5 * (v * v))
    half = (0.5 * bell) * (t * poly)
    cdf = jnp.where(v >= 0, 1.0 - half, half)
    return v * cdf, cdf + (v * INV_SQRT2PI) * bell


def window(full, index):
    base = WINDOWS[index][0]
    return full[:, base : base + 256]


def column_softmax(scores):
    e = jnp.exp(scores - jnp.max(scores, 0, keepdims=True))
    return (e * (1.0 / jnp.sum(e, 0, keepdims=True))).astype(BF)


def score_grads(probs, grads):
    p = probs.astype(F32)
    return (p * (grads - jnp.sum(grads * p, 0, keepdims=True))).astype(BF)


def stack_heads(full, index):
    base, off = WINDOWS[index]
    win = full[:, base : base + 256]
    lane = lax.broadcasted_iota(jnp.int32, win.shape, 1)
    blocks = []
    for h in range(3):
        lo = off + 64 * h
        blocks.append(jnp.where((lane >= lo) & (lane < lo + 64), win, 0.0))
    return jnp.concatenate(blocks, 0).astype(BF)


def unstack_heads(stacked, index, rows):
    _, off = WINDOWS[index]
    lane = lax.broadcasted_iota(jnp.int32, (rows, 256), 1)
    out = None
    for h in range(3):
        lo = off + 64 * h
        part = jnp.where((lane >= lo) & (lane < lo + 64), stacked[rows * h : rows * (h + 1)], 0.0)
        out = part if out is None else out + part
    return out


def join_windows(parts):
    a, b, c, d = parts
    return jnp.concatenate(
        [
            a[:, :128],
            a[:, 128:] + b[:, :128],
            b[:, 128:],
            c[:, :128],
            c[:, 128:] + d[:, :128],
            d[:, 128:],
        ],
        1,
    )


def self_block(x32, bias, mats, vecs, put, att_s):
    rb, length, width = x32.shape
    n = rb * length
    wq, wk, wv, wo, wc = mats
    qb, vb, ob, g1, b1, pb = vecs
    x32 = x32.reshape(n, width)
    x = x32.astype(BF)
    q_o, k_o, v_o, p_o = put("q"), put("k"), put("v"), put("p")
    q_o[...] = (nn(x, wq()) + qb).reshape(rb, length, width).astype(BF)
    k_o[...] = nn(x, wk()).reshape(rb, length, width).astype(BF)
    v_o[...] = (nn(x, wv()) + vb).reshape(rb, length, width).astype(BF)

    def row(r, carry):
        qr = q_o[r].astype(F32) * 0.125
        kr = k_o[r].astype(F32)
        vr = v_o[r].astype(F32)
        kws = [window(kr, i).astype(BF) for i in range(4)]
        vws = [window(vr, i).astype(BF) for i in range(4)]
        qss = [stack_heads(qr, i) for i in range(4)]
        mask = bias[r]
        scores = [nt(kws[i], qss[i]) + mask for i in range(4)]
        ps = [column_softmax(st) for st in scores]
        outs = [tn(ps[i], vws[i]) for i in range(4)]
        for i in range(4):
            p_o[r, i] = ps[i]
        att_s[r] = join_windows([unstack_heads(outs[i], i, length) for i in range(4)])
        return carry

    lax.fori_loop(0, rb, row, 0)
    att32 = att_s[...]
    put("att")[...] = att32.astype(BF)
    att = att32.reshape(n, width).astype(BF)
    u1 = x32 + nn(att, wo()) + ob
    put("u1")[...] = u1.reshape(rb, length, width)
    xhat, _ = norm_parts(u1)
    first32 = xhat * g1 + b1
    put("first")[...] = first32.reshape(rb, length, width).astype(BF)
    put("probe")[...] = (nn(first32.astype(BF), wc()) + pb).reshape(rb, length, width).astype(BF)


SELF_OUTS = ("q", "k", "v", "p", "att", "u1", "first", "probe")


def self_forward(
    tok, bias, wq, wk, wv, wo, wc, qb, vb, ob, g1, b1, pb, q_o, k_o, v_o, p_o, att_o, u1_o, f_o, pr_o, att_s
):
    outs = dict(zip(SELF_OUTS, (q_o, k_o, v_o, p_o, att_o, u1_o, f_o, pr_o)))
    mats = [lambda ref=ref: ref[...] for ref in (wq, wk, wv, wo, wc)]
    vecs = [ref[...] for ref in (qb, vb, ob, g1, b1, pb)]
    self_block(tok[...].astype(F32), bias, mats, vecs, lambda name: outs[name], att_s)


def cross_forward(starts, order, proj, wk, wv, cb, probe, k_o, v_o, p_o, mix_o, pr_s):
    i = pl.program_id(0)
    points = proj.shape[1]
    length = probe.shape[1]

    @pl.when(i == 0)
    def _():
        pr_s[...] = jnp.zeros_like(pr_s)

    lo, hi = starts[i], starts[i + 1]

    @pl.when(hi > lo)
    def _():
        pr_s[0:points, :] = proj[0]
        pr = pr_s[...]
        k_o[0] = nn(pr, wk[...]).astype(BF)
        v_o[0] = (nn(pr, wv[...]) + cb[...]).astype(BF)

        def row(j, carry):
            r = order[j]
            qr = probe[r].astype(F32) * 0.125
            qss = [stack_heads(qr, g) for g in range(4)]
            scores = [nt(k_o[0, :, WINDOWS[g][0] : WINDOWS[g][0] + 256], qss[g]) for g in range(4)]
            point = lax.broadcasted_iota(jnp.int32, scores[0].shape, 0)
            ps = [column_softmax(jnp.where(point < points, st, -1e30)) for st in scores]
            outs = [tn(ps[g], v_o[0, :, WINDOWS[g][0] : WINDOWS[g][0] + 256]) for g in range(4)]
            for g in range(4):
                p_o[r, g] = ps[g]
            mix_o[r] = join_windows([unstack_heads(outs[g], g, length) for g in range(4)]).astype(BF)
            return carry

        lax.fori_loop(lo, hi, row, 0)


def tail_kernel(
    u1, mix, og, wco, w1, w2, g1, b1, cb, g2, s2, wb, nb, g3, s3,
    out_o, act_o, gi_o, sec_o, gb3_o, gm_o, gb2_o, gc_o, vec_o, wbg_o,
    act_s, gp_s, acc_s,
):
    step = pl.program_id(0)
    rb, length, width = u1.shape
    n = rb * length
    chunks = w1.shape[0]

    @pl.when(step == 0)
    def _():
        vec_o[...] = jnp.zeros_like(vec_o)
        wbg_o[...] = jnp.zeros_like(wbg_o)

    def flat(ref):
        return ref[...].astype(F32).reshape(n, width)

    def fold(value):
        return value.reshape(rb, length, width)

    xhat1, _ = norm_parts(flat(u1))
    first = xhat1 * g1[...] + b1[...]
    u2 = first + nn(flat(mix).astype(BF), wco[...]) + cb[...]
    xhat2, inv2 = norm_parts(u2)
    second = (xhat2 * g2[...] + s2[...]).astype(BF)
    sec32 = second.astype(F32)
    sec_o[...] = fold(sec32).astype(BF)
    acc_s[...] = sec32 + nb[...]

    def up(c, carry):
        inner = nn(second, w1[c]) + wb[c]
        act, slope = gelu_parts(inner)
        act = act.astype(BF)
        gp_s[c] = slope
        act_o[c] = act
        acc_s[...] += nn(act, w2[c])
        return carry

    lax.fori_loop(0, chunks, up, 0)
    xhat3, inv3 = norm_parts(acc_s[...])
    out_o[...] = fold(xhat3 * g3[...] + s3[...]).astype(BF)
    y = flat(og)
    grad_summed = norm_back(y, g3[...], xhat3, inv3)
    gb3 = grad_summed.astype(BF)
    gb3f = gb3.astype(F32)
    gb3_o[...] = fold(gb3f).astype(BF)
    vec_o[0:1] += jnp.sum(y * xhat3, 0, keepdims=True)
    vec_o[1:2] += jnp.sum(y, 0, keepdims=True)
    vec_o[2:3] += jnp.sum(gb3f, 0, keepdims=True)
    acc_s[...] = grad_summed

    def down(c, carry):
        gi = (nt(gb3, w2[c]) * gp_s[c]).astype(BF)
        gi_o[c] = gi
        wbg_o[c] += jnp.sum(gi.astype(F32), 0, keepdims=True)
        acc_s[...] += nt(gi, w1[c])
        return carry

    lax.fori_loop(0, chunks, down, 0)
    y2 = acc_s[...].astype(BF).astype(F32)
    gm = norm_back(y2, g2[...], xhat2, inv2)
    gm_o[...] = fold(gm)
    gb2 = gm.astype(BF)
    gb2f = gb2.astype(F32)
    gb2_o[...] = fold(gb2f).astype(BF)
    vec_o[3:4] += jnp.sum(y2 * xhat2, 0, keepdims=True)
    vec_o[4:5] += jnp.sum(y2, 0, keepdims=True)
    vec_o[5:6] += jnp.sum(gb2f, 0, keepdims=True)
    gc_o[...] = fold(nt(gb2, wco[...])).astype(BF)


def cross_backward(
    starts, order, proj, keys, values, wk, wv, probe, grad, probs,
    dpr_o, dproj_o, dwk_o, dwv_o, dcb_o,
    pr_s, dk_s, dv_s, dwk_s, dwv_s,
):
    i = pl.program_id(0)
    points = proj.shape[1]
    length = probe.shape[1]

    @pl.when(i == 0)
    def _():
        pr_s[...] = jnp.zeros_like(pr_s)
        dwk_s[...] = jnp.zeros_like(dwk_s)
        dwv_s[...] = jnp.zeros_like(dwv_s)
        dcb_o[...] = jnp.zeros_like(dcb_o)

    lo, hi = starts[i], starts[i + 1]

    @pl.when(hi == lo)
    def _():
        dproj_o[...] = jnp.zeros_like(dproj_o)

    @pl.when(hi > lo)
    def _():
        dk_s[...] = jnp.zeros_like(dk_s)
        dv_s[...] = jnp.zeros_like(dv_s)

        def row(j, carry):
            r = order[j]
            qr = probe[r].astype(F32) * 0.125
            gr = grad[r].astype(F32)
            gss = [stack_heads(gr, g) for g in range(4)]
            dps = [nt(values[0, :, WINDOWS[g][0] : WINDOWS[g][0] + 256], gss[g]) for g in range(4)]
            qss = [stack_heads(qr, g) for g in range(4)]
            pbs = [probs[r, g] for g in range(4)]
            dvs = [nn(pbs[g], gss[g]) for g in range(4)]
            dss = [score_grads(pbs[g], dps[g]) for g in range(4)]
            dks = [nn(dss[g], qss[g]) for g in range(4)]
            outs = [tn(dss[g], keys[0, :, WINDOWS[g][0] : WINDOWS[g][0] + 256]) for g in range(4)]
            dv_s[...] += join_windows(dvs)
            dk_s[...] += join_windows(dks)
            dpr_o[r] = (join_windows([unstack_heads(outs[g], g, length) for g in range(4)]) * 0.125).astype(BF)
            return carry

        lax.fori_loop(lo, hi, row, 0)
        pr_s[0:points, :] = proj[0]
        pr = pr_s[...]
        dk = dk_s[...].astype(BF)
        dv = dv_s[...].astype(BF)
        dcb_o[0:1] += jnp.sum(dv.astype(F32), 0, keepdims=True)
        dproj = (nt(dk, wk[...]) + nt(dv, wv[...])).astype(BF)
        dproj_o[0] = dproj[0:points]
        dwk_s[...] += tn(pr, dk)
        dwv_s[...] += tn(pr, dv)

    @pl.when(i == pl.num_programs(0) - 1)
    def _():
        dwk_o[...] = dwk_s[...].astype(BF)
        dwv_o[...] = dwv_s[...].astype(BF)


def self_back_block(gm, dpr32, u1, heads, mats, g1, add, temps):
    q, k, v, probs = heads
    wq, wk, wv, wo, wc = mats
    ga_s, dq_s, dk_s, dv_s = temps
    rb, length, width = ga_s.shape
    n = rb * length
    grad_first = gm + nt(dpr32.astype(BF), wc())
    xhat, inv = norm_parts(u1)
    low = norm_back(grad_first, g1, xhat, inv)
    gb1 = low.astype(BF)
    add(3, grad_first * xhat)
    add(4, grad_first)
    add(2, gb1.astype(F32))
    add(6, dpr32)
    ga_s[...] = nt(gb1, wo()).astype(BF).astype(F32).reshape(rb, length, width)

    def row(r, carry):
        qr = q[r].astype(F32) * 0.125
        kr = k[r].astype(F32)
        vr = v[r].astype(F32)
        gr = ga_s[r]
        gss = [stack_heads(gr, i) for i in range(4)]
        vws = [window(vr, i).astype(BF) for i in range(4)]
        dps = [nt(vws[i], gss[i]) for i in range(4)]
        qss = [stack_heads(qr, i) for i in range(4)]
        kws = [window(kr, i).astype(BF) for i in range(4)]
        pbs = [probs[r, i] for i in range(4)]
        dvs = [nn(pbs[i], gss[i]) for i in range(4)]
        dss = [score_grads(pbs[i], dps[i]) for i in range(4)]
        dks = [nn(dss[i], qss[i]) for i in range(4)]
        outs = [tn(dss[i], kws[i]) for i in range(4)]
        dq_s[r] = join_windows([unstack_heads(outs[i], i, length) for i in range(4)]) * 0.125
        dk_s[r] = join_windows(dks)
        dv_s[r] = join_windows(dvs)
        return carry

    lax.fori_loop(0, rb, row, 0)
    dq = dq_s[...].reshape(n, width).astype(BF)
    dk = dk_s[...].reshape(n, width).astype(BF)
    dv = dv_s[...].reshape(n, width).astype(BF)
    add(0, dq.astype(F32))
    add(1, dv.astype(F32))
    total = low + nt(dq, wq()) + nt(dk, wk()) + nt(dv, wv())
    return gb1, dq, dk, dv, total.reshape(rb, length, width).astype(BF)


def self_backward(
    gm, dpr, u1, q, k, v, probs, wq, wk, wv, wo, wc, g1, gb1_o, dq_o, dk_o, dv_o, tg_o, vec_o, *temps
):
    rb, length, width = u1.shape
    n = rb * length

    @pl.when(pl.program_id(0) == 0)
    def _():
        vec_o[...] = jnp.zeros_like(vec_o)

    def add(row, value):
        vec_o[row : row + 1] += jnp.sum(value, 0, keepdims=True)

    def flat(ref):
        return ref[...].astype(F32).reshape(n, width)

    mats = [lambda ref=ref: ref[...] for ref in (wq, wk, wv, wo, wc)]
    *grads, tokens_grad = self_back_block(
        flat(gm), flat(dpr), flat(u1), (q, k, v, probs), mats, g1[...], add, temps
    )
    for ref, value in zip((gb1_o, dq_o, dk_o, dv_o), grads):
        ref[...] = value.astype(F32).reshape(rb, length, width).astype(BF)
    tg_o[...] = tokens_grad


def sds(shape, dtype):
    return jax.ShapeDtypeStruct(shape, dtype)


def whole(shape, *, single=True):
    zeros = (0,) * len(shape)
    mode = pl.Buffered(1) if single else None
    return pl.BlockSpec(shape, lambda i, *_: zeros, pipeline_mode=mode)


def rows_block(shape, rb):
    rest = tuple(shape[1:])
    return pl.BlockSpec((rb,) + rest, lambda i, *_: (i,) + (0,) * len(rest))


def params(mib):
    return pltpu.CompilerParams(
        dimension_semantics=("arbitrary",), vmem_limit_bytes=mib * 1024 * 1024
    )


def cost(flops, bytes_accessed):
    return pl.CostEstimate(flops=int(flops), bytes_accessed=int(bytes_accessed), transcendentals=0)


def my_place():
    dp, fs = lax.axis_index("dp"), lax.axis_index("fsdp")
    return dp // 2, dp % 2, fs // 2, fs % 2


def device_at(z, y, x, c):
    return (z * 2 + y, x * 2 + c)


def meet(z, y, x, c):
    sem = pltpu.get_barrier_semaphore()
    others = [device_at((z + k) % 4, y, x, c) for k in (1, 2, 3)]
    others += [device_at(z, 1 - y, x, c), device_at(z, y, 1 - x, c), device_at(z, y, x, 1 - c)]
    for other in others:
        pl.semaphore_signal(sem, inc=1, device_id=other, device_id_type=pl.DeviceIdType.MESH)
    pl.semaphore_wait(sem, len(others))


class Copies:
    def __init__(self, send, recv, local):
        self.send, self.recv, self.local = send, recv, local
        self.far = self.near = 0
        self.sent = []

    def prepare(self, src, dst, device):
        i = self.far
        self.far += 1
        return pltpu.make_async_remote_copy(
            src_ref=src, dst_ref=dst, send_sem=self.send.at[i], recv_sem=self.recv.at[i],
            device_id=device, device_id_type=pl.DeviceIdType.MESH,
        )

    def remote(self, src, dst, device):
        copy = self.prepare(src, dst, device)
        copy.start()
        return copy

    def here(self, src, dst):
        i = self.near
        self.near += 1
        copy = pltpu.make_async_copy(src, dst, self.local.at[i])
        copy.start()
        return copy


def arrived(copies):
    for copy in copies:
        copy.wait()


def drive(jobs, order):
    for name in order:
        next(jobs[name], None)
    for job in jobs.values():
        for _ in job:
            pass


PATCH, EXTRA, QUERY, KEY, VALUE, OUT, CQ, CK, W1 = range(9)
CV, CO = 12, 13


FRONT_ORDER = (
    "P", "Q", "P", "P", "Q", "P", "Q", "R", "P", "P", "P", "F", "Q", "P", "Q", "Q", "F", "P",
    "weights", "F", "i0", "i1", "Q", "F", "i0", "i3", "G", "F", "R", "i1", "i3", "Q", "G", "G",
    "i0", "i0", "F", "Q", "self", "i2", "i3", "G", "self", "R", "i2", "F", "G", "self", "i3", "i1",
    "G", "self", "G", "R", "R", "i1", "F", "i2", "self", "R", "R", "G", "i2", "R",
)
BACK_ORDER = (
    "p2", "S", "E", "E", "p0", "p2", "p1", "S", "p0", "S", "p1", "p3", "S", "S", "D1", "D2", "L2",
    "E", "L2", "p3", "L1", "L1", "L2", "p2", "p0", "L1", "p1", "E", "p3", "V1", "V1", "V2", "L2",
    "E", "V2", "L1", "V1", "V1", "V2", "V2", "L2", "V1", "L1", "V2",
)


def front_kernel(
    parts, tails, nv, rb, w_in, n_in, pat, tok, bias, w_out, n_out, p_out, q_o, k_o, v_o, pr_o, att_o, u1_o, f_o, prb_o, vec_o,
    pw, ex, wm, proj_s, q_s, k_s, v_s, pr_s, att_b, u1_s, f_s, prb_s, att_s, send, recv, local,
):
    z, y, x, c = my_place()
    meet(z, y, x, c)
    copies = Copies(send, recv, local)
    rows, length, width = tok.shape
    images = pat.shape[0]

    inner = (z + 1) % 4 >= 2
    partner = z + 1 - 2 * (z % 2)
    across = 3 - z
    ours, theirs = 2 * (z // 2), 2 - 2 * (z // 2)

    def along_z(source, view, tell, local):
        step = copies.remote(source, view(z, 0), device_at(partner, y, x, c))
        tell("own")
        yield
        step.wait()
        if local is not None:
            local.wait()
        tell("partner")
        middle = copies.prepare(view(ours, 2), view(ours, 2), device_at(across, y, x, c))
        outward = copies.prepare(view(theirs, 2), view(theirs, 2), device_at(partner, y, x, c))

        @pl.when(inner)
        def _():
            middle.start()

        yield

        @pl.when(inner)
        def _():
            middle.wait()
            outward.start()
            tell("inner")

        yield

        @pl.when(jnp.logical_not(inner))
        def _():
            outward.wait_recv()
            tell("outer")

        copies.sent.append((inner, outward))
        yield

    def exchanged(source, view, local):
        own = copies.prepare(source, view(z, 0), device_at(z, 1 - y, x, c))
        second = copies.prepare(view(partner, 0), view(partner, 0), device_at(z, 1 - y, x, c))
        third = copies.prepare(view(theirs, 2), view(theirs, 2), device_at(z, 1 - y, x, c))
        start = {"own": own, "partner": second, "inner": third, "outer": third}
        return along_z(source, view, lambda which: start[which].start(), local), (own, second, third)

    def slabs(source, out):
        every = slice(None)

        def view(at, many):
            return out(pl.ds(at, many) if many else at, y, x, c)

        def plane(at, many):
            return out(pl.ds(at, many) if many else at, every, x, c)

        local = copies.here(source, view(z, 0))
        moving, (own, second, third) = exchanged(source, view, None)
        next(moving)
        yield
        own.wait()
        local.wait()
        steps = [copies.remote(plane(z, 0), plane(z, 0), device_at(z, y, 1 - x, c))]
        yield
        for _ in range(3):
            next(moving)
            yield
        second.wait()
        steps.append(copies.remote(plane(partner, 0), plane(partner, 0), device_at(z, y, 1 - x, c)))
        yield
        third.wait()
        steps.append(copies.remote(plane(theirs, 2), plane(theirs, 2), device_at(z, y, 1 - x, c)))
        yield
        arrived(steps)
        half = out(every, every, every, c)
        step = copies.remote(half, half, device_at(z, y, x, 1 - c))
        yield
        step.wait()

    def patch_weights():
        rest = pw.shape[4] - tails
        arrived(
            [
                copies.here(w_out.at[PATCH], pw.at[:, :, :, :, 0:rest]),
                copies.here(w_out.at[EXTRA, :, :, :, :, 0:tails], pw.at[:, :, :, :, rest:]),
                copies.here(w_out.at[EXTRA], ex),
            ]
        )
        total = jnp.zeros(ex.shape[4:], F32)
        for zz in range(4):
            for yy in range(2):
                for xx in range(2):
                    for cc in range(2):
                        total = total + ex[zz, yy, xx, cc].astype(F32)
        vec_o[...] = total
        yield

    def vec(j):
        return vec_o[tails + j : tails + j + 1, :]

    def image(i):
        full = pw[...].reshape(pat.shape[2], width)
        proj_s[i] = (nn(pat[i], full) + vec(5)).astype(BF)

        def view(at, many):
            return p_out.at[pl.ds(at, many) if many else at, y, i]

        moving, steps = exchanged(proj_s.at[i], view, copies.here(proj_s.at[i], view(z, 0)))
        yield from moving
        arrived(steps)

    def attention():
        arrived([copies.here(w_out.at[QUERY + m], wm.at[m]) for m in range(5)])
        yield
        scratch = dict(zip(SELF_OUTS, (q_s, k_s, v_s, pr_s, att_b, u1_s, f_s, prb_s)))
        finals = dict(zip(SELF_OUTS, (q_o, k_o, v_o, pr_o, att_o, u1_o, f_o, prb_o)))
        mats = [lambda m=m: wm[m].reshape(width, width) for m in range(5)]
        outgoing = []
        for b in range(rows // rb):
            pick = pl.ds(b * rb, rb)
            self_block(
                tok[pick].astype(F32), bias.at[pick], mats, [vec(j) for j in (0, 1, 2, 3, 4, 6)],
                lambda name: scratch[name].at[pick], att_s,
            )
            outgoing += [copies.here(scratch[name].at[pick], finals[name].at[pick]) for name in SELF_OUTS]
            yield
        arrived(outgoing)

    def stacked(lo, n):
        pick = pl.ds(lo, n)
        return slabs(w_in.at[pick], lambda *at: w_out.at[(pick,) + at])

    jobs = {name: stacked(lo, n) for name, (lo, n) in parts.items()}
    jobs["G"] = slabs(n_in, lambda *at: n_out.at[at])
    jobs["weights"] = patch_weights()
    for i in range(images):
        jobs["i%d" % i] = image(i)
    jobs["self"] = attention()
    drive(jobs, FRONT_ORDER)
    for when, copy in copies.sent:

        @pl.when(when)
        def _(copy=copy):
            copy.wait_send()


def back_kernel(
    rb, tails, w_in, p_in, gm, dpr, u1, q, k, v, probs, tok, att, w_all, pat, g1, vt_in, wb_in,
    w_out, p_out, tg_o,
    wm, gm_s, dpr_s, u1_s, q_s, k_s, v_s, p_s, ga_t, dq_t, dk_t, dv_t, gb1_f, dq_f, dk_f, dv_f, tg_s, vec_s,
    acc, lw, pv, rc, rx, ry, rz, pacc, pry, prz, send, recv, local,
):
    z, y, x, c = my_place()
    meet(z, y, x, c)
    copies = Copies(send, recv, local)
    rows, length, width = gm.shape
    images = pat.shape[0]
    sr = w_out.shape[1]

    def up(ref, *at):
        return ref[at].astype(F32)

    def slabs(lo, n, sibling, own, base, own_c):
        pick = pl.ds(lo, n)
        last = (c,) if own_c else ()

        def cell(s, zz, yy, xx):
            return (s - base, zz, yy, xx) + last

        def view(zz, yy, xx):
            return own.at[(pl.ds(lo - base, n), zz, yy, xx) + last]

        every = slice(None)
        step = copies.remote(sibling, rc.at[pick], device_at(z, y, x, 1 - c))
        yield
        step.wait()

        def add_x(i, carry):
            s, zz = lo + i // 4, i % 4
            for yy in range(2):
                at = cell(s, zz, yy, 1 - x)
                own[at] = (up(own, *at) + up(rc, s, zz, yy, 1 - x)).astype(BF)
            return carry

        lax.fori_loop(0, 4 * n, add_x, 0)
        step = copies.remote(view(every, every, 1 - x), rx.at[pick], device_at(z, y, 1 - x, c))
        yield
        step.wait()

        def add_y(i, carry):
            s, zz = lo + i // 4, i % 4
            at = cell(s, zz, 1 - y, x)
            own[at] = (up(own, *at) + up(rc, s, zz, 1 - y, x) + up(rx, s, zz, 1 - y)).astype(BF)
            return carry

        lax.fori_loop(0, 4 * n, add_y, 0)
        step = copies.remote(view(every, 1 - y, x), ry.at[pick], device_at(z, 1 - y, x, c))
        yield
        step.wait()
        steps = []
        for hop in (1, 3, 2):
            zz = (z + hop) % 4

            def add_z(i, carry):
                s = lo + i
                at = cell(s, zz, y, x)
                own[at] = (up(own, *at) + up(rc, s, zz, y, x) + up(rx, s, zz, y) + up(ry, s, zz)).astype(BF)
                return carry

            lax.fori_loop(0, n, add_z, 0)
            steps.append(copies.remote(view(zz, y, x), rz.at[hop - 1, pick], device_at(zz, y, x, c)))
        yield
        arrived(steps)

        def add_last(i, carry):
            s = lo + i
            w_out[s] = (
                up(own, *cell(s, z, y, x)) + up(rc, s, z, y, x) + up(rx, s, z, y) + up(ry, s, z)
                + up(rz, 0, s) + up(rz, 1, s) + up(rz, 2, s)
            )
            return carry

        lax.fori_loop(0, n, add_last, 0)
        yield

    def early():
        own = copies.here(w_in.at[:, :, :, :, c], acc)
        job = slabs(4, 3, w_in.at[:, :, :, :, 1 - c], acc, 4, False)
        next(job)
        yield
        own.wait()
        yield from job

    def image(i):
        own = copies.here(p_in.at[:, y, i], pacc.at[i])
        step = copies.remote(p_in.at[:, 1 - y, i], pry.at[i], device_at(z, 1 - y, x, c))
        yield
        own.wait()
        step.wait()
        steps = []
        for hop in (1, 3, 2):
            zz = (z + hop) % 4
            pacc[i, zz] = (up(pacc, i, zz) + up(pry, i, zz)).astype(BF)
            steps.append(copies.remote(pacc.at[i, zz], prz.at[hop - 1, i], device_at(zz, y, x, c)))
        yield
        arrived(steps)
        p_out[i] = (
            up(pacc, i, z) + up(pry, i, z) + up(prz, 0, i) + up(prz, 1, i) + up(prz, 2, i)
        ).astype(BF)
        yield

    def attention():
        weights = [
            copies.here(w_all.at[m], wm.at[pl.ds(width * at, width)])
            for at, m in enumerate((QUERY, KEY, VALUE, OUT, CQ))
        ]
        vec_s[...] = vt_in[...]
        mats = [lambda at=at: wm[pl.ds(width * at, width)] for at in range(5)]
        streams = ((gm, gm_s), (dpr, dpr_s), (u1, u1_s), (q, q_s), (k, k_s), (v, v_s), (probs, p_s))
        size = gm_s.shape[0]
        n = rb * length

        def add(row, value):
            vec_s[row : row + 1] += jnp.sum(value, 0, keepdims=True)

        leaving = None
        for stage in range(rows // size):
            coming = [copies.here(src.at[pl.ds(stage * size, size)], dst) for src, dst in streams]
            arrived(weights + coming)
            weights = []
            if leaving is not None:
                leaving.wait()

            def block(b, carry):
                pick = pl.ds(b * rb, rb)

                def flat(ref):
                    return ref[pick].astype(F32).reshape(n, width)

                heads = tuple(ref.at[pick] for ref in (q_s, k_s, v_s, p_s))
                *grads, tokens_grad = self_back_block(
                    flat(gm_s), flat(dpr_s), flat(u1_s), heads, mats, g1[...], add, (ga_t, dq_t, dk_t, dv_t)
                )
                at = pl.ds(pl.multiple_of(stage * size * length + b * n, n), n)
                for ref, value in zip((gb1_f, dq_f, dk_f, dv_f), grads):
                    ref[at] = value
                tg_s[pick] = tokens_grad
                return carry

            lax.fori_loop(0, size // rb, block, 0)
            leaving = copies.here(tg_s, tg_o.at[pl.ds(stage * size, size)])
            yield
        leaving.wait()
        count = rows * length
        arrived(
            [
                copies.here(tok, wm.at[pl.ds(0, count)]),
                copies.here(att, wm.at[pl.ds(count, count)]),
            ]
        )
        yield

    def gradient(pairs):
        count = rows * length
        for m, first, right in pairs:
            left = wm[pl.ds(first * count, count)]
            lw[m] = tn(left, right[...]).reshape(lw.shape[1:]).astype(BF)
        yield

    def late(lo):
        yield from slabs(lo, 2, lw.at[pl.ds(lo, 2), :, :, :, 1 - c], lw, 0, True)

    def patch_sums(first):
        pwidth = pat.shape[2]
        rows_each = pwidth // 32
        step = 128
        bias = jnp.sum(p_out[0].astype(F32), 0, keepdims=True)
        for i in range(1, images):
            bias = bias + jnp.sum(p_out[i].astype(F32), 0, keepdims=True)
        vec_s[5:6] = bias

        for lo in range(0, pwidth, step):
            total = tn(pat[0, :, lo : lo + step], p_out[0])
            for i in range(1, images):
                total = total + tn(pat[i, :, lo : lo + step], p_out[i])
            for at in range(step // rows_each):
                d = lo // rows_each + at
                zz, yy, xx, cc = d // 8, (d // 4) % 2, (d // 2) % 2, d % 2
                part = total[at * rows_each : (at + 1) * rows_each]
                pv[0, zz, yy, xx, cc] = part[:sr].astype(BF)
                vecs = vec_s[...]
                row = lax.broadcasted_iota(jnp.int32, vecs.shape, 0)
                vecs = jnp.where(row == vecs.shape[0] - 2, wb_in[d : d + 1], vecs)
                pv[1, zz, yy, xx, cc] = jnp.concatenate([part[sr:], vecs], 0).astype(BF)

        yield from slabs(first, 1, pv.at[pl.ds(0, 1), :, :, :, 1 - c], pv, first, True)

    def second_patch(first):
        yield from slabs(first, 1, pv.at[pl.ds(1, 1), :, :, :, 1 - c], pv, first - 1, True)

    jobs = {"p%d" % i: image(i) for i in range(images)}
    jobs["E"] = early()
    jobs["S"] = attention()
    jobs["D1"] = gradient(((0, 0, dq_f), (1, 0, dk_f)))
    jobs["D2"] = gradient(((2, 0, dv_f), (3, 1, gb1_f)))
    jobs["L1"], jobs["L2"] = late(0), late(2)
    jobs["V1"], jobs["V2"] = patch_sums(7), second_patch(8)
    drive(jobs, BACK_ORDER)


def front(slabs, narrow, patches, tokens, bias, tails, nv):
    n, sr, width = slabs.shape
    images, points, pwidth = patches.shape
    rows, length, _ = tokens.shape
    rb = 8 if rows % 8 == 0 else 1
    parts = {"P": (PATCH, 2), "Q": (QUERY, 6), "F": (W1, 4), "R": (CV, 2)}
    nr = narrow.shape[0]
    remote = 10 * (len(parts) + 1) + 6 * images
    near = len(parts) + 1 + images + 3 + 5 + len(SELF_OUTS) * (rows // rb)
    tok_sh = (rows, length, width)
    probs = (rows, 4, length, 3 * length)
    kept = [sds(tok_sh, BF), sds(tok_sh, BF), sds(tok_sh, BF), sds(probs, BF), sds(tok_sh, BF), sds(tok_sh, F32), sds(tok_sh, BF), sds(tok_sh, BF)]
    hbm = pl.BlockSpec(memory_space=pl.ANY)
    vmem = pl.BlockSpec(memory_space=pltpu.VMEM)
    w_all, n_all, p_all, *rest = pl.pallas_call(
        functools.partial(front_kernel, parts, tails, nv, rb),
        in_specs=[hbm, hbm, vmem, vmem, vmem],
        out_specs=[hbm] * 11 + [vmem],
        out_shape=[
            sds((n, 4, 2, 2, 2, sr, width), BF), sds((4, 2, 2, 2, nr, width), BF),
            sds((4, 2, images, points, width), BF), *kept, sds((sr, width), F32),
        ],
        scratch_shapes=[
            pltpu.VMEM((4, 2, 2, 2, pwidth // 32, width), BF),
            pltpu.VMEM((4, 2, 2, 2, sr, width), BF),
            pltpu.VMEM((5, 4, 2, 2, 2, sr, width), BF),
            pltpu.VMEM((images, points, width), BF),
            *[pltpu.VMEM(item.shape, item.dtype) for item in kept],
            pltpu.VMEM((rb, length, width), F32),
            pltpu.SemaphoreType.DMA((remote,)),
            pltpu.SemaphoreType.DMA((remote,)),
            pltpu.SemaphoreType.DMA((near,)),
        ],
        compiler_params=pltpu.CompilerParams(
            collective_id=0, has_side_effects=True, vmem_limit_bytes=58 * 1024 * 1024
        ),
        name="front",
    )(slabs, narrow, patches, tokens, bias)
    return w_all.reshape(n, 32 * sr, width), n_all.reshape(32 * nr, width), p_all.reshape(8 * images, points, width), rest[:8], rest[8]


def back(slabs, grads, streams, tok, att, w_all, patches, g1, vecs, wb_rows, tails):
    n, full, width = slabs.shape
    sr = full // 32
    total, points, _ = grads.shape
    images, _, pwidth = patches.shape
    rows, length, _ = streams[0].shape
    m = n + 6
    size, rb = 8, 4
    hbm = pl.BlockSpec(memory_space=pl.ANY)
    vmem = pl.BlockSpec(memory_space=pltpu.VMEM)
    remote = 6 * 5 + 4 * images
    near = 1 + images + 5 + 8 * (rows // size) + 2
    part = (sr, width)
    w_shard, p_shard, tokens_grad = pl.pallas_call(
        functools.partial(back_kernel, rb, tails),
        in_specs=[hbm] * 12 + [vmem] * 4,
        out_specs=[vmem, vmem, hbm],
        out_shape=[sds((m, sr, width), F32), sds((images, points, width), BF), sds((rows, length, width), BF)],
        scratch_shapes=[
            pltpu.VMEM((5 * width, width), BF),
            *[pltpu.VMEM((size,) + item.shape[1:], item.dtype) for item in streams],
            *[pltpu.VMEM((rb, length, width), F32)] * 4,
            *[pltpu.VMEM((rows * length, width), BF)] * 4,
            pltpu.VMEM((size, length, width), BF),
            pltpu.VMEM(vecs.shape, F32),
            pltpu.VMEM((n, 4, 2, 2) + part, BF),
            pltpu.VMEM((4, 4, 2, 2, 2) + part, BF),
            pltpu.VMEM((2, 4, 2, 2, 2) + part, BF),
            pltpu.VMEM((m, 4, 2, 2) + part, BF),
            pltpu.VMEM((m, 4, 2) + part, BF),
            pltpu.VMEM((m, 4) + part, BF),
            pltpu.VMEM((3, m) + part, BF),
            pltpu.VMEM((images, 4, points, width), BF),
            pltpu.VMEM((images, 4, points, width), BF),
            pltpu.VMEM((3, images, points, width), BF),
            pltpu.SemaphoreType.DMA((remote,)),
            pltpu.SemaphoreType.DMA((remote,)),
            pltpu.SemaphoreType.DMA((near,)),
        ],
        compiler_params=pltpu.CompilerParams(
            collective_id=1, has_side_effects=True, vmem_limit_bytes=62 * 1024 * 1024
        ),
        name="back",
    )(
        slabs.reshape(n, 4, 2, 2, 2, sr, width), grads.reshape(4, 2, images, points, width), *streams,
        tok, att, w_all, patches, g1, vecs, wb_rows,
    )
    return w_shard, p_shard, tokens_grad


def gather(value, axis):
    return lax.all_gather(value, AXES, axis=axis, tiled=True)


def on_device(
    tokens, patches, segments, owner, image_slot, out_grad,
    self_query, query_bias, self_key, self_value, value_bias, self_output, output_bias,
    first_gain, first_norm_bias, patch_proj, patch_bias, cross_query, probe_bias, cross_key,
    cross_value, content_bias, cross_output, cross_bias, second_gain, second_shift,
    widen_weight, widen_bias, narrow_weight, narrow_bias, third_gain, third_shift,
):
    rows, length, width = tokens.shape
    images, points, pwidth = patches.shape
    groups = lax.axis_size("dp")
    shards = groups * lax.axis_size("fsdp")
    total_images = groups * images
    hidden = widen_weight.shape[1]
    chunks = hidden // width
    sr = self_query.shape[0]
    wr = widen_bias.shape[0]

    place = lax.axis_index("dp") * lax.axis_size("fsdp") + lax.axis_index("fsdp")
    vec_list = (
        query_bias, value_bias, output_bias, first_gain, first_norm_bias, patch_bias, probe_bias,
        content_bias, cross_bias, second_gain, second_shift, narrow_bias, third_gain, third_shift,
    )
    nv = len(vec_list)
    pr = patch_proj.shape[0]
    tails = pr - sr
    lane_block = jnp.arange(width, dtype=jnp.int32)[None, :] // sr
    vec_rows = jnp.where(lane_block == place, jnp.tile(jnp.stack(vec_list), (1, shards)), jnp.zeros((), BF))
    wb_row = jnp.pad(widen_bias, (0, width - wr))[None]
    extra = jnp.concatenate([patch_proj[sr:], vec_rows, wb_row], 0)
    er = max(sr, extra.shape[0])
    own_rows = er == sr and groups == 8 and shards == 32
    extra = jnp.pad(extra, ((0, er - extra.shape[0]), (0, 0)))
    slabs_in = jnp.stack(
        [
            patch_proj[:sr], extra[:sr], self_query, self_key, self_value, self_output, cross_query, cross_key,
            *[widen_weight[:, width * at : width * (at + 1)] for at in range(chunks)],
            cross_value, cross_output,
        ]
    )

    image = owner * images + image_slot
    idx = jnp.arange(rows, dtype=jnp.int32)
    before = (image[None, :] < image[:, None]) | ((image[None, :] == image[:, None]) & (idx[None, :] < idx[:, None]))
    rank = jnp.sum(before.astype(jnp.int32), 1)
    order = jnp.sum(jnp.where(rank[:, None] == idx[None, :], idx[:, None], 0), 0).astype(jnp.int32)
    starts = jnp.sum((image[None, :] < jnp.arange(total_images + 1, dtype=jnp.int32)[:, None]).astype(jnp.int32), 1)

    same = segments[:, :, None] == segments[:, None, :]
    bias = jnp.where(same, 0.0, mask_fill).astype(F32)
    bias = jnp.concatenate([bias, bias, bias], 2)

    rb = 8 if rows % 8 == 0 else 1
    grid = (rows // rb,)
    tok_sh = (rows, length, width)
    slab = (width, width)

    def wspec(j):
        return pl.BlockSpec((None, width, width), lambda i, *_: (j, 0, 0), pipeline_mode=pl.Buffered(1))

    vspec = whole((1, width))
    tb = rows_block(tok_sh, rb)
    self_p = (rows, 4, length, 3 * length)
    if own_rows:
        w_a, narrow_all, proj_all, kept, vec_all = front(
            slabs_in, narrow_weight, patches, tokens, bias, tails, nv
        )
        vec_all = vec_all[tails : tails + nv]
        extra_all = w_a[EXTRA].reshape(shards, er, width)
    else:
        w_a = gather(slabs_in, 1)
        narrow_all = gather(narrow_weight, 0)
        extra_all = gather(extra, 0).reshape(shards, er, width)
        vec_all = jnp.sum(extra_all[:, tails : tails + nv].astype(F32), 0)
    (qb, vb, ob, g1, b1, pab, prb, cob, crb, g2, s2, nab, g3, s3) = [vec_all[j : j + 1] for j in range(nv)]
    wb = extra_all[:, tails + nv, :wr].astype(F32).reshape(chunks, 1, width)
    narrow_all = narrow_all.reshape(chunks, width, width)
    patch_full = jnp.concatenate([w_a[PATCH].reshape(shards, sr, width), extra_all[:, :tails]], 1)
    patch_full = patch_full.reshape(shards * pr, width)
    if not own_rows:
        projected = lax.dot_general(patches, patch_full, (((2,), (0,)), ((), ())), preferred_element_type=F32)
        proj_all = lax.all_gather((projected + pab).astype(BF), "dp", axis=0, tiled=True)
        kept = pl.pallas_call(
            self_forward,
            grid=grid,
            in_specs=[tb, rows_block((rows, length, 3 * length), rb)]
            + [wspec(j) for j in (QUERY, KEY, VALUE, OUT, CQ)]
            + [vspec] * 6,
            out_specs=[tb, tb, tb, rows_block(self_p, rb), tb, tb, tb, tb],
            out_shape=[
                sds(tok_sh, BF), sds(tok_sh, BF), sds(tok_sh, BF), sds(self_p, BF),
                sds(tok_sh, BF), sds(tok_sh, F32), sds(tok_sh, BF), sds(tok_sh, BF),
            ],
            scratch_shapes=[pltpu.VMEM((rb, length, width), F32)],
            compiler_params=params(48),
            cost_estimate=cost(11 * rows * length * width * width, 30e6),
            name="self_forward",
        )(tokens, bias, w_a, w_a, w_a, w_a, w_a, qb, vb, ob, g1, b1, prb)
    q, k, v, probs, attended, u1, first_low, probe = kept

    padded = -(-points // 16) * 16
    kv_sh = (total_images, padded, width)
    cross_p = (rows, 4, padded, 3 * length)
    img_spec = pl.BlockSpec((1, points, width), lambda i, *_: (i, 0, 0))
    kv_spec = pl.BlockSpec((1, padded, width), lambda i, *_: (i, 0, 0))
    image_keys, image_values, cprobs, mixed = pl.pallas_call(
        cross_forward,
        grid_spec=pltpu.PrefetchScalarGridSpec(
            num_scalar_prefetch=2,
            grid=(total_images,),
            in_specs=[img_spec, wspec(CK), wspec(CV), vspec, whole(tok_sh)],
            out_specs=[kv_spec, kv_spec, whole(cross_p), whole(tok_sh)],
            scratch_shapes=[pltpu.VMEM((padded, width), BF)],
        ),
        out_shape=[sds(kv_sh, BF), sds(kv_sh, BF), sds(cross_p, BF), sds(tok_sh, BF)],
        compiler_params=params(48),
        cost_estimate=cost(4 * total_images * points * width * width, 40e6),
        name="cross_forward",
    )(starts, order, proj_all, w_a, w_a, cob, probe)

    w1_spec = pl.BlockSpec(
        (chunks, width, width), lambda i, *_: (W1 // chunks, 0, 0), pipeline_mode=pl.Buffered(1)
    )
    n_tok = rows * length
    hid_sh = (chunks, n_tok, width)
    hid_spec = pl.BlockSpec((chunks, rb * length, width), lambda i, *_: (0, i, 0))
    (output, active, grad_inner, second, gb3, grad_mid, gb2, grad_crossed, vec_t, wb_grad) = pl.pallas_call(
        tail_kernel,
        grid=grid,
        in_specs=[tb, tb, tb, wspec(CO), w1_spec, whole((chunks, width, width))]
        + [vspec] * 5
        + [whole((chunks, 1, width))]
        + [vspec] * 3,
        out_specs=[tb, hid_spec, hid_spec, tb, tb, tb, tb, tb, whole((8, width)), whole((chunks, 1, width))],
        out_shape=[
            sds(tok_sh, BF), sds(hid_sh, BF), sds(hid_sh, BF), sds(tok_sh, BF), sds(tok_sh, BF),
            sds(tok_sh, F32), sds(tok_sh, BF), sds(tok_sh, BF), sds((8, width), F32), sds((chunks, 1, width), F32),
        ],
        scratch_shapes=[
            pltpu.VMEM((8, 128), BF),
            pltpu.VMEM((chunks, rb * length, width), F32),
            pltpu.VMEM((rb * length, width), F32),
        ],
        compiler_params=params(56),
        cost_estimate=cost(18 * n_tok * width * width + 8 * n_tok * width * hidden, 50e6),
        name="tail",
    )(u1, mixed, out_grad, w_a, w_a, narrow_all, g1, b1, crb, g2, s2, wb, nab, g3, s3)

    dprobe, dproj, dwk, dwv, dcb = pl.pallas_call(
        cross_backward,
        grid_spec=pltpu.PrefetchScalarGridSpec(
            num_scalar_prefetch=2,
            grid=(total_images,),
            in_specs=[img_spec, kv_spec, kv_spec, wspec(CK), wspec(CV), whole(tok_sh), whole(tok_sh), whole(cross_p)],
            out_specs=[whole(tok_sh), img_spec, whole(slab), whole(slab), whole((8, width))],
            scratch_shapes=[
                pltpu.VMEM((padded, width), BF),
                pltpu.VMEM((padded, width), F32),
                pltpu.VMEM((padded, width), F32),
                pltpu.VMEM((width, width), F32),
                pltpu.VMEM((width, width), F32),
            ],
        ),
        out_shape=[sds(tok_sh, BF), sds((total_images, points, width), BF), sds(slab, BF), sds(slab, BF), sds((8, width), F32)],
        compiler_params=params(56),
        cost_estimate=cost(8 * total_images * points * width * width, 50e6),
        name="cross_backward",
    )(starts, order, proj_all, image_keys, image_values, w_a, w_a, probe, grad_crossed, cprobs)

    def wgrad(left, right):
        return tn(left.reshape(n_tok, width), right.reshape(n_tok, width)).astype(BF)

    ffn = [wgrad(second, grad_inner[at]).reshape(shards, sr, width) for at in range(chunks)]
    ffn.append(wgrad(mixed, gb2).reshape(shards, sr, width))
    narrow_grad = [wgrad(active[at], gb3).reshape(shards // chunks, wr, width) for at in range(chunks)]
    ffn.append(jnp.concatenate(narrow_grad))
    ffn_shard = lax.psum_scatter(
        jnp.concatenate(ffn, 1).reshape(-1, width), AXES, scatter_dimension=0, tiled=True
    ).astype(F32)
    ffn_parts = [ffn_shard[sr * at : sr * (at + 1)] for at in range(chunks + 1)]
    widen_shard = jnp.concatenate(ffn_parts[:chunks], 1)
    narrow_shard = ffn_shard[sr * (chunks + 1) :]

    zero = jnp.zeros((1, width), F32)
    vecs = jnp.concatenate(
        [zero, zero, zero, zero, zero, zero, zero, dcb[0:1]]
        + [vec_t[5:6], vec_t[3:4], vec_t[4:5], vec_t[2:3], vec_t[0:1], vec_t[1:2], zero, zero]
    )
    wb_rows = wb_grad.reshape(shards, wr)
    wb_rows = jnp.pad(wb_rows, ((0, 0), (0, width - wr)))
    cross_slabs = [wgrad(first_low, dprobe), dwk, dwv]
    streams = (grad_mid, dprobe, u1, q, k, v, probs)
    if own_rows:
        slab_shard, grad_projected, tokens_grad = back(
            jnp.stack(cross_slabs), dproj, streams, tokens.reshape(n_tok, width),
            attended.reshape(n_tok, width), w_a, patches, g1, vecs, wb_rows, tails,
        )
        extra_shard = slab_shard[8]
    else:
        gb1, dq, dk, dv, tokens_grad, vec_s = pl.pallas_call(
            self_backward,
            grid=grid,
            in_specs=[tb, tb, tb, tb, tb, tb, rows_block(self_p, rb)]
            + [wspec(j) for j in (QUERY, KEY, VALUE, OUT, CQ)]
            + [vspec],
            out_specs=[tb, tb, tb, tb, tb, whole((16, width))],
            out_shape=[sds(tok_sh, BF)] * 5 + [sds((16, width), F32)],
            scratch_shapes=[pltpu.VMEM((rb, length, width), F32)] * 4,
            compiler_params=params(52),
            cost_estimate=cost(14 * n_tok * width * width, 40e6),
            name="self_backward",
        )(grad_mid, dprobe, u1, q, k, v, probs, w_a, w_a, w_a, w_a, w_a, g1)
        slabs = [wgrad(tokens, dq), wgrad(tokens, dk), wgrad(tokens, dv), wgrad(attended, gb1)] + cross_slabs
        grad_projected = lax.psum_scatter(dproj, "dp", scatter_dimension=0, tiled=True)
        dwp = lax.dot_general(patches, grad_projected, (((0, 1), (0, 1)), ((), ())), preferred_element_type=F32)
        dwp = dwp.reshape(shards, pr, width)
        vecs = vecs + vec_s
        vecs = vecs.at[5].set(jnp.sum(grad_projected.astype(F32), (0, 1)))
        vecs = jnp.broadcast_to(vecs[None, :nv], (shards, nv, width))
        slabs.append(dwp[:, :sr].reshape(slab).astype(BF))
        slab_shard = lax.psum_scatter(jnp.stack(slabs), AXES, scatter_dimension=1, tiled=True).astype(F32)
        extra_grad = jnp.concatenate([dwp[:, sr:], vecs, wb_rows[:, None]], 1).astype(BF)
        extra_shard = lax.psum_scatter(extra_grad, AXES, scatter_dimension=0, tiled=True)[0].astype(F32)
    patch_shard = jnp.concatenate([slab_shard[7], extra_shard[:tails]], 0)
    patches_grad = lax.dot_general(
        grad_projected, patch_full, (((2,), (1,)), ((), ())), preferred_element_type=F32
    ).astype(BF)
    vg = lax.dynamic_slice(extra_shard, (tails, place * sr), (nv, sr))
    vg = [vg[j] for j in range(nv)]
    wbg = extra_shard[tails + nv, :wr]
    return (
        output, tokens_grad, patches_grad,
        slab_shard[0], vg[0], slab_shard[1], slab_shard[2], vg[1], slab_shard[3], vg[2], vg[3], vg[4],
        patch_shard, vg[5], slab_shard[4], vg[6], slab_shard[5], slab_shard[6], vg[7], ffn_parts[chunks],
        vg[8], vg[9], vg[10], widen_shard, wbg, narrow_shard, vg[11], vg[12], vg[13],
    )


def solution(mesh):
    three, two, one = P(AXES, None, None), P(AXES, None), P(AXES)
    in_specs = (
        three, three, two, one, one, three,
        two, one, two, two, one, two, one, one, one, two, one, two, one, two,
        two, one, two, one, one, one, two, one, two, one, one, one,
    )
    out_specs = (
        three, three, three,
        two, one, two, two, one, two, one, one, one, two, one, two, one, two, two, one, two,
        one, one, one, two, one, two, one, one, one,
    )
    return jax.shard_map(on_device, mesh=mesh, in_specs=in_specs, out_specs=out_specs, check_vma=False)
```

```python
import functools

import jax
import jax.numpy as jnp
from jax import lax
from jax.experimental import pallas as pl
from jax.experimental.pallas import tpu as pltpu
from jax.sharding import PartitionSpec as P

HEADS = 12
AXES = ("dp", "fsdp")
BF = jnp.bfloat16
F32 = jnp.float32
norm_eps = 1e-06
mask_fill = -1000000000.0

WINDOWS = ((0, 0), (128, 64), (384, 0), (512, 64))

ERFC_POLE = 0.3
ERFC_POLY = (
    0.16918935391840687,
    0.17069093065701252,
    0.14852123834149009,
    0.214181489197379,
    -0.09282620690981414,
    0.5449671942862269,
    -0.5097726086693966,
    0.4843018450108595,
    -0.12925324449453648,
)
INV_SQRT2 = 0.7071067811865476
INV_SQRT2PI = 0.3989422804014327


def nn(left, right):
    return lax.dot_general(left, right, (((1,), (0,)), ((), ())), preferred_element_type=F32)


def nt(left, right):
    return lax.dot_general(left, right, (((1,), (1,)), ((), ())), preferred_element_type=F32)


def tn(left, right):
    return lax.dot_general(left, right, (((0,), (0,)), ((), ())), preferred_element_type=F32)


def norm_parts(value):
    mean = jnp.mean(value, -1, keepdims=True)
    centred = value - mean
    spread = jnp.mean(centred * centred, -1, keepdims=True)
    inv = lax.rsqrt(spread + norm_eps)
    return centred * inv, inv


def norm_back(grad, gain, xhat, inv):
    scaled = grad * gain
    first = jnp.mean(scaled, -1, keepdims=True)
    second = jnp.mean(scaled * xhat, -1, keepdims=True)
    return inv * (scaled - first - xhat * second)


def gelu_parts(v):
    z = jnp.abs(v) * INV_SQRT2
    t = 1.0 / (1.0 + ERFC_POLE * z)
    poly = jnp.full_like(t, ERFC_POLY[-1])
    for c in ERFC_POLY[-2::-1]:
        poly = poly * t + c
    bell = jnp.exp(-0.5 * (v * v))
    half = (0.5 * bell) * (t * poly)
    cdf = jnp.where(v >= 0, 1.0 - half, half)
    return v * cdf, cdf + (v * INV_SQRT2PI) * bell


def window(full, index):
    base = WINDOWS[index][0]
    return full[:, base : base + 256]


def column_softmax(scores):
    e = jnp.exp(scores - jnp.max(scores, 0, keepdims=True))
    return (e * (1.0 / jnp.sum(e, 0, keepdims=True))).astype(BF)


def score_grads(probs, grads):
    p = probs.astype(F32)
    return (p * (grads - jnp.sum(grads * p, 0, keepdims=True))).astype(BF)


def stack_heads(full, index):
    base, off = WINDOWS[index]
    win = full[:, base : base + 256]
    lane = lax.broadcasted_iota(jnp.int32, win.shape, 1)
    blocks = []
    for h in range(3):
        lo = off + 64 * h
        blocks.append(jnp.where((lane >= lo) & (lane < lo + 64), win, 0.0))
    return jnp.concatenate(blocks, 0).astype(BF)


def unstack_heads(stacked, index, rows):
    _, off = WINDOWS[index]
    lane = lax.broadcasted_iota(jnp.int32, (rows, 256), 1)
    out = None
    for h in range(3):
        lo = off + 64 * h
        part = jnp.where((lane >= lo) & (lane < lo + 64), stacked[rows * h : rows * (h + 1)], 0.0)
        out = part if out is None else out + part
    return out


def join_windows(parts):
    a, b, c, d = parts
    return jnp.concatenate(
        [
            a[:, :128],
            a[:, 128:] + b[:, :128],
            b[:, 128:],
            c[:, :128],
            c[:, 128:] + d[:, :128],
            d[:, 128:],
        ],
        1,
    )


def self_block(x32, bias, mats, vecs, put, att_s):
    rb, length, width = x32.shape
    n = rb * length
    wq, wk, wv, wo, wc = mats
    qb, vb, ob, g1, b1, pb = vecs
    x32 = x32.reshape(n, width)
    x = x32.astype(BF)
    q_o, k_o, v_o, p_o = put("q"), put("k"), put("v"), put("p")
    q_o[...] = (nn(x, wq()) + qb).reshape(rb, length, width).astype(BF)
    k_o[...] = nn(x, wk()).reshape(rb, length, width).astype(BF)
    v_o[...] = (nn(x, wv()) + vb).reshape(rb, length, width).astype(BF)

    def row(r, carry):
        qr = q_o[r].astype(F32) * 0.125
        kr = k_o[r].astype(F32)
        vr = v_o[r].astype(F32)
        kws = [window(kr, i).astype(BF) for i in range(4)]
        vws = [window(vr, i).astype(BF) for i in range(4)]
        qss = [stack_heads(qr, i) for i in range(4)]
        mask = bias[r]
        scores = [nt(kws[i], qss[i]) + mask for i in range(4)]
        ps = [column_softmax(st) for st in scores]
        outs = [tn(ps[i], vws[i]) for i in range(4)]
        for i in range(4):
            p_o[r, i] = ps[i]
        att_s[r] = join_windows([unstack_heads(outs[i], i, length) for i in range(4)])
        return carry

    lax.fori_loop(0, rb, row, 0)
    att32 = att_s[...]
    put("att")[...] = att32.astype(BF)
    att = att32.reshape(n, width).astype(BF)
    u1 = x32 + nn(att, wo()) + ob
    put("u1")[...] = u1.reshape(rb, length, width)
    xhat, _ = norm_parts(u1)
    first32 = xhat * g1 + b1
    put("first")[...] = first32.reshape(rb, length, width).astype(BF)
    put("probe")[...] = (nn(first32.astype(BF), wc()) + pb).reshape(rb, length, width).astype(BF)


SELF_OUTS = ("q", "k", "v", "p", "att", "u1", "first", "probe")


def self_forward(
    tok, bias, wq, wk, wv, wo, wc, qb, vb, ob, g1, b1, pb, q_o, k_o, v_o, p_o, att_o, u1_o, f_o, pr_o, att_s
):
    outs = dict(zip(SELF_OUTS, (q_o, k_o, v_o, p_o, att_o, u1_o, f_o, pr_o)))
    mats = [lambda ref=ref: ref[...] for ref in (wq, wk, wv, wo, wc)]
    vecs = [ref[...] for ref in (qb, vb, ob, g1, b1, pb)]
    self_block(tok[...].astype(F32), bias, mats, vecs, lambda name: outs[name], att_s)


def cross_forward(starts, order, proj, wk, wv, cb, probe, k_o, v_o, p_o, mix_o, pr_s):
    i = pl.program_id(0)
    points = proj.shape[1]
    length = probe.shape[1]

    @pl.when(i == 0)
    def _():
        pr_s[...] = jnp.zeros_like(pr_s)

    lo, hi = starts[i], starts[i + 1]

    @pl.when(hi > lo)
    def _():
        pr_s[0:points, :] = proj[0]
        pr = pr_s[...]
        k_o[0] = nn(pr, wk[...]).astype(BF)
        v_o[0] = (nn(pr, wv[...]) + cb[...]).astype(BF)

        def row(j, carry):
            r = order[j]
            qr = probe[r].astype(F32) * 0.125
            qss = [stack_heads(qr, g) for g in range(4)]
            scores = [nt(k_o[0, :, WINDOWS[g][0] : WINDOWS[g][0] + 256], qss[g]) for g in range(4)]
            point = lax.broadcasted_iota(jnp.int32, scores[0].shape, 0)
            ps = [column_softmax(jnp.where(point < points, st, -1e30)) for st in scores]
            outs = [tn(ps[g], v_o[0, :, WINDOWS[g][0] : WINDOWS[g][0] + 256]) for g in range(4)]
            for g in range(4):
                p_o[r, g] = ps[g]
            mix_o[r] = join_windows([unstack_heads(outs[g], g, length) for g in range(4)]).astype(BF)
            return carry

        lax.fori_loop(lo, hi, row, 0)


def tail_kernel(
    u1, mix, og, wco, w1, w2, g1, b1, cb, g2, s2, wb, nb, g3, s3,
    out_o, act_o, gi_o, sec_o, gb3_o, gm_o, gb2_o, gc_o, vec_o, wbg_o,
    act_s, gp_s, acc_s,
):
    step = pl.program_id(0)
    rb, length, width = u1.shape
    n = rb * length
    chunks = w1.shape[0]

    @pl.when(step == 0)
    def _():
        vec_o[...] = jnp.zeros_like(vec_o)
        wbg_o[...] = jnp.zeros_like(wbg_o)

    def flat(ref):
        return ref[...].astype(F32).reshape(n, width)

    def fold(value):
        return value.reshape(rb, length, width)

    xhat1, _ = norm_parts(flat(u1))
    first = xhat1 * g1[...] + b1[...]
    u2 = first + nn(flat(mix).astype(BF), wco[...]) + cb[...]
    xhat2, inv2 = norm_parts(u2)
    second = (xhat2 * g2[...] + s2[...]).astype(BF)
    sec32 = second.astype(F32)
    sec_o[...] = fold(sec32).astype(BF)
    total = sec32 + nb[...]
    inner = nn(second, w1[0]) + wb[0]
    for at in range(chunks):
        following = nn(second, w1[at + 1]) + wb[at + 1] if at + 1 < chunks else None
        act, slope = gelu_parts(inner)
        act = act.astype(BF)
        gp_s[at] = slope
        act_o[at] = act
        total = total + nn(act, w2[at])
        inner = following
    acc_s[...] = total
    xhat3, inv3 = norm_parts(acc_s[...])
    out_o[...] = fold(xhat3 * g3[...] + s3[...]).astype(BF)
    y = flat(og)
    grad_summed = norm_back(y, g3[...], xhat3, inv3)
    gb3 = grad_summed.astype(BF)
    gb3f = gb3.astype(F32)
    gb3_o[...] = fold(gb3f).astype(BF)
    vec_o[0:1] += jnp.sum(y * xhat3, 0, keepdims=True)
    vec_o[1:2] += jnp.sum(y, 0, keepdims=True)
    vec_o[2:3] += jnp.sum(gb3f, 0, keepdims=True)
    total = grad_summed
    back = nt(gb3, w2[0])
    for at in range(chunks):
        following = nt(gb3, w2[at + 1]) if at + 1 < chunks else None
        gi = (back * gp_s[at]).astype(BF)
        gi_o[at] = gi
        wbg_o[at] += jnp.sum(gi.astype(F32), 0, keepdims=True)
        total = total + nt(gi, w1[at])
        back = following
    acc_s[...] = total
    y2 = acc_s[...].astype(BF).astype(F32)
    gm = norm_back(y2, g2[...], xhat2, inv2)
    gm_o[...] = fold(gm)
    gb2 = gm.astype(BF)
    gb2f = gb2.astype(F32)
    gb2_o[...] = fold(gb2f).astype(BF)
    vec_o[3:4] += jnp.sum(y2 * xhat2, 0, keepdims=True)
    vec_o[4:5] += jnp.sum(y2, 0, keepdims=True)
    vec_o[5:6] += jnp.sum(gb2f, 0, keepdims=True)
    gc_o[...] = fold(nt(gb2, wco[...])).astype(BF)


def cross_backward(
    starts, order, proj, keys, values, wk, wv, probe, grad, probs,
    dpr_o, dproj_o, dwk_o, dwv_o, dcb_o,
    pr_s, dk_s, dv_s, dwk_s, dwv_s,
):
    i = pl.program_id(0)
    points = proj.shape[1]
    length = probe.shape[1]

    @pl.when(i == 0)
    def _():
        pr_s[...] = jnp.zeros_like(pr_s)
        dwk_s[...] = jnp.zeros_like(dwk_s)
        dwv_s[...] = jnp.zeros_like(dwv_s)
        dcb_o[...] = jnp.zeros_like(dcb_o)

    lo, hi = starts[i], starts[i + 1]

    @pl.when(hi == lo)
    def _():
        dproj_o[...] = jnp.zeros_like(dproj_o)

    @pl.when(hi > lo)
    def _():
        dk_s[...] = jnp.zeros_like(dk_s)
        dv_s[...] = jnp.zeros_like(dv_s)

        def row(j, carry):
            r = order[j]
            qr = probe[r].astype(F32) * 0.125
            gr = grad[r].astype(F32)
            gss = [stack_heads(gr, g) for g in range(4)]
            dps = [nt(values[0, :, WINDOWS[g][0] : WINDOWS[g][0] + 256], gss[g]) for g in range(4)]
            qss = [stack_heads(qr, g) for g in range(4)]
            pbs = [probs[r, g] for g in range(4)]
            dvs = [nn(pbs[g], gss[g]) for g in range(4)]
            dss = [score_grads(pbs[g], dps[g]) for g in range(4)]
            dks = [nn(dss[g], qss[g]) for g in range(4)]
            outs = [tn(dss[g], keys[0, :, WINDOWS[g][0] : WINDOWS[g][0] + 256]) for g in range(4)]
            dv_s[...] += join_windows(dvs)
            dk_s[...] += join_windows(dks)
            dpr_o[r] = (join_windows([unstack_heads(outs[g], g, length) for g in range(4)]) * 0.125).astype(BF)
            return carry

        lax.fori_loop(lo, hi, row, 0)
        pr_s[0:points, :] = proj[0]
        pr = pr_s[...]
        dk = dk_s[...].astype(BF)
        dv = dv_s[...].astype(BF)
        dcb_o[0:1] += jnp.sum(dv.astype(F32), 0, keepdims=True)
        dproj = (nt(dk, wk[...]) + nt(dv, wv[...])).astype(BF)
        dproj_o[0] = dproj[0:points]
        dwk_s[...] += tn(pr, dk)
        dwv_s[...] += tn(pr, dv)

    @pl.when(i == pl.num_programs(0) - 1)
    def _():
        dwk_o[...] = dwk_s[...].astype(BF)
        dwv_o[...] = dwv_s[...].astype(BF)


def self_back_block(gm, dpr32, u1, heads, mats, g1, add, temps):
    q, k, v, probs = heads
    wq, wk, wv, wo, wc = mats
    ga_s, dq_s, dk_s, dv_s = temps
    rb, length, width = ga_s.shape
    n = rb * length
    grad_first = gm + nt(dpr32.astype(BF), wc())
    xhat, inv = norm_parts(u1)
    low = norm_back(grad_first, g1, xhat, inv)
    gb1 = low.astype(BF)
    add(3, grad_first * xhat)
    add(4, grad_first)
    add(2, gb1.astype(F32))
    add(6, dpr32)
    ga_s[...] = nt(gb1, wo()).astype(BF).astype(F32).reshape(rb, length, width)

    def row(r, carry):
        qr = q[r].astype(F32) * 0.125
        kr = k[r].astype(F32)
        vr = v[r].astype(F32)
        gr = ga_s[r]
        gss = [stack_heads(gr, i) for i in range(4)]
        vws = [window(vr, i).astype(BF) for i in range(4)]
        dps = [nt(vws[i], gss[i]) for i in range(4)]
        qss = [stack_heads(qr, i) for i in range(4)]
        kws = [window(kr, i).astype(BF) for i in range(4)]
        pbs = [probs[r, i] for i in range(4)]
        dvs = [nn(pbs[i], gss[i]) for i in range(4)]
        dss = [score_grads(pbs[i], dps[i]) for i in range(4)]
        dks = [nn(dss[i], qss[i]) for i in range(4)]
        outs = [tn(dss[i], kws[i]) for i in range(4)]
        dq_s[r] = join_windows([unstack_heads(outs[i], i, length) for i in range(4)]) * 0.125
        dk_s[r] = join_windows(dks)
        dv_s[r] = join_windows(dvs)
        return carry

    lax.fori_loop(0, rb, row, 0)
    dq = dq_s[...].reshape(n, width).astype(BF)
    dk = dk_s[...].reshape(n, width).astype(BF)
    dv = dv_s[...].reshape(n, width).astype(BF)
    add(0, dq.astype(F32))
    add(1, dv.astype(F32))
    total = low + nt(dq, wq()) + nt(dk, wk()) + nt(dv, wv())
    return gb1, dq, dk, dv, total.reshape(rb, length, width).astype(BF)


def self_backward(
    gm, dpr, u1, q, k, v, probs, wq, wk, wv, wo, wc, g1, gb1_o, dq_o, dk_o, dv_o, tg_o, vec_o, *temps
):
    rb, length, width = u1.shape
    n = rb * length

    @pl.when(pl.program_id(0) == 0)
    def _():
        vec_o[...] = jnp.zeros_like(vec_o)

    def add(row, value):
        vec_o[row : row + 1] += jnp.sum(value, 0, keepdims=True)

    def flat(ref):
        return ref[...].astype(F32).reshape(n, width)

    mats = [lambda ref=ref: ref[...] for ref in (wq, wk, wv, wo, wc)]
    *grads, tokens_grad = self_back_block(
        flat(gm), flat(dpr), flat(u1), (q, k, v, probs), mats, g1[...], add, temps
    )
    for ref, value in zip((gb1_o, dq_o, dk_o, dv_o), grads):
        ref[...] = value.astype(F32).reshape(rb, length, width).astype(BF)
    tg_o[...] = tokens_grad


def sds(shape, dtype):
    return jax.ShapeDtypeStruct(shape, dtype)


def whole(shape, *, single=True):
    zeros = (0,) * len(shape)
    mode = pl.Buffered(1) if single else None
    return pl.BlockSpec(shape, lambda i, *_: zeros, pipeline_mode=mode)


def rows_block(shape, rb):
    rest = tuple(shape[1:])
    return pl.BlockSpec((rb,) + rest, lambda i, *_: (i,) + (0,) * len(rest))


def params(mib):
    return pltpu.CompilerParams(
        dimension_semantics=("arbitrary",), vmem_limit_bytes=mib * 1024 * 1024
    )


def cost(flops, bytes_accessed):
    return pl.CostEstimate(flops=int(flops), bytes_accessed=int(bytes_accessed), transcendentals=0)


def my_place():
    dp, fs = lax.axis_index("dp"), lax.axis_index("fsdp")
    return dp // 2, dp % 2, fs // 2, fs % 2


def device_at(z, y, x, c):
    return (z * 2 + y, x * 2 + c)


def meet(z, y, x, c):
    sem = pltpu.get_barrier_semaphore()
    others = [device_at((z + k) % 4, y, x, c) for k in (1, 2, 3)]
    others += [device_at(z, 1 - y, x, c), device_at(z, y, 1 - x, c), device_at(z, y, x, 1 - c)]
    for other in others:
        pl.semaphore_signal(sem, inc=1, device_id=other, device_id_type=pl.DeviceIdType.MESH)
    pl.semaphore_wait(sem, len(others))


class Copies:
    def __init__(self, send, recv, local):
        self.send, self.recv, self.local = send, recv, local
        self.far = self.near = 0
        self.sent = []

    def prepare(self, src, dst, device):
        i = self.far
        self.far += 1
        return pltpu.make_async_remote_copy(
            src_ref=src, dst_ref=dst, send_sem=self.send.at[i], recv_sem=self.recv.at[i],
            device_id=device, device_id_type=pl.DeviceIdType.MESH,
        )

    def remote(self, src, dst, device):
        copy = self.prepare(src, dst, device)
        copy.start()
        return copy

    def here(self, src, dst):
        i = self.near
        self.near += 1
        copy = pltpu.make_async_copy(src, dst, self.local.at[i])
        copy.start()
        return copy


def arrived(copies):
    for copy in copies:
        copy.wait()


def drive(jobs, order):
    for name in order:
        next(jobs[name], None)
    for job in jobs.values():
        for _ in job:
            pass


PATCH, EXTRA, QUERY, KEY, VALUE, OUT, CQ, CK, W1 = range(9)
CV, CO = 12, 13


FRONT_ORDER = (
    "P", "Q", "P", "P", "Q", "P", "Q", "R", "P", "P", "P", "F", "Q", "P", "Q", "Q", "F", "P",
    "weights", "F", "i0", "i1", "Q", "F", "i0", "i3", "G", "F", "R", "i1", "i3", "Q", "G", "G",
    "i0", "i0", "F", "Q", "self", "i2", "i3", "G", "self", "R", "i2", "F", "G", "self", "i3", "i1",
    "G", "self", "G", "R", "R", "i1", "F", "i2", "self", "R", "R", "G", "i2", "R",
)
BACK_ORDER = (
    "p2", "S", "E", "E", "p0", "p2", "p1", "S", "p0", "S", "p1", "p3", "S", "S", "D1", "D2", "L2",
    "E", "L2", "p3", "L1", "L1", "L2", "p2", "p0", "L1", "p1", "E", "p3", "V1", "V1", "V2", "L2",
    "E", "V2", "L1", "V1", "V1", "V2", "V2", "L2", "V1", "L1", "V2",
)


def front_kernel(
    parts, tails, nv, rb, w_in, n_in, pat, tok, bias, w_out, n_out, p_out, q_o, k_o, v_o, pr_o, att_o, u1_o, f_o, prb_o, vec_o,
    pw, ex, wm, proj_s, q_s, k_s, v_s, pr_s, att_b, u1_s, f_s, prb_s, att_s, send, recv, local,
):
    z, y, x, c = my_place()
    meet(z, y, x, c)
    copies = Copies(send, recv, local)
    rows, length, width = tok.shape
    images = pat.shape[0]

    inner = (z + 1) % 4 >= 2
    partner = z + 1 - 2 * (z % 2)
    across = 3 - z
    ours, theirs = 2 * (z // 2), 2 - 2 * (z // 2)

    def along_z(source, view, tell, local):
        step = copies.remote(source, view(z, 0), device_at(partner, y, x, c))
        tell("own")
        yield
        step.wait()
        if local is not None:
            local.wait()
        tell("partner")
        middle = copies.prepare(view(ours, 2), view(ours, 2), device_at(across, y, x, c))
        outward = copies.prepare(view(theirs, 2), view(theirs, 2), device_at(partner, y, x, c))

        @pl.when(inner)
        def _():
            middle.start()

        yield

        @pl.when(inner)
        def _():
            middle.wait()
            outward.start()
            tell("inner")

        yield

        @pl.when(jnp.logical_not(inner))
        def _():
            outward.wait_recv()
            tell("outer")

        copies.sent.append((inner, outward))
        yield

    def exchanged(source, view, local):
        own = copies.prepare(source, view(z, 0), device_at(z, 1 - y, x, c))
        second = copies.prepare(view(partner, 0), view(partner, 0), device_at(z, 1 - y, x, c))
        third = copies.prepare(view(theirs, 2), view(theirs, 2), device_at(z, 1 - y, x, c))
        start = {"own": own, "partner": second, "inner": third, "outer": third}
        return along_z(source, view, lambda which: start[which].start(), local), (own, second, third)

    def slabs(source, out):
        every = slice(None)

        def view(at, many):
            return out(pl.ds(at, many) if many else at, y, x, c)

        def plane(at, many):
            return out(pl.ds(at, many) if many else at, every, x, c)

        local = copies.here(source, view(z, 0))
        moving, (own, second, third) = exchanged(source, view, None)
        next(moving)
        yield
        own.wait()
        local.wait()
        steps = [copies.remote(plane(z, 0), plane(z, 0), device_at(z, y, 1 - x, c))]
        yield
        for _ in range(3):
            next(moving)
            yield
        second.wait()
        steps.append(copies.remote(plane(partner, 0), plane(partner, 0), device_at(z, y, 1 - x, c)))
        yield
        third.wait()
        steps.append(copies.remote(plane(theirs, 2), plane(theirs, 2), device_at(z, y, 1 - x, c)))
        yield
        arrived(steps)
        half = out(every, every, every, c)
        step = copies.remote(half, half, device_at(z, y, x, 1 - c))
        yield
        step.wait()

    def patch_weights():
        rest = pw.shape[4] - tails
        arrived(
            [
                copies.here(w_out.at[PATCH], pw.at[:, :, :, :, 0:rest]),
                copies.here(w_out.at[EXTRA, :, :, :, :, 0:tails], pw.at[:, :, :, :, rest:]),
                copies.here(w_out.at[EXTRA], ex),
            ]
        )
        total = jnp.zeros(ex.shape[4:], F32)
        for zz in range(4):
            for yy in range(2):
                for xx in range(2):
                    for cc in range(2):
                        total = total + ex[zz, yy, xx, cc].astype(F32)
        vec_o[...] = total
        yield

    def vec(j):
        return vec_o[tails + j : tails + j + 1, :]

    def image(i):
        full = pw[...].reshape(pat.shape[2], width)
        proj_s[i] = (nn(pat[i], full) + vec(5)).astype(BF)

        def view(at, many):
            return p_out.at[pl.ds(at, many) if many else at, y, i]

        moving, steps = exchanged(proj_s.at[i], view, copies.here(proj_s.at[i], view(z, 0)))
        yield from moving
        arrived(steps)

    def attention():
        arrived([copies.here(w_out.at[QUERY + m], wm.at[m]) for m in range(5)])
        yield
        scratch = dict(zip(SELF_OUTS, (q_s, k_s, v_s, pr_s, att_b, u1_s, f_s, prb_s)))
        finals = dict(zip(SELF_OUTS, (q_o, k_o, v_o, pr_o, att_o, u1_o, f_o, prb_o)))
        mats = [lambda m=m: wm[m].reshape(width, width) for m in range(5)]
        outgoing = []
        for b in range(rows // rb):
            pick = pl.ds(b * rb, rb)
            self_block(
                tok[pick].astype(F32), bias.at[pick], mats, [vec(j) for j in (0, 1, 2, 3, 4, 6)],
                lambda name: scratch[name].at[pick], att_s,
            )
            outgoing += [copies.here(scratch[name].at[pick], finals[name].at[pick]) for name in SELF_OUTS]
            yield
        arrived(outgoing)

    def stacked(lo, n):
        pick = pl.ds(lo, n)
        return slabs(w_in.at[pick], lambda *at: w_out.at[(pick,) + at])

    jobs = {name: stacked(lo, n) for name, (lo, n) in parts.items()}
    jobs["G"] = slabs(n_in, lambda *at: n_out.at[at])
    jobs["weights"] = patch_weights()
    for i in range(images):
        jobs["i%d" % i] = image(i)
    jobs["self"] = attention()
    drive(jobs, FRONT_ORDER)
    for when, copy in copies.sent:

        @pl.when(when)
        def _(copy=copy):
            copy.wait_send()


def back_kernel(
    rb, tails, w_in, p_in, gm, dpr, u1, q, k, v, probs, tok, att, w_all, pat, g1, vt_in, wb_in,
    w_out, p_out, tg_o,
    wm, gm_s, dpr_s, u1_s, q_s, k_s, v_s, p_s, ga_t, dq_t, dk_t, dv_t, gb1_f, dq_f, dk_f, dv_f, tg_s, vec_s,
    acc, lw, pv, rc, rx, ry, rz, pacc, pry, prz, send, recv, local,
):
    z, y, x, c = my_place()
    meet(z, y, x, c)
    copies = Copies(send, recv, local)
    rows, length, width = gm.shape
    images = pat.shape[0]
    sr = w_out.shape[1]

    def up(ref, *at):
        return ref[at].astype(F32)

    def slabs(lo, n, sibling, own, base, own_c):
        pick = pl.ds(lo, n)
        last = (c,) if own_c else ()

        def cell(s, zz, yy, xx):
            return (s - base, zz, yy, xx) + last

        def view(zz, yy, xx):
            return own.at[(pl.ds(lo - base, n), zz, yy, xx) + last]

        every = slice(None)
        step = copies.remote(sibling, rc.at[pick], device_at(z, y, x, 1 - c))
        yield
        step.wait()

        def add_x(i, carry):
            s, zz = lo + i // 4, i % 4
            for yy in range(2):
                at = cell(s, zz, yy, 1 - x)
                own[at] = (up(own, *at) + up(rc, s, zz, yy, 1 - x)).astype(BF)
            return carry

        lax.fori_loop(0, 4 * n, add_x, 0)
        step = copies.remote(view(every, every, 1 - x), rx.at[pick], device_at(z, y, 1 - x, c))
        yield
        step.wait()

        def add_y(i, carry):
            s, zz = lo + i // 4, i % 4
            at = cell(s, zz, 1 - y, x)
            own[at] = (up(own, *at) + up(rc, s, zz, 1 - y, x) + up(rx, s, zz, 1 - y)).astype(BF)
            return carry

        lax.fori_loop(0, 4 * n, add_y, 0)
        step = copies.remote(view(every, 1 - y, x), ry.at[pick], device_at(z, 1 - y, x, c))
        yield
        step.wait()
        steps = []
        for hop in (1, 3, 2):
            zz = (z + hop) % 4

            def add_z(i, carry):
                s = lo + i
                at = cell(s, zz, y, x)
                own[at] = (up(own, *at) + up(rc, s, zz, y, x) + up(rx, s, zz, y) + up(ry, s, zz)).astype(BF)
                return carry

            lax.fori_loop(0, n, add_z, 0)
            steps.append(copies.remote(view(zz, y, x), rz.at[hop - 1, pick], device_at(zz, y, x, c)))
        yield
        arrived(steps)

        def add_last(i, carry):
            s = lo + i
            w_out[s] = (
                up(own, *cell(s, z, y, x)) + up(rc, s, z, y, x) + up(rx, s, z, y) + up(ry, s, z)
                + up(rz, 0, s) + up(rz, 1, s) + up(rz, 2, s)
            )
            return carry

        lax.fori_loop(0, n, add_last, 0)
        yield

    def early():
        own = copies.here(w_in.at[:, :, :, :, c], acc)
        job = slabs(4, 3, w_in.at[:, :, :, :, 1 - c], acc, 4, False)
        next(job)
        yield
        own.wait()
        yield from job

    def image(i):
        own = copies.here(p_in.at[:, y, i], pacc.at[i])
        step = copies.remote(p_in.at[:, 1 - y, i], pry.at[i], device_at(z, 1 - y, x, c))
        yield
        own.wait()
        step.wait()
        steps = []
        for hop in (1, 3, 2):
            zz = (z + hop) % 4
            pacc[i, zz] = (up(pacc, i, zz) + up(pry, i, zz)).astype(BF)
            steps.append(copies.remote(pacc.at[i, zz], prz.at[hop - 1, i], device_at(zz, y, x, c)))
        yield
        arrived(steps)
        p_out[i] = (
            up(pacc, i, z) + up(pry, i, z) + up(prz, 0, i) + up(prz, 1, i) + up(prz, 2, i)
        ).astype(BF)
        yield

    def attention():
        weights = [
            copies.here(w_all.at[m], wm.at[pl.ds(width * at, width)])
            for at, m in enumerate((QUERY, KEY, VALUE, OUT, CQ))
        ]
        vec_s[...] = vt_in[...]
        mats = [lambda at=at: wm[pl.ds(width * at, width)] for at in range(5)]
        streams = ((gm, gm_s), (dpr, dpr_s), (u1, u1_s), (q, q_s), (k, k_s), (v, v_s), (probs, p_s))
        size = gm_s.shape[0]
        n = rb * length

        def add(row, value):
            vec_s[row : row + 1] += jnp.sum(value, 0, keepdims=True)

        leaving = None
        for stage in range(rows // size):
            coming = [copies.here(src.at[pl.ds(stage * size, size)], dst) for src, dst in streams]
            arrived(weights + coming)
            weights = []
            if leaving is not None:
                leaving.wait()

            def block(b, carry):
                pick = pl.ds(b * rb, rb)

                def flat(ref):
                    return ref[pick].astype(F32).reshape(n, width)

                heads = tuple(ref.at[pick] for ref in (q_s, k_s, v_s, p_s))
                *grads, tokens_grad = self_back_block(
                    flat(gm_s), flat(dpr_s), flat(u1_s), heads, mats, g1[...], add, (ga_t, dq_t, dk_t, dv_t)
                )
                at = pl.ds(pl.multiple_of(stage * size * length + b * n, n), n)
                for ref, value in zip((gb1_f, dq_f, dk_f, dv_f), grads):
                    ref[at] = value
                tg_s[pick] = tokens_grad
                return carry

            lax.fori_loop(0, size // rb, block, 0)
            leaving = copies.here(tg_s, tg_o.at[pl.ds(stage * size, size)])
            yield
        leaving.wait()
        count = rows * length
        arrived(
            [
                copies.here(tok, wm.at[pl.ds(0, count)]),
                copies.here(att, wm.at[pl.ds(count, count)]),
            ]
        )
        yield

    def gradient(pairs):
        count = rows * length
        for m, first, right in pairs:
            left = wm[pl.ds(first * count, count)]
            lw[m] = tn(left, right[...]).reshape(lw.shape[1:]).astype(BF)
        yield

    def late(lo):
        yield from slabs(lo, 2, lw.at[pl.ds(lo, 2), :, :, :, 1 - c], lw, 0, True)

    def patch_sums(first):
        pwidth = pat.shape[2]
        rows_each = pwidth // 32
        step = 128
        bias = jnp.sum(p_out[0].astype(F32), 0, keepdims=True)
        for i in range(1, images):
            bias = bias + jnp.sum(p_out[i].astype(F32), 0, keepdims=True)
        vec_s[5:6] = bias

        for lo in range(0, pwidth, step):
            total = tn(pat[0, :, lo : lo + step], p_out[0])
            for i in range(1, images):
                total = total + tn(pat[i, :, lo : lo + step], p_out[i])
            for at in range(step // rows_each):
                d = lo // rows_each + at
                zz, yy, xx, cc = d // 8, (d // 4) % 2, (d // 2) % 2, d % 2
                part = total[at * rows_each : (at + 1) * rows_each]
                pv[0, zz, yy, xx, cc] = part[:sr].astype(BF)
                vecs = vec_s[...]
                row = lax.broadcasted_iota(jnp.int32, vecs.shape, 0)
                vecs = jnp.where(row == vecs.shape[0] - 2, wb_in[d : d + 1], vecs)
                pv[1, zz, yy, xx, cc] = jnp.concatenate([part[sr:], vecs], 0).astype(BF)

        yield from slabs(first, 1, pv.at[pl.ds(0, 1), :, :, :, 1 - c], pv, first, True)

    def second_patch(first):
        yield from slabs(first, 1, pv.at[pl.ds(1, 1), :, :, :, 1 - c], pv, first - 1, True)

    jobs = {"p%d" % i: image(i) for i in range(images)}
    jobs["E"] = early()
    jobs["S"] = attention()
    jobs["D1"] = gradient(((0, 0, dq_f), (1, 0, dk_f)))
    jobs["D2"] = gradient(((2, 0, dv_f), (3, 1, gb1_f)))
    jobs["L1"], jobs["L2"] = late(0), late(2)
    jobs["V1"], jobs["V2"] = patch_sums(7), second_patch(8)
    drive(jobs, BACK_ORDER)


def front(slabs, narrow, patches, tokens, bias, tails, nv):
    n, sr, width = slabs.shape
    images, points, pwidth = patches.shape
    rows, length, _ = tokens.shape
    rb = 8 if rows % 8 == 0 else 1
    parts = {"P": (PATCH, 2), "Q": (QUERY, 6), "F": (W1, 4), "R": (CV, 2)}
    nr = narrow.shape[0]
    remote = 10 * (len(parts) + 1) + 6 * images
    near = len(parts) + 1 + images + 3 + 5 + len(SELF_OUTS) * (rows // rb)
    tok_sh = (rows, length, width)
    probs = (rows, 4, length, 3 * length)
    kept = [sds(tok_sh, BF), sds(tok_sh, BF), sds(tok_sh, BF), sds(probs, BF), sds(tok_sh, BF), sds(tok_sh, F32), sds(tok_sh, BF), sds(tok_sh, BF)]
    hbm = pl.BlockSpec(memory_space=pl.ANY)
    vmem = pl.BlockSpec(memory_space=pltpu.VMEM)
    w_all, n_all, p_all, *rest = pl.pallas_call(
        functools.partial(front_kernel, parts, tails, nv, rb),
        in_specs=[hbm, hbm, vmem, vmem, vmem],
        out_specs=[hbm] * 11 + [vmem],
        out_shape=[
            sds((n, 4, 2, 2, 2, sr, width), BF), sds((4, 2, 2, 2, nr, width), BF),
            sds((4, 2, images, points, width), BF), *kept, sds((sr, width), F32),
        ],
        scratch_shapes=[
            pltpu.VMEM((4, 2, 2, 2, pwidth // 32, width), BF),
            pltpu.VMEM((4, 2, 2, 2, sr, width), BF),
            pltpu.VMEM((5, 4, 2, 2, 2, sr, width), BF),
            pltpu.VMEM((images, points, width), BF),
            *[pltpu.VMEM(item.shape, item.dtype) for item in kept],
            pltpu.VMEM((rb, length, width), F32),
            pltpu.SemaphoreType.DMA((remote,)),
            pltpu.SemaphoreType.DMA((remote,)),
            pltpu.SemaphoreType.DMA((near,)),
        ],
        compiler_params=pltpu.CompilerParams(
            collective_id=0, has_side_effects=True, vmem_limit_bytes=58 * 1024 * 1024
        ),
        name="front",
    )(slabs, narrow, patches, tokens, bias)
    return w_all.reshape(n, 32 * sr, width), n_all.reshape(32 * nr, width), p_all.reshape(8 * images, points, width), rest[:8], rest[8]


def back(slabs, grads, streams, tok, att, w_all, patches, g1, vecs, wb_rows, tails):
    n, full, width = slabs.shape
    sr = full // 32
    total, points, _ = grads.shape
    images, _, pwidth = patches.shape
    rows, length, _ = streams[0].shape
    m = n + 6
    size, rb = 8, 4
    hbm = pl.BlockSpec(memory_space=pl.ANY)
    vmem = pl.BlockSpec(memory_space=pltpu.VMEM)
    remote = 6 * 5 + 4 * images
    near = 1 + images + 5 + 8 * (rows // size) + 2
    part = (sr, width)
    w_shard, p_shard, tokens_grad = pl.pallas_call(
        functools.partial(back_kernel, rb, tails),
        in_specs=[hbm] * 12 + [vmem] * 4,
        out_specs=[vmem, vmem, hbm],
        out_shape=[sds((m, sr, width), F32), sds((images, points, width), BF), sds((rows, length, width), BF)],
        scratch_shapes=[
            pltpu.VMEM((5 * width, width), BF),
            *[pltpu.VMEM((size,) + item.shape[1:], item.dtype) for item in streams],
            *[pltpu.VMEM((rb, length, width), F32)] * 4,
            *[pltpu.VMEM((rows * length, width), BF)] * 4,
            pltpu.VMEM((size, length, width), BF),
            pltpu.VMEM(vecs.shape, F32),
            pltpu.VMEM((n, 4, 2, 2) + part, BF),
            pltpu.VMEM((4, 4, 2, 2, 2) + part, BF),
            pltpu.VMEM((2, 4, 2, 2, 2) + part, BF),
            pltpu.VMEM((m, 4, 2, 2) + part, BF),
            pltpu.VMEM((m, 4, 2) + part, BF),
            pltpu.VMEM((m, 4) + part, BF),
            pltpu.VMEM((3, m) + part, BF),
            pltpu.VMEM((images, 4, points, width), BF),
            pltpu.VMEM((images, 4, points, width), BF),
            pltpu.VMEM((3, images, points, width), BF),
            pltpu.SemaphoreType.DMA((remote,)),
            pltpu.SemaphoreType.DMA((remote,)),
            pltpu.SemaphoreType.DMA((near,)),
        ],
        compiler_params=pltpu.CompilerParams(
            collective_id=1, has_side_effects=True, vmem_limit_bytes=62 * 1024 * 1024
        ),
        name="back",
    )(
        slabs.reshape(n, 4, 2, 2, 2, sr, width), grads.reshape(4, 2, images, points, width), *streams,
        tok, att, w_all, patches, g1, vecs, wb_rows,
    )
    return w_shard, p_shard, tokens_grad


def pack_kernel(chunks, patch, extra, *refs):
    *mats, out = refs
    sr, width = extra.shape
    out[PATCH] = patch[0:sr]
    out[EXTRA] = extra[...]
    for at, ref in enumerate(mats[: W1 - QUERY]):
        out[QUERY + at] = ref[...]
    for at in range(chunks):
        out[W1 + at] = mats[W1 - QUERY][:, width * at : width * (at + 1)]
    for at, ref in enumerate(mats[W1 - QUERY + 1 :]):
        out[CV + at] = ref[...]


def pack(patch, extra, before, widen, after):
    sr, width = extra.shape
    chunks = widen.shape[1] // width
    count = 2 + len(before) + chunks + len(after)
    vmem = pl.BlockSpec(memory_space=pltpu.VMEM)
    return pl.pallas_call(
        functools.partial(pack_kernel, chunks),
        in_specs=[vmem] * (3 + len(before) + len(after)),
        out_specs=vmem,
        out_shape=sds((count, sr, width), BF),
        name="pack",
    )(patch, extra, *before, widen, *after)


def gather(value, axis):
    return lax.all_gather(value, AXES, axis=axis, tiled=True)


def on_device(
    tokens, patches, segments, owner, image_slot, out_grad,
    self_query, query_bias, self_key, self_value, value_bias, self_output, output_bias,
    first_gain, first_norm_bias, patch_proj, patch_bias, cross_query, probe_bias, cross_key,
    cross_value, content_bias, cross_output, cross_bias, second_gain, second_shift,
    widen_weight, widen_bias, narrow_weight, narrow_bias, third_gain, third_shift,
):
    rows, length, width = tokens.shape
    images, points, pwidth = patches.shape
    groups = lax.axis_size("dp")
    shards = groups * lax.axis_size("fsdp")
    total_images = groups * images
    hidden = widen_weight.shape[1]
    chunks = hidden // width
    sr = self_query.shape[0]
    wr = widen_bias.shape[0]

    place = lax.axis_index("dp") * lax.axis_size("fsdp") + lax.axis_index("fsdp")
    vec_list = (
        query_bias, value_bias, output_bias, first_gain, first_norm_bias, patch_bias, probe_bias,
        content_bias, cross_bias, second_gain, second_shift, narrow_bias, third_gain, third_shift,
    )
    nv = len(vec_list)
    pr = patch_proj.shape[0]
    tails = pr - sr
    lane_block = jnp.arange(width, dtype=jnp.int32)[None, :] // sr
    vec_rows = jnp.where(lane_block == place, jnp.tile(jnp.stack(vec_list), (1, shards)), jnp.zeros((), BF))
    wb_row = jnp.pad(widen_bias, (0, width - wr))[None]
    extra = jnp.concatenate([patch_proj[sr:], vec_rows, wb_row], 0)
    er = max(sr, extra.shape[0])
    own_rows = er == sr and groups == 8 and shards == 32
    extra = jnp.pad(extra, ((0, er - extra.shape[0]), (0, 0)))
    slabs_in = pack(
        patch_proj, extra[:sr], (self_query, self_key, self_value, self_output, cross_query, cross_key),
        widen_weight, (cross_value, cross_output),
    )

    image = owner * images + image_slot
    idx = jnp.arange(rows, dtype=jnp.int32)
    before = (image[None, :] < image[:, None]) | ((image[None, :] == image[:, None]) & (idx[None, :] < idx[:, None]))
    rank = jnp.sum(before.astype(jnp.int32), 1)
    order = jnp.sum(jnp.where(rank[:, None] == idx[None, :], idx[:, None], 0), 0).astype(jnp.int32)
    starts = jnp.sum((image[None, :] < jnp.arange(total_images + 1, dtype=jnp.int32)[:, None]).astype(jnp.int32), 1)

    same = segments[:, :, None] == segments[:, None, :]
    bias = jnp.where(same, 0.0, mask_fill).astype(F32)
    bias = jnp.concatenate([bias, bias, bias], 2)

    rb = 8 if rows % 8 == 0 else 1
    grid = (rows // rb,)
    tok_sh = (rows, length, width)
    slab = (width, width)

    def wspec(j):
        return pl.BlockSpec((None, width, width), lambda i, *_: (j, 0, 0), pipeline_mode=pl.Buffered(1))

    vspec = whole((1, width))
    tb = rows_block(tok_sh, rb)
    self_p = (rows, 4, length, 3 * length)
    if own_rows:
        w_a, narrow_all, proj_all, kept, vec_all = front(
            slabs_in, narrow_weight, patches, tokens, bias, tails, nv
        )
        vec_all = vec_all[tails : tails + nv]
        extra_all = w_a[EXTRA].reshape(shards, er, width)
    else:
        w_a = gather(slabs_in, 1)
        narrow_all = gather(narrow_weight, 0)
        extra_all = gather(extra, 0).reshape(shards, er, width)
        vec_all = jnp.sum(extra_all[:, tails : tails + nv].astype(F32), 0)
    (qb, vb, ob, g1, b1, pab, prb, cob, crb, g2, s2, nab, g3, s3) = [vec_all[j : j + 1] for j in range(nv)]
    wb = extra_all[:, tails + nv, :wr].astype(F32).reshape(chunks, 1, width)
    narrow_all = narrow_all.reshape(chunks, width, width)
    patch_full = jnp.concatenate([w_a[PATCH].reshape(shards, sr, width), extra_all[:, :tails]], 1)
    patch_full = patch_full.reshape(shards * pr, width)
    if not own_rows:
        projected = lax.dot_general(patches, patch_full, (((2,), (0,)), ((), ())), preferred_element_type=F32)
        proj_all = lax.all_gather((projected + pab).astype(BF), "dp", axis=0, tiled=True)
        kept = pl.pallas_call(
            self_forward,
            grid=grid,
            in_specs=[tb, rows_block((rows, length, 3 * length), rb)]
            + [wspec(j) for j in (QUERY, KEY, VALUE, OUT, CQ)]
            + [vspec] * 6,
            out_specs=[tb, tb, tb, rows_block(self_p, rb), tb, tb, tb, tb],
            out_shape=[
                sds(tok_sh, BF), sds(tok_sh, BF), sds(tok_sh, BF), sds(self_p, BF),
                sds(tok_sh, BF), sds(tok_sh, F32), sds(tok_sh, BF), sds(tok_sh, BF),
            ],
            scratch_shapes=[pltpu.VMEM((rb, length, width), F32)],
            compiler_params=params(48),
            cost_estimate=cost(11 * rows * length * width * width, 30e6),
            name="self_forward",
        )(tokens, bias, w_a, w_a, w_a, w_a, w_a, qb, vb, ob, g1, b1, prb)
    q, k, v, probs, attended, u1, first_low, probe = kept

    padded = -(-points // 16) * 16
    kv_sh = (total_images, padded, width)
    cross_p = (rows, 4, padded, 3 * length)
    img_spec = pl.BlockSpec((1, points, width), lambda i, *_: (i, 0, 0))
    kv_spec = pl.BlockSpec((1, padded, width), lambda i, *_: (i, 0, 0))
    image_keys, image_values, cprobs, mixed = pl.pallas_call(
        cross_forward,
        grid_spec=pltpu.PrefetchScalarGridSpec(
            num_scalar_prefetch=2,
            grid=(total_images,),
            in_specs=[img_spec, wspec(CK), wspec(CV), vspec, whole(tok_sh)],
            out_specs=[kv_spec, kv_spec, whole(cross_p), whole(tok_sh)],
            scratch_shapes=[pltpu.VMEM((padded, width), BF)],
        ),
        out_shape=[sds(kv_sh, BF), sds(kv_sh, BF), sds(cross_p, BF), sds(tok_sh, BF)],
        compiler_params=params(48),
        cost_estimate=cost(4 * total_images * points * width * width, 40e6),
        name="cross_forward",
    )(starts, order, proj_all, w_a, w_a, cob, probe)

    w1_spec = pl.BlockSpec(
        (chunks, width, width), lambda i, *_: (W1 // chunks, 0, 0), pipeline_mode=pl.Buffered(1)
    )
    n_tok = rows * length
    hid_sh = (chunks, n_tok, width)
    hid_spec = pl.BlockSpec((chunks, rb * length, width), lambda i, *_: (0, i, 0))
    (output, active, grad_inner, second, gb3, grad_mid, gb2, grad_crossed, vec_t, wb_grad) = pl.pallas_call(
        tail_kernel,
        grid=grid,
        in_specs=[tb, tb, tb, wspec(CO), w1_spec, whole((chunks, width, width))]
        + [vspec] * 5
        + [whole((chunks, 1, width))]
        + [vspec] * 3,
        out_specs=[tb, hid_spec, hid_spec, tb, tb, tb, tb, tb, whole((8, width)), whole((chunks, 1, width))],
        out_shape=[
            sds(tok_sh, BF), sds(hid_sh, BF), sds(hid_sh, BF), sds(tok_sh, BF), sds(tok_sh, BF),
            sds(tok_sh, F32), sds(tok_sh, BF), sds(tok_sh, BF), sds((8, width), F32), sds((chunks, 1, width), F32),
        ],
        scratch_shapes=[
            pltpu.VMEM((8, 128), BF),
            pltpu.VMEM((chunks, rb * length, width), F32),
            pltpu.VMEM((rb * length, width), F32),
        ],
        compiler_params=params(56),
        cost_estimate=cost(18 * n_tok * width * width + 8 * n_tok * width * hidden, 50e6),
        name="tail",
    )(u1, mixed, out_grad, w_a, w_a, narrow_all, g1, b1, crb, g2, s2, wb, nab, g3, s3)

    dprobe, dproj, dwk, dwv, dcb = pl.pallas_call(
        cross_backward,
        grid_spec=pltpu.PrefetchScalarGridSpec(
            num_scalar_prefetch=2,
            grid=(total_images,),
            in_specs=[img_spec, kv_spec, kv_spec, wspec(CK), wspec(CV), whole(tok_sh), whole(tok_sh), whole(cross_p)],
            out_specs=[whole(tok_sh), img_spec, whole(slab), whole(slab), whole((8, width))],
            scratch_shapes=[
                pltpu.VMEM((padded, width), BF),
                pltpu.VMEM((padded, width), F32),
                pltpu.VMEM((padded, width), F32),
                pltpu.VMEM((width, width), F32),
                pltpu.VMEM((width, width), F32),
            ],
        ),
        out_shape=[sds(tok_sh, BF), sds((total_images, points, width), BF), sds(slab, BF), sds(slab, BF), sds((8, width), F32)],
        compiler_params=params(56),
        cost_estimate=cost(8 * total_images * points * width * width, 50e6),
        name="cross_backward",
    )(starts, order, proj_all, image_keys, image_values, w_a, w_a, probe, grad_crossed, cprobs)

    def wgrad(left, right):
        return tn(left.reshape(n_tok, width), right.reshape(n_tok, width)).astype(BF)

    ffn = [wgrad(second, grad_inner[at]).reshape(shards, sr, width) for at in range(chunks)]
    ffn.append(wgrad(mixed, gb2).reshape(shards, sr, width))
    narrow_grad = [wgrad(active[at], gb3).reshape(shards // chunks, wr, width) for at in range(chunks)]
    ffn.append(jnp.concatenate(narrow_grad))
    ffn_shard = lax.psum_scatter(
        jnp.concatenate(ffn, 1).reshape(-1, width), AXES, scatter_dimension=0, tiled=True
    ).astype(F32)
    ffn_parts = [ffn_shard[sr * at : sr * (at + 1)] for at in range(chunks + 1)]
    widen_shard = jnp.concatenate(ffn_parts[:chunks], 1)
    narrow_shard = ffn_shard[sr * (chunks + 1) :]

    zero = jnp.zeros((1, width), F32)
    vecs = jnp.concatenate(
        [zero, zero, zero, zero, zero, zero, zero, dcb[0:1]]
        + [vec_t[5:6], vec_t[3:4], vec_t[4:5], vec_t[2:3], vec_t[0:1], vec_t[1:2], zero, zero]
    )
    wb_rows = wb_grad.reshape(shards, wr)
    wb_rows = jnp.pad(wb_rows, ((0, 0), (0, width - wr)))
    cross_slabs = [wgrad(first_low, dprobe), dwk, dwv]
    streams = (grad_mid, dprobe, u1, q, k, v, probs)
    if own_rows:
        slab_shard, grad_projected, tokens_grad = back(
            jnp.stack(cross_slabs), dproj, streams, tokens.reshape(n_tok, width),
            attended.reshape(n_tok, width), w_a, patches, g1, vecs, wb_rows, tails,
        )
        extra_shard = slab_shard[8]
    else:
        gb1, dq, dk, dv, tokens_grad, vec_s = pl.pallas_call(
            self_backward,
            grid=grid,
            in_specs=[tb, tb, tb, tb, tb, tb, rows_block(self_p, rb)]
            + [wspec(j) for j in (QUERY, KEY, VALUE, OUT, CQ)]
            + [vspec],
            out_specs=[tb, tb, tb, tb, tb, whole((16, width))],
            out_shape=[sds(tok_sh, BF)] * 5 + [sds((16, width), F32)],
            scratch_shapes=[pltpu.VMEM((rb, length, width), F32)] * 4,
            compiler_params=params(52),
            cost_estimate=cost(14 * n_tok * width * width, 40e6),
            name="self_backward",
        )(grad_mid, dprobe, u1, q, k, v, probs, w_a, w_a, w_a, w_a, w_a, g1)
        slabs = [wgrad(tokens, dq), wgrad(tokens, dk), wgrad(tokens, dv), wgrad(attended, gb1)] + cross_slabs
        grad_projected = lax.psum_scatter(dproj, "dp", scatter_dimension=0, tiled=True)
        dwp = lax.dot_general(patches, grad_projected, (((0, 1), (0, 1)), ((), ())), preferred_element_type=F32)
        dwp = dwp.reshape(shards, pr, width)
        vecs = vecs + vec_s
        vecs = vecs.at[5].set(jnp.sum(grad_projected.astype(F32), (0, 1)))
        vecs = jnp.broadcast_to(vecs[None, :nv], (shards, nv, width))
        slabs.append(dwp[:, :sr].reshape(slab).astype(BF))
        slab_shard = lax.psum_scatter(jnp.stack(slabs), AXES, scatter_dimension=1, tiled=True).astype(F32)
        extra_grad = jnp.concatenate([dwp[:, sr:], vecs, wb_rows[:, None]], 1).astype(BF)
        extra_shard = lax.psum_scatter(extra_grad, AXES, scatter_dimension=0, tiled=True)[0].astype(F32)
    patch_shard = jnp.concatenate([slab_shard[7], extra_shard[:tails]], 0)
    patches_grad = lax.dot_general(
        grad_projected, patch_full, (((2,), (1,)), ((), ())), preferred_element_type=F32
    ).astype(BF)
    vg = lax.dynamic_slice(extra_shard, (tails, place * sr), (nv, sr))
    vg = [vg[j] for j in range(nv)]
    wbg = extra_shard[tails + nv, :wr]
    return (
        output, tokens_grad, patches_grad,
        slab_shard[0], vg[0], slab_shard[1], slab_shard[2], vg[1], slab_shard[3], vg[2], vg[3], vg[4],
        patch_shard, vg[5], slab_shard[4], vg[6], slab_shard[5], slab_shard[6], vg[7], ffn_parts[chunks],
        vg[8], vg[9], vg[10], widen_shard, wbg, narrow_shard, vg[11], vg[12], vg[13],
    )


def solution(mesh):
    three, two, one = P(AXES, None, None), P(AXES, None), P(AXES)
    in_specs = (
        three, three, two, one, one, three,
        two, one, two, two, one, two, one, one, one, two, one, two, one, two,
        two, one, two, one, one, one, two, one, two, one, one, one,
    )
    out_specs = (
        three, three, three,
        two, one, two, two, one, two, one, one, one, two, one, two, one, two, two, one, two,
        one, one, one, two, one, two, one, one, one,
    )
    return jax.shard_map(on_device, mesh=mesh, in_specs=in_specs, out_specs=out_specs, check_vma=False)
```

```python
import functools

import jax
import jax.numpy as jnp
from jax import lax
from jax.experimental import pallas as pl
from jax.experimental.pallas import tpu as pltpu
from jax.sharding import PartitionSpec as P

HEADS = 12
AXES = ("dp", "fsdp")
BF = jnp.bfloat16
F32 = jnp.float32
norm_eps = 1e-06
mask_fill = -1000000000.0

WINDOWS = ((0, 0), (128, 64), (384, 0), (512, 64))

ERFC_POLE = 0.3
ERFC_POLY = (
    0.16918935391840687,
    0.17069093065701252,
    0.14852123834149009,
    0.214181489197379,
    -0.09282620690981414,
    0.5449671942862269,
    -0.5097726086693966,
    0.4843018450108595,
    -0.12925324449453648,
)
INV_SQRT2 = 0.7071067811865476
INV_SQRT2PI = 0.3989422804014327


def nn(left, right):
    return lax.dot_general(left, right, (((1,), (0,)), ((), ())), preferred_element_type=F32)


def nt(left, right):
    return lax.dot_general(left, right, (((1,), (1,)), ((), ())), preferred_element_type=F32)


def tn(left, right):
    return lax.dot_general(left, right, (((0,), (0,)), ((), ())), preferred_element_type=F32)


def norm_parts(value):
    mean = jnp.mean(value, -1, keepdims=True)
    centred = value - mean
    spread = jnp.mean(centred * centred, -1, keepdims=True)
    inv = lax.rsqrt(spread + norm_eps)
    return centred * inv, inv


def norm_back(grad, gain, xhat, inv):
    scaled = grad * gain
    first = jnp.mean(scaled, -1, keepdims=True)
    second = jnp.mean(scaled * xhat, -1, keepdims=True)
    return inv * (scaled - first - xhat * second)


def gelu_parts(v):
    z = jnp.abs(v) * INV_SQRT2
    t = 1.0 / (1.0 + ERFC_POLE * z)
    poly = jnp.full_like(t, ERFC_POLY[-1])
    for c in ERFC_POLY[-2::-1]:
        poly = poly * t + c
    bell = jnp.exp(-0.5 * (v * v))
    half = (0.5 * bell) * (t * poly)
    cdf = jnp.where(v >= 0, 1.0 - half, half)
    return v * cdf, cdf + (v * INV_SQRT2PI) * bell


def window(full, index):
    base = WINDOWS[index][0]
    return full[:, base : base + 256]


def column_softmax(scores):
    e = jnp.exp(scores - jnp.max(scores, 0, keepdims=True))
    return (e * (1.0 / jnp.sum(e, 0, keepdims=True))).astype(BF)


def score_grads(probs, grads):
    p = probs.astype(F32)
    return (p * (grads - jnp.sum(grads * p, 0, keepdims=True))).astype(BF)


def stack_heads(full, index):
    base, off = WINDOWS[index]
    win = full[:, base : base + 256]
    lane = lax.broadcasted_iota(jnp.int32, win.shape, 1)
    blocks = []
    for h in range(3):
        lo = off + 64 * h
        blocks.append(jnp.where((lane >= lo) & (lane < lo + 64), win, 0.0))
    return jnp.concatenate(blocks, 0).astype(BF)


def unstack_heads(stacked, index, rows):
    _, off = WINDOWS[index]
    lane = lax.broadcasted_iota(jnp.int32, (rows, 256), 1)
    out = None
    for h in range(3):
        lo = off + 64 * h
        part = jnp.where((lane >= lo) & (lane < lo + 64), stacked[rows * h : rows * (h + 1)], 0.0)
        out = part if out is None else out + part
    return out


def join_windows(parts):
    a, b, c, d = parts
    return jnp.concatenate(
        [
            a[:, :128],
            a[:, 128:] + b[:, :128],
            b[:, 128:],
            c[:, :128],
            c[:, 128:] + d[:, :128],
            d[:, 128:],
        ],
        1,
    )


def self_block(x32, bias, mats, vecs, put, att_s):
    rb, length, width = x32.shape
    n = rb * length
    wq, wk, wv, wo, wc = mats
    qb, vb, ob, g1, b1, pb = vecs
    x32 = x32.reshape(n, width)
    x = x32.astype(BF)
    q_o, k_o, v_o, p_o = put("q"), put("k"), put("v"), put("p")
    q_o[...] = (nn(x, wq()) + qb).reshape(rb, length, width).astype(BF)
    k_o[...] = nn(x, wk()).reshape(rb, length, width).astype(BF)
    v_o[...] = (nn(x, wv()) + vb).reshape(rb, length, width).astype(BF)

    def row(r, carry):
        qr = q_o[r].astype(F32) * 0.125
        kr = k_o[r].astype(F32)
        vr = v_o[r].astype(F32)
        kws = [window(kr, i).astype(BF) for i in range(4)]
        vws = [window(vr, i).astype(BF) for i in range(4)]
        qss = [stack_heads(qr, i) for i in range(4)]
        mask = bias[r]
        scores = [nt(kws[i], qss[i]) + mask for i in range(4)]
        ps = [column_softmax(st) for st in scores]
        outs = [tn(ps[i], vws[i]) for i in range(4)]
        for i in range(4):
            p_o[r, i] = ps[i]
        att_s[r] = join_windows([unstack_heads(outs[i], i, length) for i in range(4)])
        return carry

    lax.fori_loop(0, rb, row, 0)
    att32 = att_s[...]
    put("att")[...] = att32.astype(BF)
    att = att32.reshape(n, width).astype(BF)
    u1 = x32 + nn(att, wo()) + ob
    put("u1")[...] = u1.reshape(rb, length, width)
    xhat, _ = norm_parts(u1)
    first32 = xhat * g1 + b1
    put("first")[...] = first32.reshape(rb, length, width).astype(BF)
    put("probe")[...] = (nn(first32.astype(BF), wc()) + pb).reshape(rb, length, width).astype(BF)


SELF_OUTS = ("q", "k", "v", "p", "att", "u1", "first", "probe")


def self_forward(
    tok, bias, wq, wk, wv, wo, wc, qb, vb, ob, g1, b1, pb, q_o, k_o, v_o, p_o, att_o, u1_o, f_o, pr_o, att_s
):
    outs = dict(zip(SELF_OUTS, (q_o, k_o, v_o, p_o, att_o, u1_o, f_o, pr_o)))
    mats = [lambda ref=ref: ref[...] for ref in (wq, wk, wv, wo, wc)]
    vecs = [ref[...] for ref in (qb, vb, ob, g1, b1, pb)]
    self_block(tok[...].astype(F32), bias, mats, vecs, lambda name: outs[name], att_s)


def cross_forward(starts, order, proj, wk, wv, cb, probe, k_o, v_o, p_o, mix_o, pr_s):
    i = pl.program_id(0)
    points = proj.shape[1]
    length = probe.shape[1]

    @pl.when(i == 0)
    def _():
        pr_s[...] = jnp.zeros_like(pr_s)

    lo, hi = starts[i], starts[i + 1]

    @pl.when(hi > lo)
    def _():
        pr_s[0:points, :] = proj[0]
        pr = pr_s[...]
        k_o[0] = nn(pr, wk[...]).astype(BF)
        v_o[0] = (nn(pr, wv[...]) + cb[...]).astype(BF)

        def row(j, carry):
            r = order[j]
            qr = probe[r].astype(F32) * 0.125
            qss = [stack_heads(qr, g) for g in range(4)]
            scores = [nt(k_o[0, :, WINDOWS[g][0] : WINDOWS[g][0] + 256], qss[g]) for g in range(4)]
            point = lax.broadcasted_iota(jnp.int32, scores[0].shape, 0)
            ps = [column_softmax(jnp.where(point < points, st, -1e30)) for st in scores]
            outs = [tn(ps[g], v_o[0, :, WINDOWS[g][0] : WINDOWS[g][0] + 256]) for g in range(4)]
            for g in range(4):
                p_o[r, g] = ps[g]
            mix_o[r] = join_windows([unstack_heads(outs[g], g, length) for g in range(4)]).astype(BF)
            return carry

        lax.fori_loop(lo, hi, row, 0)


def tail_kernel(
    u1, mix, og, wco, w1, w2, g1, b1, cb, g2, s2, wb, nb, g3, s3,
    out_o, act_o, gi_o, sec_o, gb3_o, gm_o, gb2_o, gc_o, vec_o, wbg_o,
    act_s, gp_s, acc_s,
):
    step = pl.program_id(0)
    rb, length, width = u1.shape
    n = rb * length
    chunks = w1.shape[0]

    @pl.when(step == 0)
    def _():
        vec_o[...] = jnp.zeros_like(vec_o)
        wbg_o[...] = jnp.zeros_like(wbg_o)

    def flat(ref):
        return ref[...].astype(F32).reshape(n, width)

    def fold(value):
        return value.reshape(rb, length, width)

    xhat1, _ = norm_parts(flat(u1))
    first = xhat1 * g1[...] + b1[...]
    u2 = first + nn(flat(mix).astype(BF), wco[...]) + cb[...]
    xhat2, inv2 = norm_parts(u2)
    second = (xhat2 * g2[...] + s2[...]).astype(BF)
    sec32 = second.astype(F32)
    sec_o[...] = fold(sec32).astype(BF)
    total = sec32 + nb[...]
    inner = nn(second, w1[0]) + wb[0]
    for at in range(chunks):
        following = nn(second, w1[at + 1]) + wb[at + 1] if at + 1 < chunks else None
        act, slope = gelu_parts(inner)
        act = act.astype(BF)
        gp_s[at] = slope
        act_o[:, width * at : width * (at + 1)] = act
        total = total + nn(act, w2[at])
        inner = following
    acc_s[...] = total
    xhat3, inv3 = norm_parts(acc_s[...])
    out_o[...] = fold(xhat3 * g3[...] + s3[...]).astype(BF)
    y = flat(og)
    grad_summed = norm_back(y, g3[...], xhat3, inv3)
    gb3 = grad_summed.astype(BF)
    gb3f = gb3.astype(F32)
    gb3_o[...] = fold(gb3f).astype(BF)
    vec_o[0:1] += jnp.sum(y * xhat3, 0, keepdims=True)
    vec_o[1:2] += jnp.sum(y, 0, keepdims=True)
    vec_o[2:3] += jnp.sum(gb3f, 0, keepdims=True)
    total = grad_summed
    back = nt(gb3, w2[0])
    for at in range(chunks):
        following = nt(gb3, w2[at + 1]) if at + 1 < chunks else None
        gi = (back * gp_s[at]).astype(BF)
        gi_o[:, width * at : width * (at + 1)] = gi
        wbg_o[at] += jnp.sum(gi.astype(F32), 0, keepdims=True)
        total = total + nt(gi, w1[at])
        back = following
    acc_s[...] = total
    y2 = acc_s[...].astype(BF).astype(F32)
    gm = norm_back(y2, g2[...], xhat2, inv2)
    gm_o[...] = fold(gm)
    gb2 = gm.astype(BF)
    gb2f = gb2.astype(F32)
    gb2_o[...] = fold(gb2f).astype(BF)
    vec_o[3:4] += jnp.sum(y2 * xhat2, 0, keepdims=True)
    vec_o[4:5] += jnp.sum(y2, 0, keepdims=True)
    vec_o[5:6] += jnp.sum(gb2f, 0, keepdims=True)
    gc_o[...] = fold(nt(gb2, wco[...])).astype(BF)


def cross_backward(
    starts, order, proj, keys, values, wk, wv, probe, grad, probs,
    dpr_o, dproj_o, dwk_o, dwv_o, dcb_o,
    pr_s, dk_s, dv_s, dwk_s, dwv_s,
):
    i = pl.program_id(0)
    points = proj.shape[1]
    length = probe.shape[1]

    @pl.when(i == 0)
    def _():
        pr_s[...] = jnp.zeros_like(pr_s)
        dwk_s[...] = jnp.zeros_like(dwk_s)
        dwv_s[...] = jnp.zeros_like(dwv_s)
        dcb_o[...] = jnp.zeros_like(dcb_o)

    lo, hi = starts[i], starts[i + 1]

    @pl.when(hi == lo)
    def _():
        dproj_o[...] = jnp.zeros_like(dproj_o)

    @pl.when(hi > lo)
    def _():
        dk_s[...] = jnp.zeros_like(dk_s)
        dv_s[...] = jnp.zeros_like(dv_s)

        def row(j, carry):
            r = order[j]
            qr = probe[r].astype(F32) * 0.125
            gr = grad[r].astype(F32)
            gss = [stack_heads(gr, g) for g in range(4)]
            dps = [nt(values[0, :, WINDOWS[g][0] : WINDOWS[g][0] + 256], gss[g]) for g in range(4)]
            qss = [stack_heads(qr, g) for g in range(4)]
            pbs = [probs[r, g] for g in range(4)]
            dvs = [nn(pbs[g], gss[g]) for g in range(4)]
            dss = [score_grads(pbs[g], dps[g]) for g in range(4)]
            dks = [nn(dss[g], qss[g]) for g in range(4)]
            outs = [tn(dss[g], keys[0, :, WINDOWS[g][0] : WINDOWS[g][0] + 256]) for g in range(4)]
            dv_s[...] += join_windows(dvs)
            dk_s[...] += join_windows(dks)
            dpr_o[r] = (join_windows([unstack_heads(outs[g], g, length) for g in range(4)]) * 0.125).astype(BF)
            return carry

        lax.fori_loop(lo, hi, row, 0)
        pr_s[0:points, :] = proj[0]
        pr = pr_s[...]
        dk = dk_s[...].astype(BF)
        dv = dv_s[...].astype(BF)
        dcb_o[0:1] += jnp.sum(dv.astype(F32), 0, keepdims=True)
        dproj = (nt(dk, wk[...]) + nt(dv, wv[...])).astype(BF)
        dproj_o[0] = dproj[0:points]
        dwk_s[...] += tn(pr, dk)
        dwv_s[...] += tn(pr, dv)

    @pl.when(i == pl.num_programs(0) - 1)
    def _():
        dwk_o[...] = dwk_s[...].astype(BF)
        dwv_o[...] = dwv_s[...].astype(BF)


def self_back_block(gm, dpr32, u1, heads, mats, g1, add, temps):
    q, k, v, probs = heads
    wq, wk, wv, wo, wc = mats
    ga_s, dq_s, dk_s, dv_s = temps
    rb, length, width = ga_s.shape
    n = rb * length
    grad_first = gm + nt(dpr32.astype(BF), wc())
    xhat, inv = norm_parts(u1)
    low = norm_back(grad_first, g1, xhat, inv)
    gb1 = low.astype(BF)
    add(3, grad_first * xhat)
    add(4, grad_first)
    add(2, gb1.astype(F32))
    add(6, dpr32)
    ga_s[...] = nt(gb1, wo()).astype(BF).astype(F32).reshape(rb, length, width)

    def row(r, carry):
        qr = q[r].astype(F32) * 0.125
        kr = k[r].astype(F32)
        vr = v[r].astype(F32)
        gr = ga_s[r]
        gss = [stack_heads(gr, i) for i in range(4)]
        vws = [window(vr, i).astype(BF) for i in range(4)]
        dps = [nt(vws[i], gss[i]) for i in range(4)]
        qss = [stack_heads(qr, i) for i in range(4)]
        kws = [window(kr, i).astype(BF) for i in range(4)]
        pbs = [probs[r, i] for i in range(4)]
        dvs = [nn(pbs[i], gss[i]) for i in range(4)]
        dss = [score_grads(pbs[i], dps[i]) for i in range(4)]
        dks = [nn(dss[i], qss[i]) for i in range(4)]
        outs = [tn(dss[i], kws[i]) for i in range(4)]
        dq_s[r] = join_windows([unstack_heads(outs[i], i, length) for i in range(4)]) * 0.125
        dk_s[r] = join_windows(dks)
        dv_s[r] = join_windows(dvs)
        return carry

    lax.fori_loop(0, rb, row, 0)
    dq = dq_s[...].reshape(n, width).astype(BF)
    dk = dk_s[...].reshape(n, width).astype(BF)
    dv = dv_s[...].reshape(n, width).astype(BF)
    add(0, dq.astype(F32))
    add(1, dv.astype(F32))
    total = low + nt(dq, wq()) + nt(dk, wk()) + nt(dv, wv())
    return gb1, dq, dk, dv, total.reshape(rb, length, width).astype(BF)


def self_backward(
    gm, dpr, u1, q, k, v, probs, wq, wk, wv, wo, wc, g1, gb1_o, dq_o, dk_o, dv_o, tg_o, vec_o, *temps
):
    rb, length, width = u1.shape
    n = rb * length

    @pl.when(pl.program_id(0) == 0)
    def _():
        vec_o[...] = jnp.zeros_like(vec_o)

    def add(row, value):
        vec_o[row : row + 1] += jnp.sum(value, 0, keepdims=True)

    def flat(ref):
        return ref[...].astype(F32).reshape(n, width)

    mats = [lambda ref=ref: ref[...] for ref in (wq, wk, wv, wo, wc)]
    *grads, tokens_grad = self_back_block(
        flat(gm), flat(dpr), flat(u1), (q, k, v, probs), mats, g1[...], add, temps
    )
    for ref, value in zip((gb1_o, dq_o, dk_o, dv_o), grads):
        ref[...] = value.astype(F32).reshape(rb, length, width).astype(BF)
    tg_o[...] = tokens_grad


def sds(shape, dtype):
    return jax.ShapeDtypeStruct(shape, dtype)


def whole(shape, *, single=True):
    zeros = (0,) * len(shape)
    mode = pl.Buffered(1) if single else None
    return pl.BlockSpec(shape, lambda i, *_: zeros, pipeline_mode=mode)


def rows_block(shape, rb):
    rest = tuple(shape[1:])
    return pl.BlockSpec((rb,) + rest, lambda i, *_: (i,) + (0,) * len(rest))


def params(mib):
    return pltpu.CompilerParams(
        dimension_semantics=("arbitrary",), vmem_limit_bytes=mib * 1024 * 1024
    )


def cost(flops, bytes_accessed):
    return pl.CostEstimate(flops=int(flops), bytes_accessed=int(bytes_accessed), transcendentals=0)


def my_place():
    dp, fs = lax.axis_index("dp"), lax.axis_index("fsdp")
    return dp // 2, dp % 2, fs // 2, fs % 2


def device_at(z, y, x, c):
    return (z * 2 + y, x * 2 + c)


def meet(z, y, x, c):
    sem = pltpu.get_barrier_semaphore()
    others = [device_at((z + k) % 4, y, x, c) for k in (1, 2, 3)]
    others += [device_at(z, 1 - y, x, c), device_at(z, y, 1 - x, c), device_at(z, y, x, 1 - c)]
    for other in others:
        pl.semaphore_signal(sem, inc=1, device_id=other, device_id_type=pl.DeviceIdType.MESH)
    pl.semaphore_wait(sem, len(others))


class Copies:
    def __init__(self, send, recv, local):
        self.send, self.recv, self.local = send, recv, local
        self.far = self.near = 0
        self.sent = []

    def prepare(self, src, dst, device):
        i = self.far
        self.far += 1
        return pltpu.make_async_remote_copy(
            src_ref=src, dst_ref=dst, send_sem=self.send.at[i], recv_sem=self.recv.at[i],
            device_id=device, device_id_type=pl.DeviceIdType.MESH,
        )

    def remote(self, src, dst, device):
        copy = self.prepare(src, dst, device)
        copy.start()
        return copy

    def here(self, src, dst):
        i = self.near
        self.near += 1
        copy = pltpu.make_async_copy(src, dst, self.local.at[i])
        copy.start()
        return copy


def arrived(copies):
    for copy in copies:
        copy.wait()


def drive(jobs, order):
    for name in order:
        next(jobs[name], None)
    for job in jobs.values():
        for _ in job:
            pass


PATCH, EXTRA, QUERY, KEY, VALUE, OUT, CQ, CK, W1 = range(9)
CV, CO = 12, 13


FRONT_ORDER = (
    "P", "Q", "P", "P", "Q", "P", "Q", "R", "P", "P", "P", "F", "Q", "P", "Q", "Q", "F", "P",
    "weights", "F", "i0", "i1", "Q", "F", "i0", "i3", "G", "F", "R", "i1", "i3", "Q", "G", "G",
    "i0", "i0", "F", "Q", "self", "i2", "i3", "G", "self", "R", "i2", "F", "G", "self", "i3", "i1",
    "G", "self", "G", "R", "R", "i1", "F", "i2", "self", "R", "R", "G", "i2", "R",
)
BACK_ORDER = (
    "E", "p0", "S", "p1", "E", "S", "p0", "p2", "S", "S", "p1", "S", "D1", "L1", "p0", "p0", "p3",
    "p1", "D2", "p2", "L1", "p2", "p0", "p1", "p3", "L2", "p1", "E", "p2", "p3", "L2", "p2", "L1",
    "p3", "L2", "p3", "E", "V1", "L2", "V1", "V2", "L1", "V2", "V1", "V2", "L2", "E", "V1", "L1",
    "V2", "V1", "S", "V2",
)


def front_kernel(
    parts, tails, nv, rb, w_in, n_in, pat, tok, bias, w_out, n_out, p_out, q_o, k_o, v_o, pr_o, att_o, u1_o, f_o, prb_o, vec_o,
    pw, ex, wm, proj_s, q_s, k_s, v_s, pr_s, att_b, u1_s, f_s, prb_s, att_s, send, recv, local,
):
    z, y, x, c = my_place()
    meet(z, y, x, c)
    copies = Copies(send, recv, local)
    rows, length, width = tok.shape
    images = pat.shape[0]

    inner = (z + 1) % 4 >= 2
    partner = z + 1 - 2 * (z % 2)
    across = 3 - z
    ours, theirs = 2 * (z // 2), 2 - 2 * (z // 2)

    def along_z(source, view, tell, local):
        step = copies.remote(source, view(z, 0), device_at(partner, y, x, c))
        tell("own")
        yield
        step.wait()
        if local is not None:
            local.wait()
        tell("partner")
        middle = copies.prepare(view(ours, 2), view(ours, 2), device_at(across, y, x, c))
        outward = copies.prepare(view(theirs, 2), view(theirs, 2), device_at(partner, y, x, c))

        @pl.when(inner)
        def _():
            middle.start()

        yield

        @pl.when(inner)
        def _():
            middle.wait()
            outward.start()
            tell("inner")

        yield

        @pl.when(jnp.logical_not(inner))
        def _():
            outward.wait_recv()
            tell("outer")

        copies.sent.append((inner, outward))
        yield

    def exchanged(source, view, local):
        own = copies.prepare(source, view(z, 0), device_at(z, 1 - y, x, c))
        second = copies.prepare(view(partner, 0), view(partner, 0), device_at(z, 1 - y, x, c))
        third = copies.prepare(view(theirs, 2), view(theirs, 2), device_at(z, 1 - y, x, c))
        start = {"own": own, "partner": second, "inner": third, "outer": third}
        return along_z(source, view, lambda which: start[which].start(), local), (own, second, third)

    def slabs(source, out):
        every = slice(None)

        def view(at, many):
            return out(pl.ds(at, many) if many else at, y, x, c)

        def plane(at, many):
            return out(pl.ds(at, many) if many else at, every, x, c)

        local = copies.here(source, view(z, 0))
        moving, (own, second, third) = exchanged(source, view, None)
        next(moving)
        yield
        own.wait()
        local.wait()
        steps = [copies.remote(plane(z, 0), plane(z, 0), device_at(z, y, 1 - x, c))]
        yield
        for _ in range(3):
            next(moving)
            yield
        second.wait()
        steps.append(copies.remote(plane(partner, 0), plane(partner, 0), device_at(z, y, 1 - x, c)))
        yield
        third.wait()
        steps.append(copies.remote(plane(theirs, 2), plane(theirs, 2), device_at(z, y, 1 - x, c)))
        yield
        arrived(steps)
        half = out(every, every, every, c)
        step = copies.remote(half, half, device_at(z, y, x, 1 - c))
        yield
        step.wait()

    def patch_weights():
        rest = pw.shape[4] - tails
        arrived(
            [
                copies.here(w_out.at[PATCH], pw.at[:, :, :, :, 0:rest]),
                copies.here(w_out.at[EXTRA, :, :, :, :, 0:tails], pw.at[:, :, :, :, rest:]),
                copies.here(w_out.at[EXTRA], ex),
            ]
        )
        total = jnp.zeros(ex.shape[4:], F32)
        for zz in range(4):
            for yy in range(2):
                for xx in range(2):
                    for cc in range(2):
                        total = total + ex[zz, yy, xx, cc].astype(F32)
        vec_o[...] = total
        yield

    def vec(j):
        return vec_o[tails + j : tails + j + 1, :]

    def image(i):
        full = pw[...].reshape(pat.shape[2], width)
        proj_s[i] = (nn(pat[i], full) + vec(5)).astype(BF)

        def view(at, many):
            return p_out.at[pl.ds(at, many) if many else at, y, i]

        moving, steps = exchanged(proj_s.at[i], view, copies.here(proj_s.at[i], view(z, 0)))
        yield from moving
        arrived(steps)

    def attention():
        arrived([copies.here(w_out.at[QUERY + m], wm.at[m]) for m in range(5)])
        yield
        scratch = dict(zip(SELF_OUTS, (q_s, k_s, v_s, pr_s, att_b, u1_s, f_s, prb_s)))
        finals = dict(zip(SELF_OUTS, (q_o, k_o, v_o, pr_o, att_o, u1_o, f_o, prb_o)))
        mats = [lambda m=m: wm[m].reshape(width, width) for m in range(5)]
        outgoing = []
        for b in range(rows // rb):
            pick = pl.ds(b * rb, rb)
            self_block(
                tok[pick].astype(F32), bias.at[pick], mats, [vec(j) for j in (0, 1, 2, 3, 4, 6)],
                lambda name: scratch[name].at[pick], att_s,
            )
            outgoing += [copies.here(scratch[name].at[pick], finals[name].at[pick]) for name in SELF_OUTS]
            yield
        arrived(outgoing)

    def stacked(lo, n):
        pick = pl.ds(lo, n)
        return slabs(w_in.at[pick], lambda *at: w_out.at[(pick,) + at])

    jobs = {name: stacked(lo, n) for name, (lo, n) in parts.items()}
    jobs["G"] = slabs(n_in, lambda *at: n_out.at[at])
    jobs["weights"] = patch_weights()
    for i in range(images):
        jobs["i%d" % i] = image(i)
    jobs["self"] = attention()
    drive(jobs, FRONT_ORDER)
    for when, copy in copies.sent:

        @pl.when(when)
        def _(copy=copy):
            copy.wait_send()


def back_kernel(
    rb, tails, w_in, p_in, gm, dpr, u1, q, k, v, probs, tok, att, w_all, pat, g1, vt_in, wb_in,
    w_out, p_out, tg_o,
    wm, gm_s, dpr_s, u1_s, q_s, k_s, v_s, p_s, ga_t, dq_t, dk_t, dv_t, gb1_f, dq_f, dk_f, dv_f, tg_s, vec_s,
    acc, lw, pv, rc, rx, ry, rz, pacc, pry, prz, send, recv, local,
):
    z, y, x, c = my_place()
    meet(z, y, x, c)
    copies = Copies(send, recv, local)
    rows, length, width = gm.shape
    images = pat.shape[0]
    sr = w_out.shape[1]

    def up(ref, *at):
        return ref[at].astype(F32)

    def slabs(lo, n, sibling, own, base, own_c):
        pick = pl.ds(lo, n)
        last = (c,) if own_c else ()

        def cell(s, zz, yy, xx):
            return (s - base, zz, yy, xx) + last

        def view(zz, yy, xx):
            return own.at[(pl.ds(lo - base, n), zz, yy, xx) + last]

        every = slice(None)
        step = copies.remote(sibling, rc.at[pick], device_at(z, y, x, 1 - c))
        yield
        step.wait()

        def add_x(i, carry):
            s, zz = lo + i // 4, i % 4
            for yy in range(2):
                at = cell(s, zz, yy, 1 - x)
                own[at] = (up(own, *at) + up(rc, s, zz, yy, 1 - x)).astype(BF)
            return carry

        lax.fori_loop(0, 4 * n, add_x, 0)
        step = copies.remote(view(every, every, 1 - x), rx.at[pick], device_at(z, y, 1 - x, c))
        yield
        step.wait()

        def add_y(i, carry):
            s, zz = lo + i // 4, i % 4
            at = cell(s, zz, 1 - y, x)
            own[at] = (up(own, *at) + up(rc, s, zz, 1 - y, x) + up(rx, s, zz, 1 - y)).astype(BF)
            return carry

        lax.fori_loop(0, 4 * n, add_y, 0)
        step = copies.remote(view(every, 1 - y, x), ry.at[pick], device_at(z, 1 - y, x, c))
        yield
        step.wait()
        steps = []
        for hop in (1, 3, 2):
            zz = (z + hop) % 4

            def add_z(i, carry):
                s = lo + i
                at = cell(s, zz, y, x)
                own[at] = (up(own, *at) + up(rc, s, zz, y, x) + up(rx, s, zz, y) + up(ry, s, zz)).astype(BF)
                return carry

            lax.fori_loop(0, n, add_z, 0)
            steps.append(copies.remote(view(zz, y, x), rz.at[hop - 1, pick], device_at(zz, y, x, c)))
        yield
        arrived(steps)

        def add_last(i, carry):
            s = lo + i
            w_out[s] = (
                up(own, *cell(s, z, y, x)) + up(rc, s, z, y, x) + up(rx, s, z, y) + up(ry, s, z)
                + up(rz, 0, s) + up(rz, 1, s) + up(rz, 2, s)
            )
            return carry

        lax.fori_loop(0, n, add_last, 0)
        yield

    def early():
        own = copies.here(w_in.at[:, :, :, :, c], acc)
        job = slabs(4, 3, w_in.at[:, :, :, :, 1 - c], acc, 4, False)
        next(job)
        yield
        own.wait()
        yield from job

    inner = (z + 1) % 4 >= 2
    outer = jnp.logical_not(inner)
    partner = z + 1 - 2 * (z % 2)
    ours, theirs = 2 * (z // 2), 2 - 2 * (z // 2)

    def image(i):
        mine = copies.here(p_in.at[:, y, i], pacc.at[i])
        step = copies.remote(p_in.at[:, 1 - y, i], pry.at[i], device_at(z, 1 - y, x, c))
        yield
        mine.wait()
        step.wait()
        pair = pacc.at[i, pl.ds(theirs, 2)]
        inward = copies.prepare(pair, prz.at[i, pl.ds(0, 2)], device_at(partner, y, x, c))
        middle = copies.prepare(pair, prz.at[i, pl.ds(2, 2)], device_at(3 - z, y, x, c))
        swap = copies.prepare(pacc.at[i, partner], prz.at[i, 4], device_at(partner, y, x, c))

        def own(zz):
            return up(pacc, i, zz) + up(pry, i, zz)

        @pl.when(outer)
        def _():
            for at in range(2):
                pacc[i, theirs + at] = own(theirs + at).astype(BF)
            inward.start()
            pacc[i, partner] = own(partner).astype(BF)
            swap.start()

        yield

        @pl.when(inner)
        def _():
            inward.wait_recv()
            for at in range(2):
                pacc[i, theirs + at] = (own(theirs + at) + up(prz, i, at)).astype(BF)
            middle.start()

        yield

        @pl.when(inner)
        def _():
            middle.wait()
            pacc[i, partner] = (own(partner) + up(prz, i, 2 + partner - ours)).astype(BF)
            swap.start()

        yield
        swap.wait()

        @pl.when(inner)
        def _():
            p_out[i] = (own(z) + up(prz, i, 2 + z - ours) + up(prz, i, 4)).astype(BF)

        @pl.when(outer)
        def _():
            inward.wait_send()
            p_out[i] = (own(z) + up(prz, i, 4)).astype(BF)

        yield

    def attention():
        weights = [
            copies.here(w_all.at[m], wm.at[pl.ds(width * at, width)])
            for at, m in enumerate((QUERY, KEY, VALUE, OUT, CQ))
        ]
        vec_s[...] = vt_in[...]
        mats = [lambda at=at: wm[pl.ds(width * at, width)] for at in range(5)]
        streams = ((gm, gm_s), (dpr, dpr_s), (u1, u1_s), (q, q_s), (k, k_s), (v, v_s), (probs, p_s))
        size = gm_s.shape[0]
        n = rb * length

        def add(row, value):
            vec_s[row : row + 1] += jnp.sum(value, 0, keepdims=True)

        leaving = None
        for stage in range(rows // size):
            coming = [copies.here(src.at[pl.ds(stage * size, size)], dst) for src, dst in streams]
            arrived(weights + coming)
            weights = []
            if leaving is not None:
                leaving.wait()

            def block(b, carry):
                pick = pl.ds(b * rb, rb)

                def flat(ref):
                    return ref[pick].astype(F32).reshape(n, width)

                heads = tuple(ref.at[pick] for ref in (q_s, k_s, v_s, p_s))
                *grads, tokens_grad = self_back_block(
                    flat(gm_s), flat(dpr_s), flat(u1_s), heads, mats, g1[...], add, (ga_t, dq_t, dk_t, dv_t)
                )
                at = pl.ds(pl.multiple_of(stage * size * length + b * n, n), n)
                for ref, value in zip((gb1_f, dq_f, dk_f, dv_f), grads):
                    ref[at] = value
                tg_s[pick] = tokens_grad
                return carry

            lax.fori_loop(0, size // rb, block, 0)
            leaving = copies.here(tg_s, tg_o.at[pl.ds(stage * size, size)])
            yield
        leaving.wait()
        count = rows * length
        arrived(
            [
                copies.here(tok, wm.at[pl.ds(0, count)]),
                copies.here(att, wm.at[pl.ds(count, count)]),
            ]
        )
        yield

    def gradient(pairs):
        count = rows * length
        for m, first, right in pairs:
            left = wm[pl.ds(first * count, count)]
            lw[m] = tn(left, right[...]).reshape(lw.shape[1:]).astype(BF)
        yield

    def late(lo):
        yield from slabs(lo, 2, lw.at[pl.ds(lo, 2), :, :, :, 1 - c], lw, 0, True)

    def patch_sums(first):
        pwidth = pat.shape[2]
        rows_each = pwidth // 32
        step = 128
        bias = jnp.sum(p_out[0].astype(F32), 0, keepdims=True)
        for i in range(1, images):
            bias = bias + jnp.sum(p_out[i].astype(F32), 0, keepdims=True)
        vec_s[5:6] = bias

        for lo in range(0, pwidth, step):
            total = tn(pat[0, :, lo : lo + step], p_out[0])
            for i in range(1, images):
                total = total + tn(pat[i, :, lo : lo + step], p_out[i])
            for at in range(step // rows_each):
                d = lo // rows_each + at
                zz, yy, xx, cc = d // 8, (d // 4) % 2, (d // 2) % 2, d % 2
                part = total[at * rows_each : (at + 1) * rows_each]
                pv[0, zz, yy, xx, cc] = part[:sr].astype(BF)
                vecs = vec_s[...]
                row = lax.broadcasted_iota(jnp.int32, vecs.shape, 0)
                vecs = jnp.where(row == vecs.shape[0] - 2, wb_in[d : d + 1], vecs)
                pv[1, zz, yy, xx, cc] = jnp.concatenate([part[sr:], vecs], 0).astype(BF)

        yield from slabs(first, 1, pv.at[pl.ds(0, 1), :, :, :, 1 - c], pv, first, True)

    def second_patch(first):
        yield from slabs(first, 1, pv.at[pl.ds(1, 1), :, :, :, 1 - c], pv, first - 1, True)

    jobs = {"p%d" % i: image(i) for i in range(images)}
    jobs["E"] = early()
    jobs["S"] = attention()
    jobs["D1"] = gradient(((0, 0, dq_f), (1, 0, dk_f)))
    jobs["D2"] = gradient(((2, 0, dv_f), (3, 1, gb1_f)))
    jobs["L1"], jobs["L2"] = late(0), late(2)
    jobs["V1"], jobs["V2"] = patch_sums(7), second_patch(8)
    drive(jobs, BACK_ORDER)


def front(slabs, narrow, patches, tokens, bias, tails, nv):
    n, sr, width = slabs.shape
    images, points, pwidth = patches.shape
    rows, length, _ = tokens.shape
    rb = 8 if rows % 8 == 0 else 1
    parts = {"P": (PATCH, 2), "Q": (QUERY, 6), "F": (W1, 4), "R": (CV, 2)}
    nr = narrow.shape[0]
    remote = 10 * (len(parts) + 1) + 6 * images
    near = len(parts) + 1 + images + 3 + 5 + len(SELF_OUTS) * (rows // rb)
    tok_sh = (rows, length, width)
    probs = (rows, 4, length, 3 * length)
    kept = [sds(tok_sh, BF), sds(tok_sh, BF), sds(tok_sh, BF), sds(probs, BF), sds(tok_sh, BF), sds(tok_sh, F32), sds(tok_sh, BF), sds(tok_sh, BF)]
    hbm = pl.BlockSpec(memory_space=pl.ANY)
    vmem = pl.BlockSpec(memory_space=pltpu.VMEM)
    w_all, n_all, p_all, *rest = pl.pallas_call(
        functools.partial(front_kernel, parts, tails, nv, rb),
        in_specs=[hbm, hbm, vmem, vmem, vmem],
        out_specs=[hbm] * 11 + [vmem],
        out_shape=[
            sds((n, 4, 2, 2, 2, sr, width), BF), sds((4, 2, 2, 2, nr, width), BF),
            sds((4, 2, images, points, width), BF), *kept, sds((sr, width), F32),
        ],
        scratch_shapes=[
            pltpu.VMEM((4, 2, 2, 2, pwidth // 32, width), BF),
            pltpu.VMEM((4, 2, 2, 2, sr, width), BF),
            pltpu.VMEM((5, 4, 2, 2, 2, sr, width), BF),
            pltpu.VMEM((images, points, width), BF),
            *[pltpu.VMEM(item.shape, item.dtype) for item in kept],
            pltpu.VMEM((rb, length, width), F32),
            pltpu.SemaphoreType.DMA((remote,)),
            pltpu.SemaphoreType.DMA((remote,)),
            pltpu.SemaphoreType.DMA((near,)),
        ],
        compiler_params=pltpu.CompilerParams(
            collective_id=0, has_side_effects=True, vmem_limit_bytes=58 * 1024 * 1024
        ),
        name="front",
    )(slabs, narrow, patches, tokens, bias)
    return w_all.reshape(n, 32 * sr, width), n_all.reshape(32 * nr, width), p_all.reshape(8 * images, points, width), rest[:8], rest[8]


def back(slabs, grads, streams, tok, att, w_all, patches, g1, vecs, wb_rows, tails):
    n, full, width = slabs.shape
    sr = full // 32
    total, points, _ = grads.shape
    images, _, pwidth = patches.shape
    rows, length, _ = streams[0].shape
    m = n + 6
    size, rb = 8, 4
    hbm = pl.BlockSpec(memory_space=pl.ANY)
    vmem = pl.BlockSpec(memory_space=pltpu.VMEM)
    remote = 6 * 5 + 4 * images
    near = 1 + images + 5 + 8 * (rows // size) + 2
    part = (sr, width)
    w_shard, p_shard, tokens_grad = pl.pallas_call(
        functools.partial(back_kernel, rb, tails),
        in_specs=[hbm] * 12 + [vmem] * 4,
        out_specs=[vmem, vmem, hbm],
        out_shape=[sds((m, sr, width), F32), sds((images, points, width), BF), sds((rows, length, width), BF)],
        scratch_shapes=[
            pltpu.VMEM((5 * width, width), BF),
            *[pltpu.VMEM((size,) + item.shape[1:], item.dtype) for item in streams],
            *[pltpu.VMEM((rb, length, width), F32)] * 4,
            *[pltpu.VMEM((rows * length, width), BF)] * 4,
            pltpu.VMEM((size, length, width), BF),
            pltpu.VMEM(vecs.shape, F32),
            pltpu.VMEM((n, 4, 2, 2) + part, BF),
            pltpu.VMEM((4, 4, 2, 2, 2) + part, BF),
            pltpu.VMEM((2, 4, 2, 2, 2) + part, BF),
            pltpu.VMEM((m, 4, 2, 2) + part, BF),
            pltpu.VMEM((m, 4, 2) + part, BF),
            pltpu.VMEM((m, 4) + part, BF),
            pltpu.VMEM((3, m) + part, BF),
            pltpu.VMEM((images, 4, points, width), BF),
            pltpu.VMEM((images, 4, points, width), BF),
            pltpu.VMEM((images, 5, points, width), BF),
            pltpu.SemaphoreType.DMA((remote,)),
            pltpu.SemaphoreType.DMA((remote,)),
            pltpu.SemaphoreType.DMA((near,)),
        ],
        compiler_params=pltpu.CompilerParams(
            collective_id=1, has_side_effects=True, vmem_limit_bytes=62 * 1024 * 1024
        ),
        name="back",
    )(
        slabs.reshape(n, 4, 2, 2, 2, sr, width), grads.reshape(4, 2, images, points, width), *streams,
        tok, att, w_all, patches, g1, vecs, wb_rows,
    )
    return w_shard, p_shard, tokens_grad


def pack_kernel(chunks, patch, extra, *refs):
    *mats, out = refs
    sr, width = extra.shape
    out[PATCH] = patch[0:sr]
    out[EXTRA] = extra[...]
    for at, ref in enumerate(mats[: W1 - QUERY]):
        out[QUERY + at] = ref[...]
    for at in range(chunks):
        out[W1 + at] = mats[W1 - QUERY][:, width * at : width * (at + 1)]
    for at, ref in enumerate(mats[W1 - QUERY + 1 :]):
        out[CV + at] = ref[...]


def pack(patch, extra, before, widen, after):
    sr, width = extra.shape
    chunks = widen.shape[1] // width
    count = 2 + len(before) + chunks + len(after)
    vmem = pl.BlockSpec(memory_space=pltpu.VMEM)
    return pl.pallas_call(
        functools.partial(pack_kernel, chunks),
        in_specs=[vmem] * (3 + len(before) + len(after)),
        out_specs=vmem,
        out_shape=sds((count, sr, width), BF),
        name="pack",
    )(patch, extra, *before, widen, *after)


def gather(value, axis):
    return lax.all_gather(value, AXES, axis=axis, tiled=True)


def on_device(
    tokens, patches, segments, owner, image_slot, out_grad,
    self_query, query_bias, self_key, self_value, value_bias, self_output, output_bias,
    first_gain, first_norm_bias, patch_proj, patch_bias, cross_query, probe_bias, cross_key,
    cross_value, content_bias, cross_output, cross_bias, second_gain, second_shift,
    widen_weight, widen_bias, narrow_weight, narrow_bias, third_gain, third_shift,
):
    rows, length, width = tokens.shape
    images, points, pwidth = patches.shape
    groups = lax.axis_size("dp")
    shards = groups * lax.axis_size("fsdp")
    total_images = groups * images
    hidden = widen_weight.shape[1]
    chunks = hidden // width
    sr = self_query.shape[0]
    wr = widen_bias.shape[0]

    place = lax.axis_index("dp") * lax.axis_size("fsdp") + lax.axis_index("fsdp")
    vec_list = (
        query_bias, value_bias, output_bias, first_gain, first_norm_bias, patch_bias, probe_bias,
        content_bias, cross_bias, second_gain, second_shift, narrow_bias, third_gain, third_shift,
    )
    nv = len(vec_list)
    pr = patch_proj.shape[0]
    tails = pr - sr
    lane_block = jnp.arange(width, dtype=jnp.int32)[None, :] // sr
    vec_rows = jnp.where(lane_block == place, jnp.tile(jnp.stack(vec_list), (1, shards)), jnp.zeros((), BF))
    wb_row = jnp.pad(widen_bias, (0, width - wr))[None]
    extra = jnp.concatenate([patch_proj[sr:], vec_rows, wb_row], 0)
    er = max(sr, extra.shape[0])
    own_rows = er == sr and groups == 8 and shards == 32
    extra = jnp.pad(extra, ((0, er - extra.shape[0]), (0, 0)))
    slabs_in = pack(
        patch_proj, extra[:sr], (self_query, self_key, self_value, self_output, cross_query, cross_key),
        widen_weight, (cross_value, cross_output),
    )

    image = owner * images + image_slot
    idx = jnp.arange(rows, dtype=jnp.int32)
    before = (image[None, :] < image[:, None]) | ((image[None, :] == image[:, None]) & (idx[None, :] < idx[:, None]))
    rank = jnp.sum(before.astype(jnp.int32), 1)
    order = jnp.sum(jnp.where(rank[:, None] == idx[None, :], idx[:, None], 0), 0).astype(jnp.int32)
    starts = jnp.sum((image[None, :] < jnp.arange(total_images + 1, dtype=jnp.int32)[:, None]).astype(jnp.int32), 1)

    same = segments[:, :, None] == segments[:, None, :]
    bias = jnp.where(same, 0.0, mask_fill).astype(F32)
    bias = jnp.concatenate([bias, bias, bias], 2)

    rb = 8 if rows % 8 == 0 else 1
    grid = (rows // rb,)
    tok_sh = (rows, length, width)
    slab = (width, width)

    def wspec(j):
        return pl.BlockSpec((None, width, width), lambda i, *_: (j, 0, 0), pipeline_mode=pl.Buffered(1))

    vspec = whole((1, width))
    tb = rows_block(tok_sh, rb)
    self_p = (rows, 4, length, 3 * length)
    if own_rows:
        w_a, narrow_all, proj_all, kept, vec_all = front(
            slabs_in, narrow_weight, patches, tokens, bias, tails, nv
        )
        vec_all = vec_all[tails : tails + nv]
        extra_all = w_a[EXTRA].reshape(shards, er, width)
    else:
        w_a = gather(slabs_in, 1)
        narrow_all = gather(narrow_weight, 0)
        extra_all = gather(extra, 0).reshape(shards, er, width)
        vec_all = jnp.sum(extra_all[:, tails : tails + nv].astype(F32), 0)
    (qb, vb, ob, g1, b1, pab, prb, cob, crb, g2, s2, nab, g3, s3) = [vec_all[j : j + 1] for j in range(nv)]
    wb = extra_all[:, tails + nv, :wr].astype(F32).reshape(chunks, 1, width)
    narrow_all = narrow_all.reshape(chunks, width, width)
    patch_full = jnp.concatenate([w_a[PATCH].reshape(shards, sr, width), extra_all[:, :tails]], 1)
    patch_full = patch_full.reshape(shards * pr, width)
    if not own_rows:
        projected = lax.dot_general(patches, patch_full, (((2,), (0,)), ((), ())), preferred_element_type=F32)
        proj_all = lax.all_gather((projected + pab).astype(BF), "dp", axis=0, tiled=True)
        kept = pl.pallas_call(
            self_forward,
            grid=grid,
            in_specs=[tb, rows_block((rows, length, 3 * length), rb)]
            + [wspec(j) for j in (QUERY, KEY, VALUE, OUT, CQ)]
            + [vspec] * 6,
            out_specs=[tb, tb, tb, rows_block(self_p, rb), tb, tb, tb, tb],
            out_shape=[
                sds(tok_sh, BF), sds(tok_sh, BF), sds(tok_sh, BF), sds(self_p, BF),
                sds(tok_sh, BF), sds(tok_sh, F32), sds(tok_sh, BF), sds(tok_sh, BF),
            ],
            scratch_shapes=[pltpu.VMEM((rb, length, width), F32)],
            compiler_params=params(48),
            cost_estimate=cost(11 * rows * length * width * width, 30e6),
            name="self_forward",
        )(tokens, bias, w_a, w_a, w_a, w_a, w_a, qb, vb, ob, g1, b1, prb)
    q, k, v, probs, attended, u1, first_low, probe = kept

    padded = -(-points // 16) * 16
    kv_sh = (total_images, padded, width)
    cross_p = (rows, 4, padded, 3 * length)
    img_spec = pl.BlockSpec((1, points, width), lambda i, *_: (i, 0, 0))
    kv_spec = pl.BlockSpec((1, padded, width), lambda i, *_: (i, 0, 0))
    image_keys, image_values, cprobs, mixed = pl.pallas_call(
        cross_forward,
        grid_spec=pltpu.PrefetchScalarGridSpec(
            num_scalar_prefetch=2,
            grid=(total_images,),
            in_specs=[img_spec, wspec(CK), wspec(CV), vspec, whole(tok_sh)],
            out_specs=[kv_spec, kv_spec, whole(cross_p), whole(tok_sh)],
            scratch_shapes=[pltpu.VMEM((padded, width), BF)],
        ),
        out_shape=[sds(kv_sh, BF), sds(kv_sh, BF), sds(cross_p, BF), sds(tok_sh, BF)],
        compiler_params=params(48),
        cost_estimate=cost(4 * total_images * points * width * width, 40e6),
        name="cross_forward",
    )(starts, order, proj_all, w_a, w_a, cob, probe)

    w1_spec = pl.BlockSpec(
        (chunks, width, width), lambda i, *_: (W1 // chunks, 0, 0), pipeline_mode=pl.Buffered(1)
    )
    n_tok = rows * length
    hid_sh = (n_tok, hidden)
    hid_spec = pl.BlockSpec((rb * length, hidden), lambda i, *_: (i, 0))
    (output, active, grad_inner, second, gb3, grad_mid, gb2, grad_crossed, vec_t, wb_grad) = pl.pallas_call(
        tail_kernel,
        grid=grid,
        in_specs=[tb, tb, tb, wspec(CO), w1_spec, whole((chunks, width, width))]
        + [vspec] * 5
        + [whole((chunks, 1, width))]
        + [vspec] * 3,
        out_specs=[tb, hid_spec, hid_spec, tb, tb, tb, tb, tb, whole((8, width)), whole((chunks, 1, width))],
        out_shape=[
            sds(tok_sh, BF), sds(hid_sh, BF), sds(hid_sh, BF), sds(tok_sh, BF), sds(tok_sh, BF),
            sds(tok_sh, F32), sds(tok_sh, BF), sds(tok_sh, BF), sds((8, width), F32), sds((chunks, 1, width), F32),
        ],
        scratch_shapes=[
            pltpu.VMEM((8, 128), BF),
            pltpu.VMEM((chunks, rb * length, width), F32),
            pltpu.VMEM((rb * length, width), F32),
        ],
        compiler_params=params(56),
        cost_estimate=cost(18 * n_tok * width * width + 8 * n_tok * width * hidden, 50e6),
        name="tail",
    )(u1, mixed, out_grad, w_a, w_a, narrow_all, g1, b1, crb, g2, s2, wb, nab, g3, s3)

    dprobe, dproj, dwk, dwv, dcb = pl.pallas_call(
        cross_backward,
        grid_spec=pltpu.PrefetchScalarGridSpec(
            num_scalar_prefetch=2,
            grid=(total_images,),
            in_specs=[img_spec, kv_spec, kv_spec, wspec(CK), wspec(CV), whole(tok_sh), whole(tok_sh), whole(cross_p)],
            out_specs=[whole(tok_sh), img_spec, whole(slab), whole(slab), whole((8, width))],
            scratch_shapes=[
                pltpu.VMEM((padded, width), BF),
                pltpu.VMEM((padded, width), F32),
                pltpu.VMEM((padded, width), F32),
                pltpu.VMEM((width, width), F32),
                pltpu.VMEM((width, width), F32),
            ],
        ),
        out_shape=[sds(tok_sh, BF), sds((total_images, points, width), BF), sds(slab, BF), sds(slab, BF), sds((8, width), F32)],
        compiler_params=params(56),
        cost_estimate=cost(8 * total_images * points * width * width, 50e6),
        name="cross_backward",
    )(starts, order, proj_all, image_keys, image_values, w_a, w_a, probe, grad_crossed, cprobs)

    def wgrad(left, right):
        return tn(left.reshape(n_tok, width), right.reshape(n_tok, width)).astype(BF)

    ffn = [wgrad(second, grad_inner[:, width * at : width * (at + 1)]).reshape(shards, sr, width) for at in range(chunks)]
    ffn.append(wgrad(mixed, gb2).reshape(shards, sr, width))
    narrow_grad = [wgrad(active[:, width * at : width * (at + 1)], gb3).reshape(shards // chunks, wr, width) for at in range(chunks)]
    ffn.append(jnp.concatenate(narrow_grad))
    ffn_shard = lax.psum_scatter(
        jnp.concatenate(ffn, 1).reshape(-1, width), AXES, scatter_dimension=0, tiled=True
    ).astype(F32)
    ffn_parts = [ffn_shard[sr * at : sr * (at + 1)] for at in range(chunks + 1)]
    widen_shard = jnp.concatenate(ffn_parts[:chunks], 1)
    narrow_shard = ffn_shard[sr * (chunks + 1) :]

    zero = jnp.zeros((1, width), F32)
    vecs = jnp.concatenate(
        [zero, zero, zero, zero, zero, zero, zero, dcb[0:1]]
        + [vec_t[5:6], vec_t[3:4], vec_t[4:5], vec_t[2:3], vec_t[0:1], vec_t[1:2], zero, zero]
    )
    wb_rows = wb_grad.reshape(shards, wr)
    wb_rows = jnp.pad(wb_rows, ((0, 0), (0, width - wr)))
    cross_slabs = [wgrad(first_low, dprobe), dwk, dwv]
    streams = (grad_mid, dprobe, u1, q, k, v, probs)
    if own_rows:
        slab_shard, grad_projected, tokens_grad = back(
            jnp.stack(cross_slabs), dproj, streams, tokens.reshape(n_tok, width),
            attended.reshape(n_tok, width), w_a, patches, g1, vecs, wb_rows, tails,
        )
        extra_shard = slab_shard[8]
    else:
        gb1, dq, dk, dv, tokens_grad, vec_s = pl.pallas_call(
            self_backward,
            grid=grid,
            in_specs=[tb, tb, tb, tb, tb, tb, rows_block(self_p, rb)]
            + [wspec(j) for j in (QUERY, KEY, VALUE, OUT, CQ)]
            + [vspec],
            out_specs=[tb, tb, tb, tb, tb, whole((16, width))],
            out_shape=[sds(tok_sh, BF)] * 5 + [sds((16, width), F32)],
            scratch_shapes=[pltpu.VMEM((rb, length, width), F32)] * 4,
            compiler_params=params(52),
            cost_estimate=cost(14 * n_tok * width * width, 40e6),
            name="self_backward",
        )(grad_mid, dprobe, u1, q, k, v, probs, w_a, w_a, w_a, w_a, w_a, g1)
        slabs = [wgrad(tokens, dq), wgrad(tokens, dk), wgrad(tokens, dv), wgrad(attended, gb1)] + cross_slabs
        grad_projected = lax.psum_scatter(dproj, "dp", scatter_dimension=0, tiled=True)
        dwp = lax.dot_general(patches, grad_projected, (((0, 1), (0, 1)), ((), ())), preferred_element_type=F32)
        dwp = dwp.reshape(shards, pr, width)
        vecs = vecs + vec_s
        vecs = vecs.at[5].set(jnp.sum(grad_projected.astype(F32), (0, 1)))
        vecs = jnp.broadcast_to(vecs[None, :nv], (shards, nv, width))
        slabs.append(dwp[:, :sr].reshape(slab).astype(BF))
        slab_shard = lax.psum_scatter(jnp.stack(slabs), AXES, scatter_dimension=1, tiled=True).astype(F32)
        extra_grad = jnp.concatenate([dwp[:, sr:], vecs, wb_rows[:, None]], 1).astype(BF)
        extra_shard = lax.psum_scatter(extra_grad, AXES, scatter_dimension=0, tiled=True)[0].astype(F32)
    patch_shard = jnp.concatenate([slab_shard[7], extra_shard[:tails]], 0)
    patches_grad = lax.dot_general(
        grad_projected, patch_full, (((2,), (1,)), ((), ())), preferred_element_type=F32
    ).astype(BF)
    vg = lax.dynamic_slice(extra_shard, (tails, place * sr), (nv, sr))
    vg = [vg[j] for j in range(nv)]
    wbg = extra_shard[tails + nv, :wr]
    return (
        output, tokens_grad, patches_grad,
        slab_shard[0], vg[0], slab_shard[1], slab_shard[2], vg[1], slab_shard[3], vg[2], vg[3], vg[4],
        patch_shard, vg[5], slab_shard[4], vg[6], slab_shard[5], slab_shard[6], vg[7], ffn_parts[chunks],
        vg[8], vg[9], vg[10], widen_shard, wbg, narrow_shard, vg[11], vg[12], vg[13],
    )


def solution(mesh):
    three, two, one = P(AXES, None, None), P(AXES, None), P(AXES)
    in_specs = (
        three, three, two, one, one, three,
        two, one, two, two, one, two, one, one, one, two, one, two, one, two,
        two, one, two, one, one, one, two, one, two, one, one, one,
    )
    out_specs = (
        three, three, three,
        two, one, two, two, one, two, one, one, one, two, one, two, one, two, two, one, two,
        one, one, one, two, one, two, one, one, one,
    )
    return jax.shard_map(on_device, mesh=mesh, in_specs=in_specs, out_specs=out_specs, check_vma=False)
```
